32 devices in a mesh: dp: 16 (over z, x, core), mp: 2 (over y).
Axes of the slice: x: 2, y: 2, z: 4, core: 2. Of those that a mesh axis runs over, the one named last changes fastest.
Arguments:
- inputs: bfloat16 [2, 16384, 768], P(None, ('dp', 'mp')), may hold values from -6 to 6
- roi_features: bfloat16 [2, 16384, 768], P(None, ('dp', 'mp')), may hold values from -6 to 6
- cotangent: bfloat16 [2, 16384, 768], P(None, ('dp', 'mp')), may hold values from -6 to 6
- doc_lengths: int32 [2, 16, 8], P(None, 'dp'), may hold values from 0 to 1024, as said below
- live_mask: int32 [2, 16384], P(None, 'dp'), may hold values 0 or 1
- bucket_cells: int32 [2, 3, 16384], P(None, None, 'dp'), may hold values from 0 to 31
- gain_attn: float32 [768], replicated, may hold values from 0.4 to 1.6
- gain_ffn: float32 [768], replicated, may hold values from 0.4 to 1.6
- w_query: bfloat16 [768, 768], P(None, 'mp'), may hold values from -0.21875 to 0.21875
- w_key: bfloat16 [768, 768], P(None, 'mp'), may hold values from -0.21875 to 0.21875
- w_value: bfloat16 [768, 768], P(None, 'mp'), may hold values from -0.21875 to 0.21875
- w_out: bfloat16 [768, 768], P('mp'), may hold values from -0.875 to 0.875
- w_up: bfloat16 [768, 3072], P(None, 'mp'), may hold values from -0.21875 to 0.21875
- w_down: bfloat16 [3072, 768], P('mp'), may hold values from -0.15625 to 0.15625
- bias_tables: float32 [3, 32, 12], P(None, None, 'mp'), may hold values from -4 to 4
Outputs:
- outputs: float32 [2, 16384, 768], P(None, ('dp', 'mp'))
- grad_inputs: float32 [2, 16384, 768], P(None, ('dp', 'mp'))
- grad_gain_attn: float32 [768], replicated
- grad_gain_ffn: float32 [768], replicated
- grad_w_query: float32 [768, 768], P(None, 'mp')
- grad_w_key: float32 [768, 768], P(None, 'mp')
- grad_w_value: float32 [768, 768], P(None, 'mp')
- grad_w_out: float32 [768, 768], P('mp')
- grad_w_up: float32 [768, 3072], P(None, 'mp')
- grad_w_down: float32 [3072, 768], P('mp')
- grad_bias_tables: float32 [3, 32, 12], P(None, None, 'mp')
The draws below stay inside these ranges and needn't reach their ends.
Inputs may be any that keep to these rules, and one draw needn't show every extreme that they name: `doc_lengths`: each pack's 8 lengths sum to at most 1024; unused slots are 0; in every draw some pack is one document of 1024 tokens.
All inputs are finite; a program needn't handle non-finite values. No bound on the sum of `live_mask` on one device may be relied on, other than what follows from the above.
Results may differ from the reference program's by a relative error of at most 0.018.
Values may be sent and summed in bfloat16 or wider, within the bound.
A program may use at most 256 MiB of HBM per device.

```python
import jax
import jax.numpy as jnp
from jax import lax

D = 768
HEADS = 12
HDIM = 64
FF = 3072
BUCKETS = 32
PACK = 1024
MB = 2
DOCS = 8
TOKENS = 16384
N_DP = 16


def draw_doc_lengths(key, part):
    first_key = jax.random.fold_in(key, 11)
    second_key = jax.random.fold_in(key, 12)
    third_key = jax.random.fold_in(key, 13)
    groups = TOKENS // PACK
    shape = (MB, groups, DOCS)
    base = jax.random.randint(first_key, shape, 1, 33)
    weights = base * base * base
    counts = jax.random.randint(second_key, (MB, groups, 1), 1, DOCS + 1)
    live_total = jax.random.randint(third_key, (MB, groups, 1), PACK // 2, PACK + 1)
    first_pack = jnp.arange(MB * groups).reshape(MB, groups, 1) == 0
    counts = jnp.where(first_pack, 1, counts)
    live_total = jnp.where(first_pack, PACK, live_total)
    slots = jnp.arange(DOCS).reshape(1, 1, DOCS)
    weights = jnp.where(slots < counts, weights, 0)
    total_weight = jnp.sum(weights, axis=2, keepdims=True)
    lengths = live_total * weights // total_weight
    return lengths.astype(jnp.int32)


def place_ends(values, key, low, top_value):
    spot = [jax.random.randint(jax.random.fold_in(key, axis), (), 0, length) for axis, length in enumerate(values.shape)]
    main_axis = values.shape.index(max(values.shape))
    neighbour = spot[:main_axis] + [(spot[main_axis] + 1) % values.shape[main_axis]] + spot[main_axis + 1:]
    return values.at[tuple(spot)].set(low).at[tuple(neighbour)].set(top_value)


def block_levels(rng, extent, split, low, largest):
    def one(axis_at, shards_of):
        draws = jax.random.uniform(jax.random.fold_in(jax.random.fold_in(rng, 6), axis_at), (shards_of,), jnp.float32, low / len(split), largest / len(split))
        return jnp.repeat(jnp.exp(draws), extent[axis_at] // shards_of).reshape((-1,) + (1,) * (len(extent) - axis_at - 1))

    level = one(*split[0])
    for cut in split[1:]:
        level = level * one(*cut)
    return level


def scatter_about(key, shape, width, most, pieces=(), kind=jnp.bfloat16):
    values = width * jax.random.normal(key, shape, jnp.float32)
    if pieces:
        values = values * block_levels(key, shape, pieces, -0.22, 0.18)
    return jnp.clip(values, -most, most).astype(kind)


def setup_inputs(seed: int = 0) -> dict:
    seeds = jax.random.split(jax.random.key(seed), 16)
    inputs = scatter_about(seeds[0], (MB, TOKENS, D), 1.0, 6.0, ((1, 32),))
    roi_features = scatter_about(seeds[1], (MB, TOKENS, D), 0.7, 6.0, ((1, 32),))
    cotangent = scatter_about(seeds[2], (MB, TOKENS, D), 1.0, 6.0, ((1, 32),))
    doc_lengths = draw_doc_lengths(jax.random.fold_in(seeds[15], 71), 0)
    live_mask = place_ends((jax.random.randint(seeds[4], (MB, TOKENS), 0, 8) < 7).astype(jnp.int32), jax.random.fold_in(seeds[4], 1), 0, 1)
    bucket_cells = place_ends(jax.random.randint(seeds[5], (MB, 3, TOKENS), 0, BUCKETS), jax.random.fold_in(seeds[5], 1), 0, BUCKETS - 1).astype(jnp.int32)
    gain_attn = jnp.clip(1.0 + 0.12 * jax.random.normal(seeds[6], (D,), jnp.float32), 0.4, 1.6)
    gain_ffn = jnp.clip(1.0 + 0.12 * jax.random.normal(seeds[7], (D,), jnp.float32), 0.4, 1.6)
    w_query = scatter_about(seeds[8], (D, D), D ** -0.5, 0.21875, ((1, 2),))
    w_key = scatter_about(seeds[9], (D, D), D ** -0.5, 0.21875, ((1, 2),))
    w_value = scatter_about(seeds[10], (D, D), D ** -0.5, 0.21875, ((1, 2),))
    w_out = scatter_about(seeds[11], (D, D), (D // 16) ** -0.5, 0.875, ((0, 2),))
    w_up = scatter_about(seeds[12], (D, FF), D ** -0.5, 0.21875, ((1, 2),))
    w_down = scatter_about(seeds[13], (FF, D), (FF // 2) ** -0.5, 0.15625, ((0, 2),))
    bias_tables = scatter_about(seeds[14], (3, BUCKETS, HEADS), 0.6, 4.0, ((2, 2),), jnp.float32)
    return {"inputs": inputs, "roi_features": roi_features, "cotangent": cotangent, "doc_lengths": doc_lengths, "live_mask": live_mask, "bucket_cells": bucket_cells, "gain_attn": gain_attn, "gain_ffn": gain_ffn, "w_query": w_query, "w_key": w_key, "w_value": w_value, "w_out": w_out, "w_up": w_up, "w_down": w_down, "bias_tables": bias_tables}


@jax.custom_vjp
def low(v):
    return lax.optimization_barrier(v.astype(jnp.bfloat16)).astype(jnp.float32)

@jax.custom_vjp
def low_back(v):
    return v

def low_keep(v):
    return (low(v), None)

def low_pass(kept, grad):
    return (grad,)

def back_keep(v):
    return (v, None)

def back_low(kept, grad):
    return (low(grad),)
low.defvjp(low_keep, low_pass)
low_back.defvjp(back_keep, back_low)

def rms_norm(rows, gain):
    return rows * lax.rsqrt(lax.optimization_barrier(jnp.mean(rows * rows, axis=-1, keepdims=True)) + 1e-06) * gain

def matmul(left, right):
    return jnp.dot(left, right, precision=lax.Precision.HIGHEST)

def pack_layer(params, resid, segment, live, cells):
    gain_attn, gain_ffn, w_query, w_key, w_value, w_out, w_up, w_down, bias_tables = params
    length = resid.shape[0]
    normed = low(rms_norm(resid, gain_attn))

    def split_heads(weight):
        return low(low_back(matmul(normed, weight))).reshape(length, HEADS, HDIM)
    queries = split_heads(w_query)
    keys = split_heads(w_key)
    values = split_heads(w_value)
    half = BUCKETS // 2
    relative = jnp.clip(cells[:, None, :] - cells[:, :, None], -half, half - 1) + half
    bias = bias_tables[0][relative[0]] + bias_tables[1][relative[1]] + bias_tables[2][relative[2]]
    scores = jnp.einsum('qhd,khd->hqk', queries, keys, precision=lax.Precision.HIGHEST) * HDIM ** (-0.5)
    scores = low_back(scores + jnp.transpose(bias, (2, 0, 1)))
    token = jnp.arange(length)
    allowed = (segment[:, None] == segment[None, :]) & ((live[None, :] == 1) | (token[:, None] == token[None, :]))
    scores = jnp.where(allowed[None], scores, -1000000000.0)
    probs = jax.nn.softmax(scores, axis=-1)
    mixed = jnp.einsum('hqk,khd->qhd', low(probs), values, precision=lax.Precision.HIGHEST).reshape(length, HEADS * HDIM)
    mixed = low(low_back(mixed))
    hidden = resid + low_back(matmul(mixed, w_out))
    normed_ffn = low(rms_norm(hidden, gain_ffn))
    activ = low(jax.nn.gelu(low_back(matmul(normed_ffn, w_up)), approximate=False))
    return hidden + matmul(activ, w_down)

def reference(inputs, roi_features, cotangent, doc_lengths, live_mask, bucket_cells, gain_attn, gain_ffn, w_query, w_key, w_value, w_out, w_up, w_down, bias_tables):
    packs = doc_lengths.shape[0] * doc_lengths.shape[1]
    resid = (inputs.astype(jnp.float32) + roi_features.astype(jnp.float32)).reshape(packs, PACK, D)
    lengths = doc_lengths.reshape(packs, DOCS)
    ends = jnp.cumsum(lengths, axis=1)
    token = jnp.arange(PACK)
    segment = lax.optimization_barrier(jnp.sum((token[None, :, None] >= ends[:, None, :]).astype(jnp.int32), axis=2))
    live = live_mask.reshape(packs, PACK)
    cells = bucket_cells.reshape(MB, 3, N_DP, PACK).transpose(0, 2, 1, 3).reshape(packs, 3, PACK)
    params = tuple((item.astype(jnp.float32) for item in (gain_attn, gain_ffn, w_query, w_key, w_value, w_out, w_up, w_down, bias_tables)))

    def run(resid_all, weights):

        def one_pack(carry, item):
            return (carry, pack_layer(weights, item[0], item[1], item[2], item[3]))
        unused, result = lax.scan(jax.checkpoint(one_pack), jnp.float32(0.0), (resid_all, segment, live, cells))
        return result
    result, pullback = jax.vjp(run, resid, params)
    grad_resid, grads = pullback(cotangent.astype(jnp.float32).reshape(packs, PACK, D))
    return (result.reshape(MB, N_DP * PACK, D).astype(jnp.float32), grad_resid.reshape(MB, N_DP * PACK, D).astype(jnp.float32), grads[0], grads[1], grads[2], grads[3], grads[4], grads[5], grads[6], grads[7], grads[8])
```

```python
import functools
import math

import jax
import jax.numpy as jnp
from jax import lax
from jax.experimental import pallas as pl
from jax.experimental.pallas import tpu as pltpu
from jax.sharding import PartitionSpec as P

BF = jnp.bfloat16
F32 = jnp.float32
HDIM = 64
EPS = 1e-06
MASKED = -1e30
MESH = pl.DeviceIdType.MESH
VMEM = pl.BlockSpec(memory_space=pltpu.VMEM)
ANY = pl.BlockSpec(memory_space=pl.ANY)
SHAPE = jax.ShapeDtypeStruct


def dg(a, b, ca, cb):
    return lax.dot_general(a, b, (((ca,), (cb,)), ((), ())), preferred_element_type=F32)


def params(limit=58, **more):
    return pltpu.CompilerParams(vmem_limit_bytes=limit << 20, **more)


class Links:
    def __init__(self, send, recv):
        self.send, self.recv, self.count = send, recv, 0
        self.d, self.m = lax.axis_index("dp"), lax.axis_index("mp")

    def remote(self, src, dst, dp_flip=0, mp_flip=0):
        i = self.count
        self.count += 1
        dp = self.d ^ dp_flip if dp_flip else self.d
        mp = self.m ^ mp_flip if mp_flip else self.m
        return pltpu.make_async_remote_copy(
            src_ref=src,
            dst_ref=dst,
            send_sem=self.send.at[i],
            recv_sem=self.recv.at[i],
            device_id=(dp, mp),
            device_id_type=MESH,
        )

    def local(self, src, dst):
        i = self.count
        self.count += 1
        return pltpu.make_async_copy(src, dst, self.send.at[i])

    def barrier(self, flips):
        sem = pltpu.get_barrier_semaphore()
        for dp_flip, mp_flip in flips:
            dp = self.d ^ dp_flip if dp_flip else self.d
            mp = self.m ^ mp_flip if mp_flip else self.m
            pl.semaphore_signal(sem, inc=1, device_id=(dp, mp), device_id_type=MESH)
        pl.semaphore_wait(sem, len(flips))


def rows_at(start, size, unit):
    return pl.ds(pl.multiple_of(start, unit), size)


def gather_kernel(
    hi, cot, tab, wq, wk, wv, wo, wup, wdn,
    xf, dyf, tabo, qkvf, wof, wupf, wdnf,
    send, recv,
):
    links = Links(send, recv)
    d, m = links.d, links.m
    rows = hi.shape[1]
    width = wq.shape[0]
    third = wq.shape[1]
    hidden = wup.shape[1]
    inner = wo.shape[0]
    links.barrier(((0, 1), (1, 0), (2, 0), (4, 0)))
    core, cross, deep = d & 1, (d >> 1) & 1, (d >> 2) & 1
    other = 1 - m
    locals_ = []
    own_rows = rows_at(m * rows, rows, rows)
    waits = []

    def go(copy):
        copy.start()
        waits.append(copy)
        return copy

    targets = (
        (qkvf, 0, width, slice(3 * third, 6 * third)),
        (wof, inner, inner, slice(0, width)),
        (wupf, 0, width, slice(hidden, 2 * hidden)),
        (wdnf, hidden, hidden, slice(0, width)),
    )
    sources = ((wq, wk, wv), (wo,), (wup,), (wdn,))

    def block(entry, first, count):
        full, base, total, columns = entry
        piece = total // 8
        return full.at[rows_at(base + first * piece, count * piece, piece), columns]

    place = core * 4 + cross * 2 + deep
    stage_y = []
    for entry, parts in zip(targets, sources):
        full, base, total, columns = entry
        piece = total // 8
        group = []
        for j, part in enumerate(parts):
            span = part.shape[1]
            cols = slice(columns.start + j * span, columns.start + (j + 1) * span)
            group.append(
                go(
                    links.remote(
                        part.at[rows_at(place * piece, piece, piece)],
                        full.at[rows_at(base + place * piece, piece, piece), cols],
                        mp_flip=1,
                    )
                )
            )
        stage_y.append(group)
        if full is qkvf:
            row_copies = [
                go(links.remote(tab, tabo, mp_flip=1)),
                go(links.remote(hi.at[other], xf.at[own_rows], mp_flip=1)),
            ]
    row_copies.append(go(links.remote(cot.at[other], dyf.at[own_rows], mp_flip=1)))
    locals_.append(links.local(hi.at[m], xf.at[own_rows]))
    locals_.append(links.local(cot.at[m], dyf.at[own_rows]))
    for j, part in enumerate((wq, wk, wv)):
        locals_.append(links.local(part, qkvf.at[:, j * third : (j + 1) * third]))
    locals_.append(links.local(wo, wof.at[0:inner]))
    locals_.append(links.local(wup, wupf.at[:, 0:hidden]))
    locals_.append(links.local(wdn, wdnf.at[0:hidden]))
    for copy in locals_:
        copy.start()
    stage = stage_y
    for flip, first, count in (
        (4, place, 1),
        (2, core * 4 + cross * 2, 2),
        (1, core * 4, 4),
    ):
        following = []
        for entry, group in zip(targets, stage):
            for copy in group:
                copy.wait_recv()
            there = block(entry, first, count)
            following.append([go(links.remote(there, there, dp_flip=flip))])
        stage = following
    for group in stage:
        for copy in group:
            copy.wait_recv()
    for copy in row_copies:
        copy.wait_recv()
    for copy in waits:
        copy.wait_send()
    for copy in locals_:
        copy.wait()


def gather(hi, cot, tab, wq, wk, wv, wo, wup, wdn):
    rows, width = hi.shape[1], hi.shape[2]
    third, hidden = wq.shape[1], wup.shape[1]
    return pl.pallas_call(
        gather_kernel,
        out_shape=[
            SHAPE((2 * rows, width), BF),
            SHAPE((2 * rows, width), BF),
            SHAPE(tab.shape, F32),
            SHAPE((width, 6 * third), BF),
            SHAPE((2 * third, width), BF),
            SHAPE((width, 2 * hidden), BF),
            SHAPE((2 * hidden, width), BF),
        ],
        in_specs=[ANY] * 9,
        out_specs=[ANY] * 7,
        scratch_shapes=[pltpu.SemaphoreType.DMA((40,)), pltpu.SemaphoreType.DMA((40,))],
        compiler_params=params(16, collective_id=1, has_side_effects=True),
        name="gather",
    )(hi, cot, tab, wq, wk, wv, wo, wup, wdn)


def proj_kernel(x_ref, g_ref, w_ref, q_ref, kv_ref, *, third):
    x = x_ref[...].astype(F32)
    inverse = lax.rsqrt(jnp.mean(x * x, axis=-1, keepdims=True) + EPS)
    normed = (x * inverse * g_ref[...]).astype(BF)
    w = w_ref[...]
    q_ref[...] = dg(w[:, 0:third], normed, 0, 1).astype(BF)
    kv_ref[...] = dg(normed, w[:, third : 3 * third], 1, 0).astype(BF)


def project(x, gain, wqkv):
    tokens, width = x.shape
    third = wqkv.shape[1] // 6
    return pl.pallas_call(
        functools.partial(proj_kernel, third=third),
        grid=(2,),
        in_specs=[
            pl.BlockSpec((tokens, width), lambda i: (0, 0)),
            pl.BlockSpec((1, width), lambda i: (0, 0)),
            pl.BlockSpec((width, 3 * third), lambda i: (0, i)),
        ],
        out_specs=[
            pl.BlockSpec((third, tokens), lambda i: (i, 0)),
            pl.BlockSpec((tokens, 2 * third), lambda i: (0, i)),
        ],
        out_shape=[SHAPE((2 * third, tokens), BF), SHAPE((tokens, 4 * third), BF)],
        compiler_params=params(),
        name="project",
    )(x, gain, wqkv)


def attend_kernel(
    qt_ref, k_ref, v_ref, hot_ref, hott_ref, mats_ref, mask_ref,
    p_ref, o_ref, r_ref, kx, qx, vx,
):
    tokens = k_ref.shape[0]

    @pl.when(pl.program_id(0) == 0)
    def _():
        kx[:, 64:256] = hot_ref[...]
        vx[64:80, :] = jnp.ones((16, tokens), BF)

    vt = v_ref[...].T
    for h in range(2):
        span = slice(64 * h, 64 * h + 64)
        kx[:, 0:64] = k_ref[:, span]
        qx[0:64, :] = qt_ref[span, :] * BF(0.125)
        qx[64:256, :] = dg(mats_ref[h], hott_ref[...], 1, 0).astype(BF)
        vx[0:64, :] = vt[span, :]
        s = dg(kx[...], qx[...], 1, 0) + mask_ref[...]
        top = jnp.max(s, axis=0, keepdims=True)
        p = jnp.exp(s - top).astype(BF)
        p_ref[h] = p
        o = dg(vx[...], p, 1, 0)
        r = 1.0 / o[64:65, :]
        o_ref[span, :] = (o[0:64] * r).astype(BF)
        r_ref[0, h : h + 1, :] = r


def attend(qt, kv, hot, hott, mats, mask):
    channels, tokens = qt.shape
    pairs = channels // 128
    half = pairs // 2
    whole = lambda shape: pl.BlockSpec(shape, lambda i: (0,) * len(shape))
    return pl.pallas_call(
        attend_kernel,
        grid=(pairs,),
        in_specs=[
            pl.BlockSpec((128, tokens), lambda i: (i, 0)),
            pl.BlockSpec((tokens, 128), lambda i: (0, (i // half) * 2 * half + i % half)),
            pl.BlockSpec((tokens, 128), lambda i: (0, (i // half) * 2 * half + half + i % half)),
            whole((tokens, 192)),
            whole((96, tokens)),
            pl.BlockSpec((2, 192, 96), lambda i: (i, 0, 0)),
            whole((tokens, tokens)),
        ],
        out_specs=[
            pl.BlockSpec((2, tokens, tokens), lambda i: (i, 0, 0)),
            pl.BlockSpec((128, tokens), lambda i: (i, 0)),
            pl.BlockSpec((1, 2, tokens), lambda i: (i, 0, 0)),
        ],
        out_shape=[
            SHAPE((2 * pairs, tokens, tokens), BF),
            SHAPE((channels, tokens), BF),
            SHAPE((pairs, 2, tokens), F32),
        ],
        scratch_shapes=[
            pltpu.VMEM((tokens, 256), BF),
            pltpu.VMEM((256, tokens), BF),
            pltpu.VMEM((80, tokens), BF),
        ],
        compiler_params=params(),
        name="attend",
    )(qt, kv, kv, hot, hott, mats, mask)


def attend_back_kernel(
    p_ref, qt_ref, k_ref, v_ref, ot_ref, dot_ref, r_ref, hott_ref, hot_ref,
    dq_ref, dk_ref, dv_ref, gm_ref, vx, dox, kht,
):
    tokens = k_ref.shape[0]

    @pl.when(pl.program_id(0) == 0)
    def _():
        kht[64:160, :] = hott_ref[...]
        lanes = lax.broadcasted_iota(jnp.int32, (tokens, 64), 1)
        vx[:, 64:128] = jnp.where(lanes < 2, -1.0, 0.0).astype(BF)
        dox[64:128, :] = jnp.zeros((64, tokens), BF)

    for h in range(2):
        span = slice(64 * h, 64 * h + 64)
        scaled = dot_ref[span, :].astype(F32) * r_ref[0, h : h + 1, :]
        inner = jnp.sum(scaled * ot_ref[span, :].astype(F32), axis=0, keepdims=True)
        upper = inner.astype(BF)
        lower = (inner - upper.astype(F32)).astype(BF)
        dox[0:64, :] = scaled.astype(BF)
        dox[64:66, :] = jnp.concatenate([upper, lower], 0)
        vx[:, 0:64] = v_ref[:, span]
        kht[0:64, :] = k_ref[:, span].T
        dp = dg(vx[...], dox[...], 1, 0)
        p = p_ref[h]
        ds = (p.astype(F32) * dp).astype(BF)
        dv_ref[:, span] = dg(p, dox[0:64, :], 1, 1).astype(BF)
        dk_ref[:, span] = (dg(ds, qt_ref[span, :], 1, 1) * 0.125).astype(BF)
        both = dg(kht[...], ds, 1, 0)
        dq_ref[:, span] = (both[0:64] * 0.125).astype(BF).T
        left = both[64:160]
        left_hi = left.astype(BF)
        left_lo = (left - left_hi.astype(F32)).astype(BF)
        hot = hot_ref[:, 0:96]
        gm_ref[h] = dg(left_hi, hot, 1, 0) + dg(left_lo, hot, 1, 0)


def attend_back(p, qt, kv, ot, dot, r, hott, hot):
    channels, tokens = qt.shape
    pairs = channels // 128
    half = pairs // 2
    whole = lambda shape: pl.BlockSpec(shape, lambda i: (0,) * len(shape))
    natural = pl.BlockSpec((tokens, 128), lambda i: (0, i))
    turned = pl.BlockSpec((128, tokens), lambda i: (i, 0))
    return pl.pallas_call(
        attend_back_kernel,
        grid=(pairs,),
        in_specs=[
            pl.BlockSpec((2, tokens, tokens), lambda i: (i, 0, 0)),
            turned,
            pl.BlockSpec((tokens, 128), lambda i: (0, (i // half) * 2 * half + i % half)),
            pl.BlockSpec((tokens, 128), lambda i: (0, (i // half) * 2 * half + half + i % half)),
            turned,
            turned,
            pl.BlockSpec((1, 2, tokens), lambda i: (i, 0, 0)),
            whole((96, tokens)),
            whole((tokens, 192)),
        ],
        out_specs=[natural, natural, natural, pl.BlockSpec((2, 96, 96), lambda i: (i, 0, 0))],
        out_shape=[SHAPE((tokens, channels), BF)] * 3 + [SHAPE((2 * pairs, 96, 96), F32)],
        scratch_shapes=[
            pltpu.VMEM((tokens, 128), BF),
            pltpu.VMEM((128, tokens), BF),
            pltpu.VMEM((160, tokens), BF),
        ],
        compiler_params=params(),
        name="attend_back",
    )(p, qt, kv, kv, ot, dot, r, hott, hot)


def middle_kernel(
    x_ref, mixt_ref, wo_ref, dy_ref, gain_ref, wup_ref, wdn_ref,
    y_ref, gup_ref, gdn_ref, gwo_ref, dh_ref, dmt_ref, gg_ref,
    h1, n2, n2t, yacc, dn,
):
    step = pl.program_id(0)

    @pl.when(step == 0)
    def _():
        added = dg(mixt_ref[...], wo_ref[...], 0, 0)
        h = x_ref[...].astype(F32) + added
        h1[...] = h
        yacc[...] = added
        inverse = lax.rsqrt(jnp.mean(h * h, axis=-1, keepdims=True) + EPS)
        normed = (h * inverse * gain_ref[...]).astype(BF)
        n2[...] = normed
        n2t[...] = normed.T
        dn[...] = jnp.zeros_like(dn)

    wup, wdn, dy = wup_ref[...], wdn_ref[...], dy_ref[...]
    u = dg(n2[...], wup, 1, 0)
    cdf = 0.5 * (1.0 + lax.erf(u * 0.7071067811865476))
    act = (u * cdf).astype(BF)
    grad_act = dg(dy, wdn, 1, 1)
    density = jnp.exp(u * u * (-0.5)) * 0.3989422804014327
    du = (grad_act * (cdf + u * density)).astype(BF)
    yacc[...] += dg(act, wdn, 1, 0)
    dn[...] += dg(du, wup, 1, 1)
    gup_ref[...] = dg(n2t[...], du, 1, 0).astype(BF)
    gdn_ref[...] = dg(act, dy, 0, 0).astype(BF)

    @pl.when(step == pl.num_programs(0) - 1)
    def _():
        h = h1[...]
        inverse = lax.rsqrt(jnp.mean(h * h, axis=-1, keepdims=True) + EPS)
        normed = h * inverse
        grad = dn[...]
        gg_ref[...] = jnp.sum(grad * normed, axis=0, keepdims=True)
        inner = grad * gain_ref[...]
        added = inverse * (inner - normed * jnp.mean(inner * normed, axis=-1, keepdims=True))
        dh_ref[...] = added
        y_ref[...] = yacc[...].astype(BF)
        low = (dy_ref[...].astype(F32) + added).astype(BF)
        gwo_ref[...] = dg(low, mixt_ref[...], 0, 1).astype(BF)
        dmt_ref[...] = dg(wo_ref[...], low, 1, 1).astype(BF)


def middle(x, mixt, wo, dy, gain, wup, wdn, chunk=512):
    tokens, width = x.shape
    hidden = wup.shape[1]
    whole = lambda shape: pl.BlockSpec(shape, lambda i: (0,) * len(shape))
    return pl.pallas_call(
        middle_kernel,
        grid=(hidden // chunk,),
        in_specs=[
            whole((tokens, width)),
            whole((width, tokens)),
            whole((width, width)),
            whole((tokens, width)),
            whole((1, width)),
            pl.BlockSpec((width, chunk), lambda i: (0, i)),
            pl.BlockSpec((chunk, width), lambda i: (i, 0)),
        ],
        out_specs=[
            whole((tokens, width)),
            pl.BlockSpec((width, chunk), lambda i: (0, i)),
            pl.BlockSpec((chunk, width), lambda i: (i, 0)),
            whole((width, width)),
            whole((tokens, width)),
            whole((width, tokens)),
            whole((1, width)),
        ],
        out_shape=[
            SHAPE((tokens, width), BF),
            SHAPE((width, hidden), BF),
            SHAPE((hidden, width), BF),
            SHAPE((width, width), BF),
            SHAPE((tokens, width), F32),
            SHAPE((width, tokens), BF),
            SHAPE((1, width), F32),
        ],
        scratch_shapes=[
            pltpu.VMEM((tokens, width), F32),
            pltpu.VMEM((tokens, width), BF),
            pltpu.VMEM((width, tokens), BF),
            pltpu.VMEM((tokens, width), F32),
            pltpu.VMEM((tokens, width), F32),
        ],
        compiler_params=params(60),
        name="middle",
    )(x, mixt, wo, dy, gain, wup, wdn)


def finish_kernel(
    x_ref, gain_ref, dh_ref, dq_ref, dk_ref, dv_ref, w_ref,
    gw_ref, gin_ref, gg_ref, n1, dn, *, third,
):
    step = pl.program_id(0)
    x = x_ref[...].astype(F32)

    @pl.when(step == 0)
    def _():
        inverse = lax.rsqrt(jnp.mean(x * x, axis=-1, keepdims=True) + EPS)
        n1[...] = (x * inverse * gain_ref[...]).astype(BF)
        dn[...] = jnp.zeros_like(dn)

    w = w_ref[...]
    total = dn[...]
    for j, ref in enumerate((dq_ref, dk_ref, dv_ref)):
        span = slice(j * third, (j + 1) * third)
        gw_ref[:, span] = dg(n1[...], ref[...], 0, 0).astype(BF)
        total = total + dg(ref[...], w[:, span], 1, 1)
    dn[...] = total

    @pl.when(step == pl.num_programs(0) - 1)
    def _():
        inverse = lax.rsqrt(jnp.mean(x * x, axis=-1, keepdims=True) + EPS)
        normed = x * inverse
        gg_ref[...] = jnp.sum(total * normed, axis=0, keepdims=True)
        inner = total * gain_ref[...]
        added = inverse * (inner - normed * jnp.mean(inner * normed, axis=-1, keepdims=True))
        gin_ref[...] = (dh_ref[...] + added).astype(BF)


def finish(x, gain, dh, dq, dk, dv, wqkv):
    tokens, width = x.shape
    third = wqkv.shape[1] // 6
    whole = lambda shape: pl.BlockSpec(shape, lambda i: (0,) * len(shape))
    part = pl.BlockSpec((tokens, third), lambda i: (0, i))
    return pl.pallas_call(
        functools.partial(finish_kernel, third=third),
        grid=(2,),
        in_specs=[
            whole((tokens, width)),
            whole((1, width)),
            whole((tokens, width)),
            part,
            part,
            part,
            pl.BlockSpec((width, 3 * third), lambda i: (0, i)),
        ],
        out_specs=[
            pl.BlockSpec((width, 3 * third), lambda i: (0, i)),
            whole((tokens, width)),
            whole((1, width)),
        ],
        out_shape=[
            SHAPE((width, 6 * third), BF),
            SHAPE((tokens, width), BF),
            SHAPE((1, width), F32),
        ],
        scratch_shapes=[pltpu.VMEM((tokens, width), BF), pltpu.VMEM((tokens, width), F32)],
        compiler_params=params(),
        name="finish",
    )(x, gain, dh, dq, dk, dv, wqkv)


def reduce_kernel(y, gin, small, gqkv, gwo, gup, gdn, *rest, n_dp):
    (yret, gret, small_out, fqkv, fwo, fup, fdn) = rest[:7]
    grads = (gqkv, gwo, gup, gdn)
    finals = (fqkv, fwo, fup, fdn)
    rc, ry, rx, rz = rest[7:11], rest[11:15], rest[15:19], rest[19:23]
    sums, got = rest[23:25]
    far = rest[25:29] if n_dp > 16 else None
    send, recv = rest[-2:]
    links = Links(send, recv)
    d, m = links.d, links.m
    bits = n_dp.bit_length() - 1
    flips = [(0, 1)] + [(1 << b, 0) for b in range(bits)] + [(12, 0)]
    flips += [(r << 4, 0) for r in range(1, n_dp // 16) if r & (r - 1)]
    links.barrier(flips)
    core, cross, deep = d & 1, (d >> 1) & 1, (d >> 2) & 3
    rows = y.shape[0] // 2
    started = []

    def go(copy):
        copy.start()
        started.append(copy)
        return copy

    mine = rows_at(m * rows, rows, rows)
    theirs = rows_at((1 - m) * rows, rows, rows)
    locals_ = [links.local(y.at[mine], yret.at[m]), links.local(gin.at[mine], gret.at[m])]
    for copy in locals_:
        copy.start()

    def half(i, side, start, count, ref, based):
        own = finals[i].shape
        if i == 3:
            base = side * own[0] if based else 0
            return ref.at[rows_at(base + start, count, 16)]
        cols = slice(side * own[1], (side + 1) * own[1])
        return ref.at[rows_at(start, count, 16), cols]

    order = (3, 2, 0, 1)
    size = [f.shape[0] for f in finals]
    copies = {}

    def start_core(i):
        n = size[i] // 2
        for side in range(2):
            src = half(i, side, (1 - core) * n, n, grads[i], True)
            copies["c", i, side] = go(links.remote(src, rc[i].at[side], dp_flip=1))

    def start_y(i):
        n = size[i] // 2
        for side in range(2):
            copies["c", i, side].wait_recv()
            src = half(i, side, core * n, n, grads[i], True)
            rc[i][side] = (rc[i][side].astype(F32) + src[...].astype(F32)).astype(BF)
        copies["y", i] = go(links.remote(rc[i].at[1], ry[i], mp_flip=1))

    def start_x(i):
        n = size[i] // 4
        copies["y", i].wait_recv()
        ry[i][...] = (ry[i][...].astype(F32) + rc[i][0].astype(F32)).astype(BF)
        src = ry[i].at[rows_at((1 - cross) * n, n, 16)]
        copies["x", i] = go(links.remote(src, rx[i], dp_flip=2))

    def start_z(i):
        n = size[i] // 16
        copies["x", i].wait_recv()
        keep = ry[i][rows_at(cross * size[i] // 4, size[i] // 4, 16)]
        rx[i][...] = (rx[i][...].astype(F32) + keep.astype(F32)).astype(BF)
        for r in range(1, 4):
            src = rx[i].at[rows_at((deep ^ r) * n, n, 16)]
            copies["z", i, r] = go(links.remote(src, rz[i].at[r - 1], dp_flip=r << 2))

    def place(i, count):
        n = size[i] // 16
        at = {1: core * 8 + cross * 4 + deep, 4: core * 8 + cross * 4, 8: core * 8}[count]
        return finals[i].at[rows_at(at * n, count * n, 16)]

    def start_back_z(i):
        n = size[i] // 16
        for r in range(1, 4):
            copies["z", i, r].wait_recv()
        total = rx[i][rows_at(deep * n, n, 16)].astype(F32)
        for r in range(3):
            total = total + rz[i][r].astype(F32)
        if far is not None:
            rz_own = far[i]
            rz_own[0] = total.astype(BF)
            group = [
                go(links.remote(rz_own.at[0], rz_own.at[r], dp_flip=r << 4))
                for r in range(1, n_dp // 16)
            ]
            for r, copy in enumerate(group):
                copy.wait_recv()
                total = total + rz_own[r + 1].astype(F32)
        spot = place(i, 1)
        spot[...] = total.astype(BF)
        for r in range(1, 4):
            copies["bz", i, r] = go(links.remote(spot, spot, dp_flip=r << 2))

    def start_back_x(i):
        for r in range(1, 4):
            copies["bz", i, r].wait_recv()
        spot = place(i, 4)
        copies["bx", i] = go(links.remote(spot, spot, dp_flip=2))

    def start_back_c(i):
        copies["bx", i].wait_recv()
        spot = place(i, 8)
        copies["bc", i] = go(links.remote(spot, spot, dp_flip=1))

    def end(i):
        copies["bc", i].wait_recv()

    stages = (start_core, start_y, start_x, start_z, start_back_z, start_back_x, start_back_c, end)
    sums[0] = small[...]
    n_small = bits + 1
    tick = 0
    for t in range(len(stages) + len(order) - 1):
        for j, i in enumerate(order):
            if 0 <= t - j < len(stages):
                stages[t - j](i)
        if t == 3:
            row_copies = [
                go(links.remote(y.at[theirs], yret.at[m], mp_flip=1)),
                go(links.remote(gin.at[theirs], gret.at[m], mp_flip=1)),
            ]
        if tick <= n_small:
            if tick > 0:
                hop.wait_recv()
                if tick == 1:
                    sums[1, 0:16] = sums[0, 0:16] + got[0, 0:16]
                    sums[1, 16:24] = sums[0, 16:24] + got[0, 24:32]
                    sums[1, 24:32] = jnp.zeros_like(sums[0, 24:32])
                else:
                    sums[tick] = sums[tick - 1] + got[tick - 1]
            if tick < n_small:
                flip = (0, 1) if tick == 0 else (1 << (tick - 1), 0)
                hop = go(links.remote(sums.at[tick], got.at[tick], dp_flip=flip[0], mp_flip=flip[1]))
            tick += 1
    small_out[...] = sums[n_small]
    for copy in row_copies:
        copy.wait_recv()
    for copy in started:
        copy.wait_send()
    for copy in locals_:
        copy.wait()


def reduce_all(y, gin, small, gqkv, gwo, gup, gdn, n_dp):
    tokens, width = y.shape
    own = (
        (width, gqkv.shape[1] // 2),
        (width, gwo.shape[1] // 2),
        (width, gup.shape[1] // 2),
        (gdn.shape[0] // 2, width),
    )
    bits = n_dp.bit_length() - 1
    scratch = [pltpu.VMEM((2, a // 2, b), BF) for a, b in own]
    scratch += [pltpu.VMEM((a // 2, b), BF) for a, b in own]
    scratch += [pltpu.VMEM((a // 4, b), BF) for a, b in own]
    scratch += [pltpu.VMEM((3, a // 16, b), BF) for a, b in own]
    scratch += [pltpu.VMEM((bits + 2,) + small.shape, F32)] * 2
    count = 80
    if n_dp > 16:
        scratch += [pltpu.VMEM((n_dp // 16, a // 16, b), BF) for a, b in own]
        count += 4 * (n_dp // 16)
    scratch += [pltpu.SemaphoreType.DMA((count,))] * 2
    return pl.pallas_call(
        functools.partial(reduce_kernel, n_dp=n_dp),
        out_shape=[
            SHAPE((2, tokens // 2, width), BF),
            SHAPE((2, tokens // 2, width), BF),
            SHAPE(small.shape, F32),
        ]
        + [SHAPE(s, BF) for s in own],
        in_specs=[ANY, ANY] + [VMEM] * 5,
        out_specs=[ANY, ANY] + [VMEM] * 5,
        scratch_shapes=scratch,
        compiler_params=params(60, collective_id=2, has_side_effects=True),
        name="reduce",
    )(y, gin, small, gqkv, gwo, gup, gdn)


def local(
    n_dp, inputs, roi, cotangent, doc_lengths, live_mask, bucket_cells,
    gain_attn, gain_ffn, w_query, w_key, w_value, w_out, w_up, w_down, tables,
):
    rows, width = inputs.shape[1], inputs.shape[2]
    tokens = 2 * rows
    third = w_query.shape[1]
    heads = third // HDIM
    buckets = tables.shape[1]
    half = buckets // 2
    m = lax.axis_index("mp")

    resid = inputs.astype(F32) + roi.astype(F32)
    tab = jnp.pad(
        tables.transpose(2, 0, 1).reshape(heads, 3 * buckets), ((0, 2), (0, 128 - 3 * buckets))
    )
    x, dy, tab_other, wqkv, wo, wup, wdn = gather(
        resid.astype(BF), cotangent, tab, w_query, w_key, w_value, w_out, w_up, w_down
    )

    lengths = lax.dynamic_index_in_dim(doc_lengths, m, 0, keepdims=False)[0]
    live = lax.dynamic_index_in_dim(live_mask, m, 0, keepdims=False)
    cells = lax.dynamic_index_in_dim(bucket_cells, m, 0, keepdims=False)
    ids = jnp.arange(tokens)
    segment = jnp.sum((ids[:, None] >= jnp.cumsum(lengths)[None, :]).astype(jnp.int32), axis=1)
    allowed = (segment[:, None] == segment[None, :]) & (
        (live[:, None] == 1) | (ids[:, None] == ids[None, :])
    )
    mask = jnp.where(allowed, 0.0, MASKED).astype(F32)
    cell_ids = jnp.arange(buckets)
    hott = (cells[:, None, :] == cell_ids[None, :, None]).astype(BF).reshape(3 * buckets, tokens)
    hot = (cells.T[:, :, None] == cell_ids[None, None, :]).astype(BF).reshape(tokens, 3 * buckets)
    hot = jnp.concatenate([hot, hot], axis=1)
    relative = jnp.clip(cell_ids[:, None] - cell_ids[None, :], -half, half - 1) + half
    select = (relative[:, :, None] == cell_ids).astype(F32)
    both = jnp.concatenate([tab[:heads], tab_other[:heads]], 0)[:, : 3 * buckets]
    both = both.reshape(2 * heads, 3, buckets)
    blocks = jnp.einsum("han,xyn->haxy", both, select, precision=lax.Precision.HIGHEST)
    eye = jnp.eye(3, dtype=F32)
    mats = (blocks[:, :, :, None, :] * eye[None, :, None, :, None]).reshape(
        2 * heads, 3 * buckets, 3 * buckets
    )
    mats_hi = mats.astype(BF)
    mats_lo = (mats - mats_hi.astype(F32)).astype(BF)
    mats = jnp.concatenate([mats_hi, mats_lo], axis=1)

    ga, gf = gain_attn.reshape(1, width), gain_ffn.reshape(1, width)
    qt, kv = project(x, ga, wqkv)
    p, mixt, r = attend(qt, kv, hot, hott, mats, mask)
    y, gup, gdn, gwo, dh, dmt, gain_f = middle(x, mixt, wo, dy, gf, wup, wdn)
    dq, dk, dv, gmats = attend_back(p, qt, kv, mixt, dmt, r, hott, hot)
    gqkv, gin, gain_a = finish(x, ga, dh, dq, dk, dv, wqkv)

    gblocks = jnp.stack(
        [gmats[:, t * buckets : (t + 1) * buckets, t * buckets : (t + 1) * buckets] for t in range(3)],
        axis=1,
    )
    gtab = jnp.einsum("haxy,xyn->han", gblocks, select, precision=lax.Precision.HIGHEST)
    gtab = jnp.pad(
        gtab.reshape(2, heads, 3 * buckets), ((0, 0), (0, 2), (0, 128 - 3 * buckets))
    ).reshape(16, 128)
    small = jnp.concatenate(
        [gain_a.reshape(-1, 128), gain_f.reshape(-1, 128), jnp.zeros((4, 128), F32), gtab], 0
    )
    yret, gret, small, fqkv, fwo, fup, fdn = reduce_all(y, gin, small, gqkv, gwo, gup, gdn, n_dp)
    lines = width // 128
    out = resid + yret.astype(F32)
    grad_in = cotangent.astype(F32) + gret.astype(F32)
    table_out = small[16 : 16 + heads, : 3 * buckets].reshape(heads, 3, buckets).transpose(1, 2, 0)
    return (
        out,
        grad_in,
        small[0:lines].reshape(width),
        small[lines : 2 * lines].reshape(width),
        fqkv[:, 0:third].astype(F32),
        fqkv[:, third : 2 * third].astype(F32),
        fqkv[:, 2 * third :].astype(F32),
        fwo.T.astype(F32),
        fup.astype(F32),
        fdn.astype(F32),
        table_out,
    )


def solution(mesh):
    n_dp = mesh.shape["dp"]
    rows = P(None, ("dp", "mp"), None)
    columns, lines = P(None, "mp"), P("mp", None)
    tables = P(None, None, "mp")
    return jax.shard_map(
        functools.partial(local, n_dp),
        mesh=mesh,
        in_specs=(
            rows, rows, rows, P(None, "dp", None), P(None, "dp"), P(None, None, "dp"),
            P(), P(), columns, columns, columns, lines, columns, lines, tables,
        ),
        out_specs=(
            rows, rows, P(), P(), columns, columns, columns, lines, columns, lines, tables,
        ),
        check_vma=False,
    )
```

```python
import functools
import math

import jax
import jax.numpy as jnp
from jax import lax
from jax.experimental import pallas as pl
from jax.experimental.pallas import tpu as pltpu
from jax.sharding import PartitionSpec as P

BF = jnp.bfloat16
F32 = jnp.float32
HDIM = 64
EPS = 1e-06
MASKED = -1e30
MESH = pl.DeviceIdType.MESH
VMEM = pl.BlockSpec(memory_space=pltpu.VMEM)
ANY = pl.BlockSpec(memory_space=pltpu.HBM)
SHAPE = jax.ShapeDtypeStruct


def dg(a, b, ca, cb):
    return lax.dot_general(a, b, (((ca,), (cb,)), ((), ())), preferred_element_type=F32)


def params(limit=58, **more):
    return pltpu.CompilerParams(vmem_limit_bytes=limit << 20, **more)


class Links:
    def __init__(self, send, recv):
        self.send, self.recv, self.count = send, recv, 0
        self.d, self.m = lax.axis_index("dp"), lax.axis_index("mp")

    def remote(self, src, dst, dp_flip=0, mp_flip=0):
        i = self.count
        self.count += 1
        dp = self.d ^ dp_flip if dp_flip else self.d
        mp = self.m ^ mp_flip if mp_flip else self.m
        return pltpu.make_async_remote_copy(
            src_ref=src,
            dst_ref=dst,
            send_sem=self.send.at[i],
            recv_sem=self.recv.at[i],
            device_id=(dp, mp),
            device_id_type=MESH,
        )

    def local(self, src, dst):
        i = self.count
        self.count += 1
        return pltpu.make_async_copy(src, dst, self.send.at[i])

    def barrier(self, flips):
        sem = pltpu.get_barrier_semaphore()
        for dp_flip, mp_flip in flips:
            dp = self.d ^ dp_flip if dp_flip else self.d
            mp = self.m ^ mp_flip if mp_flip else self.m
            pl.semaphore_signal(sem, inc=1, device_id=(dp, mp), device_id_type=MESH)
        pl.semaphore_wait(sem, len(flips))


def rows_at(start, size, unit):
    return pl.ds(pl.multiple_of(start, unit), size)


def entry_kernel(
    inp, roi, tab, gain, wq, wk, wv, wup,
    xf, tabo, wqkv, qt, kv, upo,
    sent, n1, send, recv,
):
    links = Links(send, recv)
    d, m = links.d, links.m
    rows = inp.shape[1]
    width, third = wq.shape
    piece = width // 8
    core, cross, deep = d & 1, (d >> 1) & 1, (d >> 2) & 1
    place = core * 4 + cross * 2 + deep
    links.barrier(((0, 1), (1, 0), (2, 0), (4, 0)))
    started = []

    def go(copy):
        copy.start()
        started.append(copy)
        return copy

    own_cols = [slice(j * third, (j + 1) * third) for j in range(3)]
    other_cols = [slice((3 + j) * third, (4 + j) * third) for j in range(3)]
    spot = rows_at(place * piece, piece, piece)
    first = [
        go(links.remote(w.at[spot], wqkv.at[spot, c], mp_flip=1))
        for w, c in zip((wq, wk, wv), other_cols)
    ]
    tab_copy = go(links.remote(tab, tabo, mp_flip=1))
    chunk = rows // 2
    row_copies = []
    for j in range(2):
        part = slice(j * chunk, (j + 1) * chunk)
        sent[part] = (inp[1 - m, part].astype(F32) + roi[1 - m, part].astype(F32)).astype(BF)
        here = rows_at(m * rows + j * chunk, chunk, chunk)
        row_copies.append(go(links.remote(sent.at[part], xf.at[here], mp_flip=1)))
    up_copy = go(links.remote(wup.at[spot], upo.at[spot], mp_flip=1))
    for w, c in zip((wq, wk, wv), own_cols):
        wqkv[:, c] = w[...]

    def normalise(where):
        x = xf[where].astype(F32)
        inverse = lax.rsqrt(jnp.mean(x * x, axis=-1, keepdims=True) + EPS)
        n1[where] = (x * inverse * gain[...]).astype(BF)

    own = rows_at(m * rows, rows, rows)
    xf[own] = (inp[m].astype(F32) + roi[m].astype(F32)).astype(BF)
    normalise(own)

    def project(where, side):
        rows_in = n1[where]
        base = side * 3 * third
        kv[where, side * 2 * third : (side + 1) * 2 * third] = dg(
            rows_in, wqkv[:, base + third : base + 3 * third], 1, 0
        ).astype(BF)
        qt[side * third : (side + 1) * third, where] = dg(
            wqkv[:, base : base + third], rows_in, 0, 1
        ).astype(BF)

    project(own, 0)
    stage = first
    for flip, begin, count in (
        (4, place, 1),
        (2, core * 4 + cross * 2, 2),
        (1, core * 4, 4),
    ):
        for copy in stage:
            copy.wait_recv()
        there = wqkv.at[rows_at(begin * piece, count * piece, piece), 3 * third : 6 * third]
        stage = [go(links.remote(there, there, dp_flip=flip))]
    for j in range(2):
        row_copies[j].wait_recv()
        here = rows_at((1 - m) * rows + j * chunk, chunk, chunk)
        normalise(here)
        project(here, 0)
    for copy in stage:
        copy.wait_recv()
    for j in range(2):
        project(slice(j * rows, (j + 1) * rows), 1)
    tab_copy.wait_recv()
    up_copy.wait_recv()
    for copy in started:
        copy.wait_send()


def entry(inputs, roi, tab, gain, wq, wk, wv, wup):
    rows, width = inputs.shape[1], inputs.shape[2]
    third = wq.shape[1]
    tokens = 2 * rows
    return pl.pallas_call(
        entry_kernel,
        out_shape=[
            SHAPE((tokens, width), BF),
            SHAPE(tab.shape, F32),
            SHAPE((width, 6 * third), BF),
            SHAPE((2 * third, tokens), BF),
            SHAPE((tokens, 4 * third), BF),
            SHAPE(wup.shape, BF),
        ],
        in_specs=[VMEM] * 7 + [ANY],
        out_specs=[VMEM] * 5 + [ANY],
        scratch_shapes=[
            pltpu.VMEM((rows, width), BF),
            pltpu.VMEM((tokens, width), BF),
            pltpu.SemaphoreType.DMA((12,)),
            pltpu.SemaphoreType.DMA((12,)),
        ],
        compiler_params=params(58, collective_id=1, has_side_effects=True),
        name="entry",
    )(inputs, roi, tab, gain, wq, wk, wv, wup)


def attend_kernel(
    lengths, live, cells, tab, tabo, qt_ref, k_ref, v_ref, cot, wo, wup, wdn, upo_in,
    p_ref, o_ref, r_ref, hot_ref, hott_ref, dyo, woo, upo, dno,
    kx, qx, vx, mask, mats, send, recv, *, buckets,
):
    links = Links(send, recv)
    d, m = links.d, links.m
    tokens = k_ref.shape[0]
    rows = tokens // 2
    width, hidden = wup.shape
    inner = wo.shape[0]
    step = pl.program_id(0)
    core, cross, deep = d & 1, (d >> 1) & 1, (d >> 2) & 1
    place = core * 4 + cross * 2 + deep
    turned = core * 4 + deep * 2 + cross

    def block(full, begin, count):
        piece = full.shape[0] // 8
        return full.at[rows_at(begin * piece, count * piece, piece)]

    up = functools.partial(block, upo)
    down = functools.partial(block, dno)
    out = functools.partial(block, woo)
    dpiece, opiece = hidden // 8, inner // 8
    down_y = links.remote(
        wdn.at[rows_at(turned * dpiece, dpiece, dpiece)], down(turned, 1), mp_flip=1
    )
    out_y = links.remote(wo.at[rows_at(place * opiece, opiece, opiece)], out(place, 1), mp_flip=1)
    dy_y = links.remote(cot.at[1 - m], dyo, mp_flip=1)
    up_z = links.remote(up(place, 1), up(place, 1), dp_flip=4)
    pair = core * 4 + cross * 2
    up_x = links.remote(up(pair, 2), up(pair, 2), dp_flip=2)
    up_c = links.remote(up(core * 4, 4), up(core * 4, 4), dp_flip=1)
    down_x = links.remote(down(turned, 1), down(turned, 1), dp_flip=2)
    bent = core * 4 + deep * 2
    down_z = links.remote(down(bent, 2), down(bent, 2), dp_flip=4)
    down_c = links.remote(down(core * 4, 4), down(core * 4, 4), dp_flip=1)
    out_z = links.remote(out(place, 1), out(place, 1), dp_flip=4)
    out_x = links.remote(out(pair, 2), out(pair, 2), dp_flip=2)
    out_c = links.remote(out(core * 4, 4), out(core * 4, 4), dp_flip=1)

    def slot0():
        links.barrier(((0, 1), (1, 0), (2, 0), (4, 0)))
        up_z.start()
        down_y.start()
        out_y.start()
        dy_y.start()

    def slot4():
        up_z.wait_recv()
        up_x.start()

    def slot5():
        down_y.wait_recv()
        down_x.start()

    def slot6():
        out_y.wait_recv()
        out_z.start()

    def slot9():
        out_z.wait_recv()
        down_x.wait_recv()
        down_z.start()
        out_x.start()

    def slot11():
        up_x.wait_recv()
        up_c.start()

    def last():
        out_x.wait_recv()
        out_c.start()
        down_z.wait_recv()
        down_c.start()
        for copy in (dy_y, up_c, out_c, down_c):
            copy.wait_recv()
        for copy in (down_y, out_y, dy_y, up_z, up_x, up_c, down_x, down_z, down_c, out_z, out_x, out_c):
            copy.wait_send()

    slots = {0: slot0, 4: slot4, 5: slot5, 6: slot6, 9: slot9, 11: slot11}

    @pl.when(step == 0)
    def _():
        slot0()
        vx[64:80, :] = jnp.ones((16, tokens), BF)
        lane = lax.broadcasted_iota(jnp.int32, (buckets, tokens), 0)
        for t in range(3):
            row = cells[m, t : t + 1, :]
            hott_ref[t * buckets : (t + 1) * buckets, :] = jnp.where(row == lane, 1.0, 0.0).astype(BF)
        hot = hott_ref[...].T
        hot_ref[:, 0:96] = hot
        hot_ref[:, 96:192] = hot
        kx[:, 64:160] = hot
        kx[:, 160:256] = hot
        row_ids = lax.broadcasted_iota(jnp.int32, (1, tokens), 1)
        col_ids = lax.broadcasted_iota(jnp.int32, (tokens, 1), 0)
        seg_row = jnp.zeros((1, tokens), jnp.int32)
        seg_col = jnp.zeros((tokens, 1), jnp.int32)
        end = 0
        for i in range(lengths.shape[2]):
            end = end + lengths[m, 0, i]
            seg_row = seg_row + jnp.where(row_ids >= end, 1, 0)
            seg_col = seg_col + jnp.where(col_ids >= end, 1, 0)
        live_row = live[m].astype(F32)
        live_col = jnp.broadcast_to(live_row, (8, tokens)).T[:, 0:1]
        code = jnp.where(live_col == 1.0, seg_col, -1)
        allowed = (code == seg_row) | (col_ids == row_ids)
        mask[...] = jnp.where(allowed, 0.0, MASKED)
        line = lax.broadcasted_iota(jnp.int32, (128, 128), 0)
        lane = lax.broadcasted_iota(jnp.int32, (128, 128), 1)
        shift = jnp.where(lane < 64, lane, lane - 128)
        bucket = jnp.clip(-shift, -(buckets // 2), buckets // 2 - 1) + buckets // 2
        side = lax.broadcasted_iota(jnp.int32, (buckets, 128), 1)
        heads = mats.shape[0] // 2
        for part, table in enumerate((tab, tabo)):
            exact = table[...]
            upper = exact.astype(BF)
            lower = (exact - upper.astype(F32)).astype(BF)
            for t in range(3):
                pick = jnp.where(line == bucket + t * buckets, 1.0, 0.0).astype(BF)
                inside = (side >= t * buckets) & (side < (t + 1) * buckets)
                for level, source in enumerate((upper, lower)):
                    lines = dg(source, pick, 1, 0)
                    for h in range(heads):
                        wide = jnp.broadcast_to(lines[h : h + 1], (buckets, 128))
                        rolled = pltpu.roll(wide, t * buckets, 1, stride=1, stride_axis=0)
                        begin = level * 3 * buckets + t * buckets
                        mats[part * heads + h, begin : begin + buckets, :] = jnp.where(
                            inside, rolled, 0.0
                        ).astype(BF)

    vt = v_ref[...].T
    for h in range(2):
        for at, action in slots.items():
            if at % 2 == h and at > 0:
                pl.when(step == at // 2)(action)
        span = slice(64 * h, 64 * h + 64)
        kx[:, 0:64] = k_ref[:, span]
        qx[0:64, :] = qt_ref[span, :] * BF(0.125)
        qx[64:256, :] = dg(mats[2 * step + h, :, 0:96], hott_ref[...], 1, 0).astype(BF)
        vx[0:64, :] = vt[span, :]
        s = dg(kx[...], qx[...], 1, 0) + mask[...]
        top = jnp.max(s, axis=0, keepdims=True)
        p = jnp.exp(s - top).astype(BF)
        p_ref[h] = p
        o = dg(vx[...], p, 1, 0)
        r = 1.0 / o[64:65, :]
        o_ref[span, :] = (o[0:64] * r).astype(BF)
        r_ref[0, h : h + 1, :] = r
    pl.when(step == pl.num_programs(0) - 1)(last)


def attend(lengths, live, cells, tab, tabo, qt, kv, cot, wo, wup, wdn, upo, buckets):
    channels, tokens = qt.shape
    width, hidden = wup.shape
    inner = wo.shape[0]
    pairs = channels // 128
    half = pairs // 2
    whole = lambda shape: pl.BlockSpec(shape, lambda i: (0,) * len(shape))
    return pl.pallas_call(
        functools.partial(attend_kernel, buckets=buckets),
        grid=(pairs,),
        in_specs=[
            pl.BlockSpec(memory_space=pltpu.SMEM),
            whole(live.shape),
            whole(cells.shape),
            whole(tab.shape),
            whole(tabo.shape),
            pl.BlockSpec((128, tokens), lambda i: (i, 0)),
            pl.BlockSpec((tokens, 128), lambda i: (0, (i // half) * 2 * half + i % half)),
            pl.BlockSpec((tokens, 128), lambda i: (0, (i // half) * 2 * half + half + i % half)),
            ANY, ANY, ANY, ANY, ANY,
        ],
        out_specs=[
            pl.BlockSpec((2, tokens, tokens), lambda i: (i, 0, 0)),
            pl.BlockSpec((128, tokens), lambda i: (i, 0)),
            pl.BlockSpec((1, 2, tokens), lambda i: (i, 0, 0)),
            whole((tokens, 192)),
            whole((96, tokens)),
            ANY, ANY, ANY, ANY,
        ],
        out_shape=[
            SHAPE((2 * pairs, tokens, tokens), BF),
            SHAPE((channels, tokens), BF),
            SHAPE((pairs, 2, tokens), F32),
            SHAPE((tokens, 192), BF),
            SHAPE((96, tokens), BF),
            SHAPE((tokens // 2, width), BF),
            SHAPE((inner, width), BF),
            SHAPE((width, hidden), BF),
            SHAPE((hidden, width), BF),
        ],
        input_output_aliases={12: 7},
        scratch_shapes=[
            pltpu.VMEM((tokens, 256), BF),
            pltpu.VMEM((256, tokens), BF),
            pltpu.VMEM((80, tokens), BF),
            pltpu.VMEM((tokens, tokens), F32),
            pltpu.VMEM((2 * pairs, 192, 128), BF),
            pltpu.SemaphoreType.DMA((20,)),
            pltpu.SemaphoreType.DMA((20,)),
        ],
        compiler_params=params(58, collective_id=3, has_side_effects=True),
        name="attend",
    )(lengths, live, cells, tab, tabo, qt, kv, kv, cot, wo, wup, wdn, upo)


def attend_back_kernel(
    p_ref, qt_ref, k_ref, v_ref, ot_ref, dot_ref, r_ref, hott_ref, hot_ref,
    dq_ref, dk_ref, dv_ref, gm_ref, vx, dox, kht,
):
    tokens = k_ref.shape[0]

    @pl.when(pl.program_id(0) == 0)
    def _():
        kht[64:160, :] = hott_ref[...]
        lanes = lax.broadcasted_iota(jnp.int32, (tokens, 64), 1)
        vx[:, 64:128] = jnp.where(lanes < 2, -1.0, 0.0).astype(BF)
        dox[64:128, :] = jnp.zeros((64, tokens), BF)

    for h in range(2):
        span = slice(64 * h, 64 * h + 64)
        scaled = dot_ref[span, :].astype(F32) * r_ref[0, h : h + 1, :]
        inner = jnp.sum(scaled * ot_ref[span, :].astype(F32), axis=0, keepdims=True)
        upper = inner.astype(BF)
        lower = (inner - upper.astype(F32)).astype(BF)
        dox[0:64, :] = scaled.astype(BF)
        dox[64:66, :] = jnp.concatenate([upper, lower], 0)
        vx[:, 0:64] = v_ref[:, span]
        kht[0:64, :] = k_ref[:, span].T
        dp = dg(vx[...], dox[...], 1, 0)
        p = p_ref[h]
        ds = (p.astype(F32) * dp).astype(BF)
        dv_ref[:, span] = dg(p, dox[0:64, :], 1, 1).astype(BF)
        dk_ref[:, span] = (dg(ds, qt_ref[span, :], 1, 1) * 0.125).astype(BF)
        both = dg(kht[...], ds, 1, 0)
        dq_ref[:, span] = (both[0:64] * 0.125).astype(BF).T
        left = both[64:160]
        left_hi = left.astype(BF)
        left_lo = (left - left_hi.astype(F32)).astype(BF)
        hot = hot_ref[:, 0:96]
        gm_ref[h] = dg(left_hi, hot, 1, 0) + dg(left_lo, hot, 1, 0)


def attend_back(p, qt, kv, ot, dot, r, hott, hot):
    channels, tokens = qt.shape
    pairs = channels // 128
    half = pairs // 2
    whole = lambda shape: pl.BlockSpec(shape, lambda i: (0,) * len(shape))
    natural = pl.BlockSpec((tokens, 128), lambda i: (0, i))
    turned = pl.BlockSpec((128, tokens), lambda i: (i, 0))
    return pl.pallas_call(
        attend_back_kernel,
        grid=(pairs,),
        in_specs=[
            pl.BlockSpec((2, tokens, tokens), lambda i: (i, 0, 0)),
            turned,
            pl.BlockSpec((tokens, 128), lambda i: (0, (i // half) * 2 * half + i % half)),
            pl.BlockSpec((tokens, 128), lambda i: (0, (i // half) * 2 * half + half + i % half)),
            turned,
            turned,
            pl.BlockSpec((1, 2, tokens), lambda i: (i, 0, 0)),
            whole((96, tokens)),
            whole((tokens, 192)),
        ],
        out_specs=[natural, natural, natural, pl.BlockSpec((2, 96, 96), lambda i: (i, 0, 0))],
        out_shape=[SHAPE((tokens, channels), BF)] * 3 + [SHAPE((2 * pairs, 96, 96), F32)],
        scratch_shapes=[
            pltpu.VMEM((tokens, 128), BF),
            pltpu.VMEM((128, tokens), BF),
            pltpu.VMEM((160, tokens), BF),
        ],
        compiler_params=params(),
        name="attend_back",
    )(p, qt, kv, kv, ot, dot, r, hott, hot)


def middle_kernel(
    x_ref, mixt_ref, wo_in, woo_in, cot, dyo, gain_ref, wup_in, upo_in, wdn_in, dno_in,
    y_ref, gup_ref, gdn_ref, gwo_ref, dh_ref, dmt_ref, gg_ref,
    h1, n2, n2t, yacc, dn, wo_ref, dy_ref,
):
    step = pl.program_id(0)
    early = step < pl.num_programs(0) // 2

    @pl.when(step == 0)
    def _():
        m = lax.axis_index("mp")
        rows = dyo.shape[0]
        dy_ref[rows_at(m * rows, rows, rows)] = cot[m]
        dy_ref[rows_at((1 - m) * rows, rows, rows)] = dyo[...]
        inner = wo_in.shape[0]
        wo_ref[0:inner] = wo_in[...]
        wo_ref[inner:] = woo_in[...]
        added = dg(mixt_ref[...], wo_ref[...], 0, 0)
        h = x_ref[...].astype(F32) + added
        h1[...] = h
        yacc[...] = added
        inverse = lax.rsqrt(jnp.mean(h * h, axis=-1, keepdims=True) + EPS)
        normed = (h * inverse * gain_ref[...]).astype(BF)
        n2[...] = normed
        n2t[...] = normed.T
        dn[...] = jnp.zeros_like(dn)

    wup = jnp.where(early, upo_in[...], wup_in[...])
    wdn = jnp.where(early, dno_in[...], wdn_in[...])
    dy = dy_ref[...]
    u = dg(n2[...], wup, 1, 0)
    cdf = 0.5 * (1.0 + lax.erf(u * 0.7071067811865476))
    act = (u * cdf).astype(BF)
    grad_act = dg(dy, wdn, 1, 1)
    density = jnp.exp(u * u * (-0.5)) * 0.3989422804014327
    du = (grad_act * (cdf + u * density)).astype(BF)
    yacc[...] += dg(act, wdn, 1, 0)
    dn[...] += dg(du, wup, 1, 1)
    gup_ref[...] = dg(n2t[...], du, 1, 0).astype(BF)
    gdn_ref[...] = dg(act, dy, 0, 0).astype(BF)

    @pl.when(step == pl.num_programs(0) - 1)
    def _():
        h = h1[...]
        inverse = lax.rsqrt(jnp.mean(h * h, axis=-1, keepdims=True) + EPS)
        normed = h * inverse
        grad = dn[...]
        gg_ref[...] = jnp.sum(grad * normed, axis=0, keepdims=True)
        inner = grad * gain_ref[...]
        added = inverse * (inner - normed * jnp.mean(inner * normed, axis=-1, keepdims=True))
        dh_ref[...] = added
        y_ref[...] = yacc[...].astype(BF)
        low = (dy_ref[...].astype(F32) + added).astype(BF)
        gwo_ref[...] = dg(low, mixt_ref[...], 0, 1).astype(BF)
        dmt_ref[...] = dg(wo_ref[...], low, 1, 1).astype(BF)


def middle(x, mixt, wo, woo, cot, dyo, gain, wup, upo, wdn, dno, chunk=512):
    tokens, width = x.shape
    hidden = 2 * wup.shape[1]
    n = hidden // chunk
    whole = lambda shape: pl.BlockSpec(shape, lambda i: (0,) * len(shape))
    late = lambda i: jnp.maximum(i - n // 2, 0)
    early = lambda i: jnp.minimum(i, n // 2 - 1)
    slot = lambda i: lax.rem(i + n // 2, n)
    return pl.pallas_call(
        middle_kernel,
        grid=(n,),
        in_specs=[
            whole((tokens, width)),
            whole((width, tokens)),
            whole(wo.shape),
            whole(woo.shape),
            whole(cot.shape),
            whole(dyo.shape),
            whole((1, width)),
            pl.BlockSpec((width, chunk), lambda i: (0, late(i))),
            pl.BlockSpec((width, chunk), lambda i: (0, early(i))),
            pl.BlockSpec((chunk, width), lambda i: (late(i), 0)),
            pl.BlockSpec((chunk, width), lambda i: (early(i), 0)),
        ],
        out_specs=[
            whole((tokens, width)),
            pl.BlockSpec((width, chunk), lambda i: (0, slot(i))),
            pl.BlockSpec((chunk, width), lambda i: (slot(i), 0)),
            whole((width, width)),
            whole((tokens, width)),
            whole((width, tokens)),
            whole((1, width)),
        ],
        out_shape=[
            SHAPE((tokens, width), BF),
            SHAPE((width, hidden), BF),
            SHAPE((hidden, width), BF),
            SHAPE((width, width), BF),
            SHAPE((tokens, width), F32),
            SHAPE((width, tokens), BF),
            SHAPE((1, width), F32),
        ],
        scratch_shapes=[
            pltpu.VMEM((tokens, width), F32),
            pltpu.VMEM((tokens, width), BF),
            pltpu.VMEM((width, tokens), BF),
            pltpu.VMEM((tokens, width), F32),
            pltpu.VMEM((tokens, width), F32),
            pltpu.VMEM((width, width), BF),
            pltpu.VMEM((tokens, width), BF),
        ],
        compiler_params=params(60),
        name="middle",
    )(x, mixt, wo, woo, cot, dyo, gain, wup, upo, wdn, dno)


def finish_kernel(
    x_ref, gain_ref, dh_ref, dq_ref, dk_ref, dv_ref, w_ref,
    gw_ref, gin_ref, gg_ref, n1, dn, *, third,
):
    step = pl.program_id(0)
    x = x_ref[...].astype(F32)

    @pl.when(step == 0)
    def _():
        inverse = lax.rsqrt(jnp.mean(x * x, axis=-1, keepdims=True) + EPS)
        n1[...] = (x * inverse * gain_ref[...]).astype(BF)
        dn[...] = jnp.zeros_like(dn)

    w = w_ref[...]
    total = dn[...]
    for j, ref in enumerate((dq_ref, dk_ref, dv_ref)):
        span = slice(j * third, (j + 1) * third)
        gw_ref[:, span] = dg(n1[...], ref[...], 0, 0).astype(BF)
        total = total + dg(ref[...], w[:, span], 1, 1)
    dn[...] = total

    @pl.when(step == pl.num_programs(0) - 1)
    def _():
        inverse = lax.rsqrt(jnp.mean(x * x, axis=-1, keepdims=True) + EPS)
        normed = x * inverse
        gg_ref[...] = jnp.sum(total * normed, axis=0, keepdims=True)
        inner = total * gain_ref[...]
        added = inverse * (inner - normed * jnp.mean(inner * normed, axis=-1, keepdims=True))
        gin_ref[...] = (dh_ref[...] + added).astype(BF)


def finish(x, gain, dh, dq, dk, dv, wqkv):
    tokens, width = x.shape
    third = wqkv.shape[1] // 6
    whole = lambda shape: pl.BlockSpec(shape, lambda i: (0,) * len(shape))
    part = pl.BlockSpec((tokens, third), lambda i: (0, i))
    return pl.pallas_call(
        functools.partial(finish_kernel, third=third),
        grid=(2,),
        in_specs=[
            whole((tokens, width)),
            whole((1, width)),
            whole((tokens, width)),
            part,
            part,
            part,
            pl.BlockSpec((width, 3 * third), lambda i: (0, i)),
        ],
        out_specs=[
            pl.BlockSpec((width, 3 * third), lambda i: (0, i)),
            whole((tokens, width)),
            whole((1, width)),
        ],
        out_shape=[
            SHAPE((width, 6 * third), BF),
            SHAPE((tokens, width), BF),
            SHAPE((1, width), F32),
        ],
        scratch_shapes=[pltpu.VMEM((tokens, width), BF), pltpu.VMEM((tokens, width), F32)],
        compiler_params=params(),
        name="finish",
    )(x, gain, dh, dq, dk, dv, wqkv)


def reduce_kernel(y, gin, small, gqkv, gwo, gup, gdn, *rest, n_dp):
    (yret, gret, small_out, fqkv, fwo, fup, fdn) = rest[:7]
    grads = (gqkv, gwo, gup, gdn)
    finals = (fqkv, fwo, fup, fdn)
    rc, ry, rx, rz = rest[7:11], rest[11:15], rest[15:19], rest[19:23]
    sums, got = rest[23:25]
    far = rest[25:29] if n_dp > 16 else None
    send, recv = rest[-2:]
    links = Links(send, recv)
    d, m = links.d, links.m
    bits = n_dp.bit_length() - 1
    flips = [(0, 1)] + [(1 << b, 0) for b in range(bits)] + [(12, 0)]
    flips += [(r << 4, 0) for r in range(1, n_dp // 16) if r & (r - 1)]
    links.barrier(flips)
    core, cross, deep = d & 1, (d >> 1) & 1, (d >> 2) & 3
    rows = y.shape[0] // 2
    started = []

    def go(copy):
        copy.start()
        started.append(copy)
        return copy

    mine = rows_at(m * rows, rows, rows)
    theirs = rows_at((1 - m) * rows, rows, rows)
    locals_ = [links.local(y.at[mine], yret.at[m]), links.local(gin.at[mine], gret.at[m])]
    for copy in locals_:
        copy.start()

    def half(i, side, start, count, ref, based):
        own = finals[i].shape
        if i == 3:
            base = side * own[0] if based else 0
            return ref.at[rows_at(base + start, count, 16)]
        cols = slice(side * own[1], (side + 1) * own[1])
        return ref.at[rows_at(start, count, 16), cols]

    order = (3, 2, 0, 1)
    size = [f.shape[0] for f in finals]
    copies = {}

    def start_core(i):
        n = size[i] // 2
        for side in range(2):
            src = half(i, side, (1 - core) * n, n, grads[i], True)
            copies["c", i, side] = go(links.remote(src, rc[i].at[side], dp_flip=1))

    def start_y(i):
        n = size[i] // 2
        for side in range(2):
            copies["c", i, side].wait_recv()
            src = half(i, side, core * n, n, grads[i], True)
            rc[i][side] = (rc[i][side].astype(F32) + src[...].astype(F32)).astype(BF)
        copies["y", i] = go(links.remote(rc[i].at[1], ry[i], mp_flip=1))

    def start_x(i):
        n = size[i] // 4
        copies["y", i].wait_recv()
        ry[i][...] = (ry[i][...].astype(F32) + rc[i][0].astype(F32)).astype(BF)
        src = ry[i].at[rows_at((1 - cross) * n, n, 16)]
        copies["x", i] = go(links.remote(src, rx[i], dp_flip=2))

    def start_z(i):
        n = size[i] // 16
        copies["x", i].wait_recv()
        keep = ry[i][rows_at(cross * size[i] // 4, size[i] // 4, 16)]
        rx[i][...] = (rx[i][...].astype(F32) + keep.astype(F32)).astype(BF)
        for r in range(1, 4):
            src = rx[i].at[rows_at((deep ^ r) * n, n, 16)]
            copies["z", i, r] = go(links.remote(src, rz[i].at[r - 1], dp_flip=r << 2))

    def place(i, count):
        n = size[i] // 16
        at = {1: core * 8 + cross * 4 + deep, 4: core * 8 + cross * 4, 8: core * 8}[count]
        return finals[i].at[rows_at(at * n, count * n, 16)]

    def start_back_z(i):
        n = size[i] // 16
        for r in range(1, 4):
            copies["z", i, r].wait_recv()
        total = rx[i][rows_at(deep * n, n, 16)].astype(F32)
        for r in range(3):
            total = total + rz[i][r].astype(F32)
        if far is not None:
            rz_own = far[i]
            rz_own[0] = total.astype(BF)
            group = [
                go(links.remote(rz_own.at[0], rz_own.at[r], dp_flip=r << 4))
                for r in range(1, n_dp // 16)
            ]
            for r, copy in enumerate(group):
                copy.wait_recv()
                total = total + rz_own[r + 1].astype(F32)
        spot = place(i, 1)
        spot[...] = total.astype(BF)
        for r in range(1, 4):
            copies["bz", i, r] = go(links.remote(spot, spot, dp_flip=r << 2))

    def start_back_x(i):
        for r in range(1, 4):
            copies["bz", i, r].wait_recv()
        spot = place(i, 4)
        copies["bx", i] = go(links.remote(spot, spot, dp_flip=2))

    def start_back_c(i):
        copies["bx", i].wait_recv()
        spot = place(i, 8)
        copies["bc", i] = go(links.remote(spot, spot, dp_flip=1))

    def end(i):
        copies["bc", i].wait_recv()

    stages = (start_core, start_y, start_x, start_z, start_back_z, start_back_x, start_back_c, end)
    sums[0] = small[...]
    n_small = bits + 1
    tick = 0
    for t in range(len(stages) + len(order) - 1):
        for j, i in enumerate(order):
            if 0 <= t - j < len(stages):
                stages[t - j](i)
        if t == 3:
            row_copies = [
                go(links.remote(y.at[theirs], yret.at[m], mp_flip=1)),
                go(links.remote(gin.at[theirs], gret.at[m], mp_flip=1)),
            ]
        if tick <= n_small:
            if tick > 0:
                hop.wait_recv()
                if tick == 1:
                    sums[1, 0:16] = sums[0, 0:16] + got[0, 0:16]
                    sums[1, 16:24] = sums[0, 16:24] + got[0, 24:32]
                    sums[1, 24:32] = jnp.zeros_like(sums[0, 24:32])
                else:
                    sums[tick] = sums[tick - 1] + got[tick - 1]
            if tick < n_small:
                flip = (0, 1) if tick == 0 else (1 << (tick - 1), 0)
                hop = go(links.remote(sums.at[tick], got.at[tick], dp_flip=flip[0], mp_flip=flip[1]))
            tick += 1
    small_out[...] = sums[n_small]
    for copy in row_copies:
        copy.wait_recv()
    for copy in started:
        copy.wait_send()
    for copy in locals_:
        copy.wait()


def reduce_all(y, gin, small, gqkv, gwo, gup, gdn, n_dp):
    tokens, width = y.shape
    own = (
        (width, gqkv.shape[1] // 2),
        (width, gwo.shape[1] // 2),
        (width, gup.shape[1] // 2),
        (gdn.shape[0] // 2, width),
    )
    bits = n_dp.bit_length() - 1
    scratch = [pltpu.VMEM((2, a // 2, b), BF) for a, b in own]
    scratch += [pltpu.VMEM((a // 2, b), BF) for a, b in own]
    scratch += [pltpu.VMEM((a // 4, b), BF) for a, b in own]
    scratch += [pltpu.VMEM((3, a // 16, b), BF) for a, b in own]
    scratch += [pltpu.VMEM((bits + 2,) + small.shape, F32)] * 2
    count = 80
    if n_dp > 16:
        scratch += [pltpu.VMEM((n_dp // 16, a // 16, b), BF) for a, b in own]
        count += 4 * (n_dp // 16)
    scratch += [pltpu.SemaphoreType.DMA((count,))] * 2
    return pl.pallas_call(
        functools.partial(reduce_kernel, n_dp=n_dp),
        out_shape=[
            SHAPE((2, tokens // 2, width), BF),
            SHAPE((2, tokens // 2, width), BF),
            SHAPE(small.shape, F32),
        ]
        + [SHAPE(s, BF) for s in own],
        in_specs=[ANY, ANY] + [VMEM] * 5,
        out_specs=[ANY, ANY] + [VMEM] * 5,
        scratch_shapes=scratch,
        compiler_params=params(60, collective_id=2, has_side_effects=True),
        name="reduce",
    )(y, gin, small, gqkv, gwo, gup, gdn)


def local(
    n_dp, inputs, roi, cotangent, doc_lengths, live_mask, bucket_cells,
    gain_attn, gain_ffn, w_query, w_key, w_value, w_out, w_up, w_down, tables,
):
    rows, width = inputs.shape[1], inputs.shape[2]
    tokens = 2 * rows
    third = w_query.shape[1]
    heads = third // HDIM
    buckets = tables.shape[1]
    half = buckets // 2
    tab = jnp.pad(
        tables.transpose(2, 0, 1).reshape(heads, 3 * buckets), ((0, 2), (0, 128 - 3 * buckets))
    )
    ga, gf = gain_attn.reshape(1, width), gain_ffn.reshape(1, width)
    x, tabo, wqkv, qt, kv, upo = entry(
        inputs, roi, tab, ga, w_query, w_key, w_value, w_up
    )
    p, mixt, r, hot, hott, dyo, woo, upo, dno = attend(
        doc_lengths, live_mask.reshape(2, 1, tokens), bucket_cells, tab, tabo, qt, kv,
        cotangent, w_out, w_up, w_down, upo, buckets,
    )
    y, gup, gdn, gwo, dh, dmt, gain_f = middle(x, mixt, w_out, woo, cotangent, dyo, gf, w_up, upo, w_down, dno)
    dq, dk, dv, gmats = attend_back(p, qt, kv, mixt, dmt, r, hott, hot)
    gqkv, gin, gain_a = finish(x, ga, dh, dq, dk, dv, wqkv)

    cell_ids = jnp.arange(buckets)
    relative = jnp.clip(cell_ids[:, None] - cell_ids[None, :], -half, half - 1) + half
    select = (relative[:, :, None] == cell_ids).astype(F32)
    gblocks = jnp.stack(
        [gmats[:, t * buckets : (t + 1) * buckets, t * buckets : (t + 1) * buckets] for t in range(3)],
        axis=1,
    )
    gtab = jnp.einsum("haxy,xyn->han", gblocks, select, precision=lax.Precision.HIGHEST)
    gtab = jnp.pad(
        gtab.reshape(2, heads, 3 * buckets), ((0, 0), (0, 2), (0, 128 - 3 * buckets))
    ).reshape(16, 128)
    small = jnp.concatenate(
        [gain_a.reshape(-1, 128), gain_f.reshape(-1, 128), jnp.zeros((4, 128), F32), gtab], 0
    )
    yret, gret, small, fqkv, fwo, fup, fdn = reduce_all(y, gin, small, gqkv, gwo, gup, gdn, n_dp)
    lines = width // 128
    out = inputs.astype(F32) + roi.astype(F32) + yret.astype(F32)
    grad_in = cotangent.astype(F32) + gret.astype(F32)
    table_out = small[16 : 16 + heads, : 3 * buckets].reshape(heads, 3, buckets).transpose(1, 2, 0)
    return (
        out,
        grad_in,
        small[0:lines].reshape(width),
        small[lines : 2 * lines].reshape(width),
        fqkv[:, 0:third].astype(F32),
        fqkv[:, third : 2 * third].astype(F32),
        fqkv[:, 2 * third :].astype(F32),
        fwo.T.astype(F32),
        fup.astype(F32),
        fdn.astype(F32),
        table_out,
    )


def solution(mesh):
    n_dp = mesh.shape["dp"]
    rows = P(None, ("dp", "mp"), None)
    columns, lines = P(None, "mp"), P("mp", None)
    tables = P(None, None, "mp")
    return jax.shard_map(
        functools.partial(local, n_dp),
        mesh=mesh,
        in_specs=(
            rows, rows, rows, P(None, "dp", None), P(None, "dp"), P(None, None, "dp"),
            P(), P(), columns, columns, columns, lines, columns, lines, tables,
        ),
        out_specs=(
            rows, rows, P(), P(), columns, columns, columns, lines, columns, lines, tables,
        ),
        check_vma=False,
    )
```

```python
import functools
import math

import jax
import jax.numpy as jnp
from jax import lax
from jax.experimental import pallas as pl
from jax.experimental.pallas import tpu as pltpu
from jax.sharding import PartitionSpec as P

BF = jnp.bfloat16
F32 = jnp.float32
HDIM = 64
EPS = 1e-06
MASKED = -1e30
MESH = pl.DeviceIdType.MESH
VMEM = pl.BlockSpec(memory_space=pltpu.VMEM)
ANY = pl.BlockSpec(memory_space=pltpu.HBM)
SHAPE = jax.ShapeDtypeStruct


def dg(a, b, ca, cb):
    return lax.dot_general(a, b, (((ca,), (cb,)), ((), ())), preferred_element_type=F32)


def params(limit=58, **more):
    return pltpu.CompilerParams(vmem_limit_bytes=limit << 20, **more)


class Copy:
    def __init__(self, make):
        self.make = make

    def start(self):
        self.make().start()

    def wait(self):
        self.make().wait()

    def wait_recv(self):
        self.make().wait_recv()

    def wait_send(self):
        self.make().wait_send()


def now(ref):
    return ref() if callable(ref) else ref


class Links:
    def __init__(self, send, recv):
        self.send, self.recv, self.count = send, recv, 0
        self.d, self.m = lax.axis_index("dp"), lax.axis_index("mp")

    def flipped(self, dp_flip, mp_flip):
        dp = self.d ^ dp_flip if dp_flip else self.d
        mp = self.m ^ mp_flip if mp_flip else self.m
        return dp, mp

    def remote(self, src, dst, dp_flip=0, mp_flip=0):
        i = self.count
        self.count += 1
        return Copy(
            lambda: pltpu.make_async_remote_copy(
                src_ref=now(src),
                dst_ref=now(dst),
                send_sem=self.send.at[i],
                recv_sem=self.recv.at[i],
                device_id=self.flipped(dp_flip, mp_flip),
                device_id_type=MESH,
            )
        )

    def local(self, src, dst):
        i = self.count
        self.count += 1
        return Copy(lambda: pltpu.make_async_copy(now(src), now(dst), self.send.at[i]))

    def barrier(self, flips):
        sem = pltpu.get_barrier_semaphore()
        for flip in flips:
            pl.semaphore_signal(
                sem, inc=1, device_id=self.flipped(*flip), device_id_type=MESH
            )
        pl.semaphore_wait(sem, len(flips))


def rows_at(start, size, unit):
    return pl.ds(pl.multiple_of(start, unit), size)


def entry_kernel(
    inp, roi, tab, gain, wq, wk, wv, wup,
    xf, tabo, wqkv, qt, kv, upo,
    sent, n1, send, recv,
):
    links = Links(send, recv)
    d, m = links.d, links.m
    rows = inp.shape[1]
    width, third = wq.shape
    piece = width // 8
    core, cross, deep = d & 1, (d >> 1) & 1, (d >> 2) & 1
    place = core * 4 + cross * 2 + deep
    links.barrier(((0, 1), (1, 0), (2, 0), (4, 0)))
    started = []

    def go(copy):
        copy.start()
        started.append(copy)
        return copy

    own_cols = [slice(j * third, (j + 1) * third) for j in range(3)]
    other_cols = [slice((3 + j) * third, (4 + j) * third) for j in range(3)]
    spot = rows_at(place * piece, piece, piece)
    first = [
        go(links.remote(w.at[spot], wqkv.at[spot, c], mp_flip=1))
        for w, c in zip((wq, wk, wv), other_cols)
    ]
    tab_copy = go(links.remote(tab, tabo, mp_flip=1))
    chunk = rows // 2
    row_copies = []
    for j in range(2):
        part = slice(j * chunk, (j + 1) * chunk)
        sent[part] = (inp[1 - m, part].astype(F32) + roi[1 - m, part].astype(F32)).astype(BF)
        here = rows_at(m * rows + j * chunk, chunk, chunk)
        row_copies.append(go(links.remote(sent.at[part], xf.at[here], mp_flip=1)))
    up_copy = go(links.remote(wup.at[spot], upo.at[spot], mp_flip=1))
    for w, c in zip((wq, wk, wv), own_cols):
        wqkv[:, c] = w[...]

    def normalise(where):
        x = xf[where].astype(F32)
        inverse = lax.rsqrt(jnp.mean(x * x, axis=-1, keepdims=True) + EPS)
        n1[where] = (x * inverse * gain[...]).astype(BF)

    own = rows_at(m * rows, rows, rows)
    xf[own] = (inp[m].astype(F32) + roi[m].astype(F32)).astype(BF)
    normalise(own)

    def project(where, side):
        rows_in = n1[where]
        base = side * 3 * third
        kv[where, side * 2 * third : (side + 1) * 2 * third] = dg(
            rows_in, wqkv[:, base + third : base + 3 * third], 1, 0
        ).astype(BF)
        qt[side * third : (side + 1) * third, where] = dg(
            wqkv[:, base : base + third], rows_in, 0, 1
        ).astype(BF)

    project(own, 0)
    stage = first
    for flip, begin, count in (
        (4, place, 1),
        (2, core * 4 + cross * 2, 2),
        (1, core * 4, 4),
    ):
        for copy in stage:
            copy.wait_recv()
        there = wqkv.at[rows_at(begin * piece, count * piece, piece), 3 * third : 6 * third]
        stage = [go(links.remote(there, there, dp_flip=flip))]
    for j in range(2):
        row_copies[j].wait_recv()
        here = rows_at((1 - m) * rows + j * chunk, chunk, chunk)
        normalise(here)
        project(here, 0)
    for copy in stage:
        copy.wait_recv()
    for j in range(2):
        project(slice(j * rows, (j + 1) * rows), 1)
    tab_copy.wait_recv()
    up_copy.wait_recv()
    for copy in started:
        copy.wait_send()


def entry(inputs, roi, tab, gain, wq, wk, wv, wup):
    rows, width = inputs.shape[1], inputs.shape[2]
    third = wq.shape[1]
    tokens = 2 * rows
    return pl.pallas_call(
        entry_kernel,
        out_shape=[
            SHAPE((tokens, width), BF),
            SHAPE(tab.shape, F32),
            SHAPE((width, 6 * third), BF),
            SHAPE((2 * third, tokens), BF),
            SHAPE((tokens, 4 * third), BF),
            SHAPE(wup.shape, BF),
        ],
        in_specs=[VMEM] * 7 + [ANY],
        out_specs=[VMEM] * 5 + [ANY],
        scratch_shapes=[
            pltpu.VMEM((rows, width), BF),
            pltpu.VMEM((tokens, width), BF),
            pltpu.SemaphoreType.DMA((12,)),
            pltpu.SemaphoreType.DMA((12,)),
        ],
        compiler_params=params(58, collective_id=1, has_side_effects=True),
        name="entry",
    )(inputs, roi, tab, gain, wq, wk, wv, wup)


def attend_kernel(
    lengths, live, cells, tab, tabo, qt_ref, k_ref, v_ref, cot, wo, wup, wdn, upo_in,
    p_ref, o_ref, r_ref, hot_ref, back_ref, dyo, woo, upo, dno,
    kx, qx, vx, mask, mats, hott_ref, send, recv, *, buckets,
):
    links = Links(send, recv)
    d, m = links.d, links.m
    tokens = k_ref.shape[0]
    rows = tokens // 2
    width, hidden = wup.shape
    inner = wo.shape[0]
    step = pl.program_id(0)
    core, cross, deep = d & 1, (d >> 1) & 1, (d >> 2) & 1
    place = core * 4 + cross * 2 + deep
    turned = core * 4 + deep * 2 + cross

    def block(full, begin, count):
        piece = full.shape[0] // 8
        return full.at[rows_at(begin * piece, count * piece, piece)]

    up = functools.partial(block, upo)
    down = functools.partial(block, dno)
    out = functools.partial(block, woo)
    dpiece, opiece = hidden // 8, inner // 8
    down_y = links.remote(
        wdn.at[rows_at(turned * dpiece, dpiece, dpiece)], down(turned, 1), mp_flip=1
    )
    out_y = links.remote(wo.at[rows_at(place * opiece, opiece, opiece)], out(place, 1), mp_flip=1)
    dy_y = links.remote(cot.at[1 - m], dyo, mp_flip=1)
    up_z = links.remote(up(place, 1), up(place, 1), dp_flip=4)
    pair = core * 4 + cross * 2
    up_x = links.remote(up(pair, 2), up(pair, 2), dp_flip=2)
    up_c = links.remote(up(core * 4, 4), up(core * 4, 4), dp_flip=1)
    down_x = links.remote(down(turned, 1), down(turned, 1), dp_flip=2)
    bent = core * 4 + deep * 2
    down_z = links.remote(down(bent, 2), down(bent, 2), dp_flip=4)
    down_c = links.remote(down(core * 4, 4), down(core * 4, 4), dp_flip=1)
    out_z = links.remote(out(place, 1), out(place, 1), dp_flip=4)
    out_x = links.remote(out(pair, 2), out(pair, 2), dp_flip=2)
    out_c = links.remote(out(core * 4, 4), out(core * 4, 4), dp_flip=1)

    def slot0():
        links.barrier(((0, 1), (1, 0), (2, 0), (4, 0)))
        up_z.start()
        down_y.start()
        out_y.start()
        dy_y.start()

    def slot4():
        up_z.wait_recv()
        up_x.start()

    def slot5():
        down_y.wait_recv()
        down_x.start()

    def slot6():
        out_y.wait_recv()
        out_z.start()

    def slot9():
        out_z.wait_recv()
        down_x.wait_recv()
        down_z.start()
        out_x.start()

    def slot11():
        up_x.wait_recv()
        up_c.start()

    def last():
        out_x.wait_recv()
        out_c.start()
        down_z.wait_recv()
        down_c.start()
        for copy in (dy_y, up_c, out_c, down_c):
            copy.wait_recv()
        for copy in (down_y, out_y, dy_y, up_z, up_x, up_c, down_x, down_z, down_c, out_z, out_x, out_c):
            copy.wait_send()

    slots = {0: slot0, 4: slot4, 5: slot5, 6: slot6, 9: slot9, 11: slot11}

    @pl.when(step == 0)
    def _():
        slot0()
        vx[64:80, :] = jnp.ones((16, tokens), BF)
        lane = lax.broadcasted_iota(jnp.int32, (buckets, tokens), 0)
        for t in range(3):
            row = cells[m, t : t + 1, :]
            hott_ref[t * buckets : (t + 1) * buckets, :] = jnp.where(row == lane, 1.0, 0.0).astype(BF)
            mirror = jnp.where(row == buckets - 1 - lane, 1.0, 0.0).astype(BF)
            back_ref[t * buckets : (t + 1) * buckets, :] = mirror
        hott_ref[96:128, :] = jnp.zeros((32, tokens), BF)
        wide_hot = hott_ref[...].T
        hot_ref[...] = wide_hot
        hot = wide_hot[:, 0:96]
        kx[:, 64:160] = hot
        kx[:, 160:256] = hot
        row_ids = lax.broadcasted_iota(jnp.int32, (1, tokens), 1)
        col_ids = lax.broadcasted_iota(jnp.int32, (tokens, 1), 0)
        seg_row = jnp.zeros((1, tokens), jnp.int32)
        seg_col = jnp.zeros((tokens, 1), jnp.int32)
        end = 0
        for i in range(lengths.shape[2]):
            end = end + lengths[m, 0, i]
            seg_row = seg_row + jnp.where(row_ids >= end, 1, 0)
            seg_col = seg_col + jnp.where(col_ids >= end, 1, 0)
        live_row = live[m].astype(F32)
        live_col = jnp.broadcast_to(live_row, (8, tokens)).T[:, 0:1]
        code = jnp.where(live_col == 1.0, seg_col, -1)
        allowed = (code == seg_row) | (col_ids == row_ids)
        mask[...] = jnp.where(allowed, 0.0, MASKED)
        line = lax.broadcasted_iota(jnp.int32, (128, 128), 0)
        lane = lax.broadcasted_iota(jnp.int32, (128, 128), 1)
        shift = jnp.where(lane < 64, lane, lane - 128)
        bucket = jnp.clip(-shift, -(buckets // 2), buckets // 2 - 1) + buckets // 2
        side = lax.broadcasted_iota(jnp.int32, (buckets, 128), 1)
        heads = mats.shape[0] // 2
        for part, table in enumerate((tab, tabo)):
            exact = table[...]
            upper = exact.astype(BF)
            lower = (exact - upper.astype(F32)).astype(BF)
            for t in range(3):
                pick = jnp.where(line == bucket + t * buckets, 1.0, 0.0).astype(BF)
                inside = (side >= t * buckets) & (side < (t + 1) * buckets)
                for level, source in enumerate((upper, lower)):
                    lines = dg(source, pick, 1, 0)
                    for h in range(heads):
                        wide = jnp.broadcast_to(lines[h : h + 1], (buckets, 128))
                        rolled = pltpu.roll(wide, t * buckets, 1, stride=1, stride_axis=0)
                        begin = level * 3 * buckets + t * buckets
                        mats[part * heads + h, begin : begin + buckets, :] = jnp.where(
                            inside, rolled, 0.0
                        ).astype(BF)

    vt = v_ref[...].T
    for h in range(2):
        for at, action in slots.items():
            if at % 2 == h and at > 0:
                pl.when(step == at // 2)(action)
        span = slice(64 * h, 64 * h + 64)
        kx[:, 0:64] = k_ref[:, span]
        qx[0:64, :] = qt_ref[span, :] * BF(0.125)
        qx[64:256, :] = dg(mats[2 * step + h], hott_ref[...], 1, 0).astype(BF)
        vx[0:64, :] = vt[span, :]
        s = dg(kx[...], qx[...], 1, 0) + mask[...]
        top = jnp.max(s, axis=0, keepdims=True)
        p = jnp.exp(s - top).astype(BF)
        p_ref[h] = p
        o = dg(vx[...], p, 1, 0)
        r = 1.0 / o[64:65, :]
        o_ref[span, :] = (o[0:64] * r).astype(BF)
        r_ref[0, h : h + 1, :] = r
    pl.when(step == pl.num_programs(0) - 1)(last)


def attend(lengths, live, cells, tab, tabo, qt, kv, cot, wo, wup, wdn, upo, buckets):
    channels, tokens = qt.shape
    width, hidden = wup.shape
    inner = wo.shape[0]
    pairs = channels // 128
    half = pairs // 2
    whole = lambda shape: pl.BlockSpec(shape, lambda i: (0,) * len(shape))
    return pl.pallas_call(
        functools.partial(attend_kernel, buckets=buckets),
        grid=(pairs,),
        in_specs=[
            pl.BlockSpec(memory_space=pltpu.SMEM),
            whole(live.shape),
            whole(cells.shape),
            whole(tab.shape),
            whole(tabo.shape),
            pl.BlockSpec((128, tokens), lambda i: (i, 0)),
            pl.BlockSpec((tokens, 128), lambda i: (0, (i // half) * 2 * half + i % half)),
            pl.BlockSpec((tokens, 128), lambda i: (0, (i // half) * 2 * half + half + i % half)),
            ANY, ANY, ANY, ANY, ANY,
        ],
        out_specs=[
            pl.BlockSpec((2, tokens, tokens), lambda i: (i, 0, 0)),
            pl.BlockSpec((128, tokens), lambda i: (i, 0)),
            pl.BlockSpec((1, 2, tokens), lambda i: (i, 0, 0)),
            whole((tokens, 128)),
            whole((96, tokens)),
            ANY, ANY, ANY, ANY,
        ],
        out_shape=[
            SHAPE((2 * pairs, tokens, tokens), BF),
            SHAPE((channels, tokens), BF),
            SHAPE((pairs, 2, tokens), F32),
            SHAPE((tokens, 128), BF),
            SHAPE((96, tokens), BF),
            SHAPE((tokens // 2, width), BF),
            SHAPE((inner, width), BF),
            SHAPE((width, hidden), BF),
            SHAPE((hidden, width), BF),
        ],
        input_output_aliases={12: 7},
        scratch_shapes=[
            pltpu.VMEM((tokens, 256), BF),
            pltpu.VMEM((256, tokens), BF),
            pltpu.VMEM((80, tokens), BF),
            pltpu.VMEM((tokens, tokens), F32),
            pltpu.VMEM((2 * pairs, 192, 128), BF),
            pltpu.VMEM((128, tokens), BF),
            pltpu.SemaphoreType.DMA((20,)),
            pltpu.SemaphoreType.DMA((20,)),
        ],
        compiler_params=params(58, collective_id=3, has_side_effects=True),
        name="attend",
    )(lengths, live, cells, tab, tabo, qt, kv, kv, cot, wo, wup, wdn, upo)


def middle_kernel(
    x_ref, mixt_ref, wo_in, woo_in, cot, dyo, gain_ref, wup_in, upo_in, wdn_in, dno_in,
    y_ref, gwo_ref, dh_ref, dmt_ref, gg_ref,
    sum1u, sum1d, sum2u, sum2d, own3u, own3d, far3u, far3d,
    h1, n2, n2t, yacc, dn, wo_ref, dy_ref, gu, gd, rcu, rcd, ryu, ryd, send, recv,
):
    links = Links(send, recv)
    core = links.d & 1
    step = pl.program_id(0)
    last = pl.num_programs(0) - 1
    half_steps = pl.num_programs(0) // 2
    early = step < half_steps
    width, chunk = gu.shape[1:]
    keep_u, give_u = (rows_at(c * (width // 2), width // 2, 16) for c in (core, 1 - core))
    keep_d, give_d = (rows_at(c * (chunk // 2), chunk // 2, 16) for c in (core, 1 - core))

    def core_copies(i):
        return (
            pltpu.make_async_remote_copy(
                gu.at[i % 2, give_u], rcu.at[i], send.at[0, i], recv.at[0, i],
                device_id=(links.d ^ 1, links.m), device_id_type=MESH,
            ),
            pltpu.make_async_remote_copy(
                gd.at[i % 2, give_d], rcd.at[i], send.at[1, i], recv.at[1, i],
                device_id=(links.d ^ 1, links.m), device_id_type=MESH,
            ),
        )

    def pair_copies(i):
        return (
            pltpu.make_async_remote_copy(
                rcu.at[i], ryu.at[i], send.at[2, i], recv.at[2, i],
                device_id=(links.d, 1 - links.m), device_id_type=MESH,
            ),
            pltpu.make_async_remote_copy(
                rcd.at[i], ryd.at[i], send.at[3, i], recv.at[3, i],
                device_id=(links.d, 1 - links.m), device_id_type=MESH,
            ),
        )

    def settle(i):
        for copy in core_copies(i):
            copy.wait_recv()
        for copy in core_copies(i):
            copy.wait_send()
        rcu[i] = (rcu[i].astype(F32) + gu[i % 2, keep_u].astype(F32)).astype(BF)
        rcd[i] = (rcd[i].astype(F32) + gd[i % 2, keep_d].astype(F32)).astype(BF)

    @pl.when(step == 0)
    def _():
        links.barrier(((0, 1), (1, 0)))
        m = links.m
        rows = dyo.shape[0]
        dy_ref[rows_at(m * rows, rows, rows)] = cot[m]
        dy_ref[rows_at((1 - m) * rows, rows, rows)] = dyo[...]
        inner = wo_in.shape[0]
        wo_ref[0:inner] = wo_in[...]
        wo_ref[inner:] = woo_in[...]
        added = dg(mixt_ref[...], wo_ref[...], 0, 0)
        h = x_ref[...].astype(F32) + added
        h1[...] = h
        yacc[...] = added
        inverse = lax.rsqrt(jnp.mean(h * h, axis=-1, keepdims=True) + EPS)
        normed = (h * inverse * gain_ref[...]).astype(BF)
        n2[...] = normed
        n2t[...] = normed.T
        dn[...] = jnp.zeros_like(dn)

    wup = jnp.where(early, upo_in[...], wup_in[...])
    wdn = jnp.where(early, dno_in[...], wdn_in[...])
    dy = dy_ref[...]
    u = dg(n2[...], wup, 1, 0)
    cdf = 0.5 * (1.0 + lax.erf(u * 0.7071067811865476))
    act = (u * cdf).astype(BF)
    grad_act = dg(dy, wdn, 1, 1)
    density = jnp.exp(u * u * (-0.5)) * 0.3989422804014327
    du = (grad_act * (cdf + u * density)).astype(BF)
    yacc[...] += dg(act, wdn, 1, 0)

    @pl.when(step > 0)
    def _():
        settle(step - 1)

    @pl.when((step > 0) & (step < half_steps))
    def _():
        for copy in pair_copies(step - 1):
            copy.start()

    dn[...] += dg(du, wup, 1, 1)
    gu[step % 2] = dg(n2t[...], du, 1, 0).astype(BF)
    gd[step % 2] = dg(act, dy, 0, 0).astype(BF)
    for copy in core_copies(step):
        copy.start()

    @pl.when(step == last)
    def _():
        h = h1[...]
        inverse = lax.rsqrt(jnp.mean(h * h, axis=-1, keepdims=True) + EPS)
        normed = h * inverse
        grad = dn[...]
        gg_ref[...] = jnp.sum(grad * normed, axis=0, keepdims=True)
        inner = grad * gain_ref[...]
        added = inverse * (inner - normed * jnp.mean(inner * normed, axis=-1, keepdims=True))
        dh_ref[...] = added
        y_ref[...] = yacc[...].astype(BF)
        low = (dy_ref[...].astype(F32) + added).astype(BF)
        gwo_ref[...] = dg(low, mixt_ref[...], 0, 1).astype(BF)
        dmt_ref[...] = dg(wo_ref[...], low, 1, 1).astype(BF)
        settle(last)
        n = rcu.shape[0] // 2
        for k, (out_u, out_d) in enumerate(((sum1u, sum1d), (sum2u, sum2d))):
            for copy in pair_copies(k):
                copy.wait_recv()
            out_u[...] = (rcu[n + k].astype(F32) + ryu[k].astype(F32)).astype(BF)
            out_d[...] = (rcd[n + k].astype(F32) + ryd[k].astype(F32)).astype(BF)
        own3u[...] = rcu[n + 2]
        own3d[...] = rcd[n + 2]
        far3u[...] = rcu[2]
        far3d[...] = rcd[2]
        for k in range(2):
            for copy in pair_copies(k):
                copy.wait_send()


def middle(x, mixt, wo, woo, cot, dyo, gain, wup, upo, wdn, dno):
    tokens, width = x.shape
    half = wup.shape[1]
    chunk = half // 3
    n = 6
    once = lambda shape: pl.BlockSpec(
        shape, lambda i: (0,) * len(shape), pipeline_mode=pl.Buffered(1)
    )
    late = lambda i: jnp.maximum(i - n // 2, 0)
    early = lambda i: jnp.minimum(i, n // 2 - 1)
    part_u, part_d = (width // 2, chunk), (chunk // 2, width)
    outs = [
        ((tokens, width), BF),
        ((width, width), BF),
        ((tokens, width), F32),
        ((width, tokens), BF),
        ((1, width), F32),
    ] + [(part_u, BF), (part_d, BF)] * 4
    return pl.pallas_call(
        middle_kernel,
        grid=(n,),
        in_specs=[
            once((tokens, width)),
            once((width, tokens)),
            once(wo.shape),
            once(woo.shape),
            once(cot.shape),
            once(dyo.shape),
            once((1, width)),
            pl.BlockSpec((width, chunk), lambda i: (0, late(i))),
            pl.BlockSpec((width, chunk), lambda i: (0, early(i))),
            pl.BlockSpec((chunk, width), lambda i: (late(i), 0)),
            pl.BlockSpec((chunk, width), lambda i: (early(i), 0)),
        ],
        out_specs=[once(shape) for shape, _ in outs],
        out_shape=[SHAPE(*entry) for entry in outs],
        scratch_shapes=[
            pltpu.VMEM((tokens, width), F32),
            pltpu.VMEM((tokens, width), BF),
            pltpu.VMEM((width, tokens), BF),
            pltpu.VMEM((tokens, width), F32),
            pltpu.VMEM((tokens, width), F32),
            pltpu.VMEM((width, width), BF),
            pltpu.VMEM((tokens, width), BF),
            pltpu.VMEM((2, width, chunk), BF),
            pltpu.VMEM((2, chunk, width), BF),
            pltpu.VMEM((n,) + part_u, BF),
            pltpu.VMEM((n,) + part_d, BF),
            pltpu.VMEM((2,) + part_u, BF),
            pltpu.VMEM((2,) + part_d, BF),
            pltpu.SemaphoreType.DMA((4, n)),
            pltpu.SemaphoreType.DMA((4, n)),
        ],
        compiler_params=params(60, collective_id=4, has_side_effects=True),
        name="middle",
    )(x, mixt, wo, woo, cot, dyo, gain, wup, upo, wdn, dno)


class Unit:
    def __init__(self, links, n, w, rx, rz, zp, final, far, n_dp, deepest):
        self.links, self.n, self.w = links, n, w
        self.rx, self.rz, self.zp, self.final, self.far = rx, rz, zp, final, far
        self.n_dp, self.stepwise = n_dp, deepest
        d = links.d
        self.core, self.cross = d & 1, (d >> 1) & 1
        self.b0, self.b1 = (d >> 2) & 1, (d >> 3) & 1
        q = n // 16
        self.q = q
        self.xr = links.remote(lambda: self.xr.make_source(), rx, dp_flip=2)
        spot = self.core * 8 + self.cross * 4 + self.b0 * 2 + self.b1
        self.piece = lambda: final(spot * q, q)
        self.home = links.local(zp, self.piece)
        if deepest:
            keep = self.b0 * 2
            give = (1 - self.b0) * 2
            self.z1 = links.remote(lambda: rx.at[rows_at(give * q, 2 * q, 16)], rz[0], dp_flip=4)
            self.z2 = links.remote(
                lambda: rz[0].at[rows_at((1 - self.b1) * q, q, 16)], rz[1], dp_flip=8
            )
            self.g2 = links.remote(zp, self.piece, dp_flip=8)
            both = lambda: final((self.core * 8 + self.cross * 4 + keep) * q, 2 * q)
            self.g1 = links.remote(both, both, dp_flip=4)
        else:
            self.zs, self.gs = [], []
            for r in range(1, 4):
                p0, p1 = self.b0 ^ (r & 1), self.b1 ^ (r >> 1)
                src = lambda p=p0 * 2 + p1: rx.at[rows_at(p * q, q, 16)]
                dst = lambda r=r: rz[0].at[r - 1]
                self.zs.append(links.remote(src, dst, dp_flip=r << 2))
                self.gs.append(links.remote(zp, self.piece, dp_flip=r << 2))
        quad = lambda: final((self.core * 8 + self.cross * 4) * q, 4 * q)
        self.gx = links.remote(quad, quad, dp_flip=2)
        side = lambda: final(self.core * 8 * q, 8 * q)
        self.gc = links.remote(side, side, dp_flip=1)
        if far is not None:
            self.others = [
                links.remote(lambda: far.at[0], lambda r=r: far.at[r], dp_flip=r << 4)
                for r in range(1, n_dp // 16)
            ]

    def start_x(self, source):
        half = self.n // 4
        self.xr.make_source = lambda: now(source).at[rows_at((1 - self.cross) * half, half, 16)]
        self.xr.start()

    def add_x(self, kept):
        half = self.n // 4
        self.xr.wait_recv()
        mine = now(kept)[rows_at(self.cross * half, half, 16)]
        self.rx[...] = (self.rx[...].astype(F32) + mine.astype(F32)).astype(BF)

    def start_z(self, kept):
        self.add_x(kept)
        for copy in [self.z1] if self.stepwise else self.zs:
            copy.start()

    def start_z2(self):
        self.z1.wait_recv()
        mine = self.rx[rows_at(self.b0 * 2 * self.q, 2 * self.q, 16)]
        self.rz[0][...] = (self.rz[0][...].astype(F32) + mine.astype(F32)).astype(BF)
        self.z2.start()

    def start_back(self):
        q = self.q
        if self.stepwise:
            self.z2.wait_recv()
            total = self.rz[0][rows_at(self.b1 * q, q, 16)].astype(F32)
            total = total + self.rz[1][...].astype(F32)
        else:
            for copy in self.zs:
                copy.wait_recv()
            total = self.rx[rows_at((self.b0 * 2 + self.b1) * q, q, 16)].astype(F32)
            for r in range(3):
                total = total + self.rz[0][r].astype(F32)
        if self.far is not None:
            self.far[0] = total.astype(BF)
            for copy in self.others:
                copy.start()
            for r, copy in enumerate(self.others):
                copy.wait_recv()
                total = total + self.far[r + 1].astype(F32)
        self.zp[...] = total.astype(BF)
        self.home.start()
        for copy in [self.g2] if self.stepwise else self.gs:
            copy.start()

    def start_back1(self):
        self.home.wait()
        self.g2.wait_recv()
        self.g1.start()

    def start_back_x(self):
        if self.stepwise:
            self.g1.wait_recv()
        else:
            self.home.wait()
            for copy in self.gs:
                copy.wait_recv()
        self.gx.start()

    def start_back_c(self):
        self.gx.wait_recv()
        self.gc.start()

    def end(self):
        self.gc.wait_recv()
        sent = [self.xr, self.gx, self.gc]
        sent += [self.z1, self.z2, self.g2, self.g1] if self.stepwise else self.zs + self.gs
        if self.far is not None:
            sent += self.others
        for copy in sent:
            copy.wait_send()


def back_kernel(
    p_ref, qt_ref, k_ref, v_ref, ot_ref, dot_ref, r_ref, back_ref, hot_ref,
    x_ref, gain_ref, dh_ref, ggf_ref, wq_ref, wk_ref, wv_ref,
    sum1u, sum1d, sum2u, sum2d, own3u, own3d, far3u, far3d, gwo, y,
    yret, gret, fqkv, fwo, fup, fdn, small,
    vx, dox, kht, n1t, dn, gtab, gp, rcp, ryp, gin,
    k1u, k1d, k2u, k2d, k3u, k3d, ry3u, ry3d, kw, rcw, ryw,
    sums, got, *rest, n_dp, buckets,
):
    units_scratch, rest = rest[: 4 * 10], rest[4 * 10 :]
    far = rest[:10] if n_dp > 16 else [None] * 10
    send, recv = rest[-2:]
    links = Links(send, recv)
    d, m = links.d, links.m
    core = d & 1
    step = pl.program_id(0)
    tokens, width = x_ref.shape
    rows = tokens // 2
    chunk = far3u.shape[1]
    group = gp.shape[2]
    bits = n_dp.bit_length() - 1

    def region(ref, row0, col0, w, lead=None):
        def at(start, count):
            where = rows_at(row0 + start, count, 16)
            if lead is not None:
                return ref.at[lead, where]
            return ref.at[where, col0 : col0 + w]

        return at

    finals = []
    for k in range(3):
        finals.append((width, chunk, region(fup, 0, k * chunk, chunk), True))
        finals.append((chunk, width, region(fdn, k * chunk, 0, width), True))
    finals.append((width, group, region(fwo, 0, 0, group), False))
    for k in range(3):
        finals.append((width, group, region(fqkv, 0, 0, group, lead=k), False))
    units = []
    for i, (n, w, final, deepest) in enumerate(finals):
        rx, zp = units_scratch[4 * i], units_scratch[4 * i + 1]
        rz = units_scratch[4 * i + 2 : 4 * i + 4]
        units.append(Unit(links, n, w, rx, rz, zp, final, far[i], n_dp, deepest))
    ff = (units[0:2], units[2:4], units[4:6])
    wo, pairs = units[6], units[7:10]
    kept = ((k1u, k1d), (k2u, k2d), (ry3u, ry3d))
    heads_half = width // 2

    mine = rows_at(m * rows, rows, rows)
    theirs = rows_at((1 - m) * rows, rows, rows)
    y_home = links.local(lambda: y.at[mine], lambda: yret.at[m])
    y_away = links.remote(lambda: y.at[theirs], lambda: yret.at[m], mp_flip=1)
    gin_home = links.local(lambda: gin.at[mine], lambda: gret.at[m])
    gin_away = links.remote(lambda: gin.at[theirs], lambda: gret.at[m], mp_flip=1)
    loads = [
        links.local(src, dst)
        for src, dst in ((sum1u, k1u), (sum1d, k1d), (sum2u, k2u), (sum2d, k2d), (own3u, k3u), (own3d, k3d))
    ]
    keep = rows_at(core * (width // 2), width // 2, 16)
    give = rows_at((1 - core) * (width // 2), width // 2, 16)
    load_w = links.local(lambda: gwo.at[keep], kw)
    y3 = [links.remote(far3u, ry3u, mp_flip=1), links.remote(far3d, ry3d, mp_flip=1)]
    wo_c = links.remote(lambda: gwo.at[give], rcw, dp_flip=1)
    wo_y = links.remote(lambda: rcw.at[:, heads_half:], ryw, mp_flip=1)
    pair_c = [
        links.remote(lambda i=i: gp.at[i, give], lambda i=i: rcp.at[i], dp_flip=1) for i in range(6)
    ]
    pair_y = [
        links.remote(lambda i=i: rcp.at[i], lambda i=i: ryp.at[i], mp_flip=1) for i in range(3)
    ]

    def settle(i):
        pair_c[i].wait_recv()
        rcp[i] = (rcp[i].astype(F32) + gp[i, keep].astype(F32)).astype(BF)

    def send_other(i):
        settle(i)
        pair_y[i].start()

    def join_own(k):
        settle(3 + k)
        pair_y[k].wait_recv()
        ryp[k] = (ryp[k].astype(F32) + rcp[3 + k].astype(F32)).astype(BF)
        pairs[k].start_x(lambda: ryp.at[k])

    def each(group_of, name, *args):
        for unit in group_of:
            getattr(unit, name)(*args)

    def ff_z(k):
        for unit, held in zip(ff[k], kept[k]):
            unit.start_z(held)

    def slot_start():
        links.barrier(
            [(0, 1)]
            + [(1 << b, 0) for b in range(bits)]
            + [(12, 0)]
            + [(r << 4, 0) for r in range(1, n_dp // 16) if r & (r - 1)]
        )
        for copy in loads:
            copy.start()
        load_w.start()
        wo_c.start()
        for copy in y3:
            copy.start()
        for unit, source in zip(ff[0], (sum1u, sum1d)):
            unit.start_x(source)
        for unit, source in zip(ff[1], (sum2u, sum2d)):
            unit.start_x(source)
        y_home.start()

    def slot_end(i):
        pair_c[i].start()
        if i == 0:
            load_w.wait()
            wo_c.wait_recv()
            rcw[...] = (rcw[...].astype(F32) + kw[...].astype(F32)).astype(BF)
            wo_y.start()
            for copy in loads:
                copy.wait()
        if i == 1:
            ff_z(0)
            send_other(0)
        if i == 2:
            each(ff[0], "start_z2")
            ff_z(1)
            send_other(1)
            for unit, copy, held, own in zip(ff[2], y3, kept[2], (k3u, k3d)):
                copy.wait_recv()
                held[...] = (held[...].astype(F32) + own[...].astype(F32)).astype(BF)
                unit.start_x(held)
        if i == 3:
            each(ff[0], "start_back")
            each(ff[1], "start_z2")
            send_other(2)
            y_away.start()
            wo_y.wait_recv()
            ryw[...] = (ryw[...].astype(F32) + rcw[:, 0:heads_half].astype(F32)).astype(BF)
            wo.start_x(ryw)
        if i == 4:
            each(ff[0], "start_back1")
            each(ff[1], "start_back")
            ff_z(2)
            join_own(0)
            wo.start_z(ryw)
        if i == 5:
            each(ff[0], "start_back_x")
            each(ff[1], "start_back1")
            each(ff[2], "start_z2")
            join_own(1)
            wo.start_back()
            pairs[0].start_z(lambda: ryp.at[0])

    @pl.when(step == 0)
    def _():
        slot_start()
        kht[64:160, :] = back_ref[...]
        lanes = lax.broadcasted_iota(jnp.int32, (tokens, 64), 1)
        vx[:, 64:128] = jnp.where(lanes < 2, -1.0, 0.0).astype(BF)
        dox[64:128, :] = jnp.zeros((64, tokens), BF)
        x = x_ref[...].astype(F32)
        inverse = lax.rsqrt(jnp.mean(x * x, axis=-1, keepdims=True) + EPS)
        n1t[...] = (x * inverse * gain_ref[...]).astype(BF).T
        dn[...] = jnp.zeros_like(dn)
        gtab[...] = jnp.zeros_like(gtab)

    side = lax.broadcasted_iota(jnp.int32, (buckets, 128), 1)
    first_row = jnp.where(step < 3, 8 + 2 * step, 2 * (step - 3))
    dqs, dks, dvs = [], [], []
    for h in range(2):
        span = slice(64 * h, 64 * h + 64)
        scaled = dot_ref[span, :].astype(F32) * r_ref[0, h : h + 1, :]
        inner = jnp.sum(scaled * ot_ref[span, :].astype(F32), axis=0, keepdims=True)
        upper = inner.astype(BF)
        lower = (inner - upper.astype(F32)).astype(BF)
        dox[0:64, :] = scaled.astype(BF)
        dox[64:66, :] = jnp.concatenate([upper, lower], 0)
        vx[:, 0:64] = v_ref[:, span]
        kht[0:64, :] = k_ref[:, span].T
        dp = dg(vx[...], dox[...], 1, 0)
        p = p_ref[h]
        ds = (p.astype(F32) * dp).astype(BF)
        dvs.append(dg(p, dox[0:64, :], 1, 1).astype(BF))
        dks.append((dg(ds, qt_ref[span, :], 1, 1) * 0.125).astype(BF))
        both = dg(kht[...], ds, 1, 0)
        dqs.append((both[0:64] * 0.125).astype(BF).T)
        left = both[64:160]
        left_hi = left.astype(BF)
        left_lo = (left - left_hi.astype(F32)).astype(BF)
        hot = hot_ref[...]
        blocks = dg(left_hi, hot, 1, 0) + dg(left_lo, hot, 1, 0)
        for t in range(3):
            inside = (side >= t * buckets) & (side < (t + 1) * buckets)
            block = jnp.where(inside, blocks[t * buckets : (t + 1) * buckets], 0.0)
            rolled = pltpu.roll(block, (129 - (t + 1) * buckets) % 128, 1, stride=1, stride_axis=0)
            gtab[t, pl.ds(first_row + h, 1), :] = jnp.sum(rolled, axis=0, keepdims=True)
    grads = jnp.concatenate(dqs + dks + dvs, axis=1)
    weights = jnp.concatenate([wq_ref[...], wk_ref[...], wv_ref[...]], axis=1)
    dn[...] += dg(grads, weights, 1, 1)
    gp[step] = dg(n1t[...], grads, 1, 0).astype(BF)
    for i in range(6):
        pl.when(step == i)(functools.partial(slot_end, i))

    @pl.when(step == pl.num_programs(0) - 1)
    def _():
        x = x_ref[...].astype(F32)
        inverse = lax.rsqrt(jnp.mean(x * x, axis=-1, keepdims=True) + EPS)
        normed = x * inverse
        total = dn[...]
        grad_gain = jnp.sum(total * normed, axis=0, keepdims=True)
        inner = total * gain_ref[...]
        added = inverse * (inner - normed * jnp.mean(inner * normed, axis=-1, keepdims=True))
        gin[...] = (dh_ref[...] + added).astype(BF)
        gin_away.start()
        gin_home.start()
        lines = width // 128
        for j in range(lines):
            lane = slice(j * 128, (j + 1) * 128)
            sums[0, j : j + 1, :] = grad_gain[:, lane]
            sums[0, lines + j : lines + j + 1, :] = ggf_ref[:, lane]
        sums[0, 2 * lines : 16, :] = jnp.zeros((16 - 2 * lines, 128), F32)
        line = lax.broadcasted_iota(jnp.int32, (128, 128), 0)
        lane = lax.broadcasted_iota(jnp.int32, (128, 128), 1)
        shift = jnp.where(lane < 64, lane, lane - 128)
        bucket = jnp.clip(-shift, -(buckets // 2), buckets // 2 - 1) + buckets // 2
        table = jnp.zeros((16, 128), F32)
        for t in range(3):
            pick = jnp.where(line == bucket + t * buckets, 1.0, 0.0)
            table = table + lax.dot_general(
                gtab[t], pick, (((1,), (1,)), ((), ())),
                precision=lax.Precision.HIGHEST, preferred_element_type=F32,
            )
        sums[0, 16:32, :] = table
        hops = bits + 1
        hop = None
        count = 0

        def small_hop():
            nonlocal hop, count
            if hop is not None:
                hop.wait_recv()
                k = count
                if k == 1:
                    sums[1, 0:16] = sums[0, 0:16] + got[0, 0:16]
                    sums[1, 16:24] = sums[0, 16:24] + got[0, 24:32]
                    sums[1, 24:32] = jnp.zeros((8, 128), F32)
                else:
                    sums[k] = sums[k - 1] + got[k - 1]
                hop = None
            if count < hops:
                flips = dict(mp_flip=1) if count == 0 else dict(dp_flip=1 << (count - 1))
                k = count
                hop = links.remote(lambda: sums.at[k], lambda: got.at[k], **flips)
                hop.start()
                started.append(hop)
                count += 1

        started = []
        small_hop()
        join_own(2)
        each(ff[0], "start_back_c")
        each(ff[1], "start_back_x")
        each(ff[2], "start_back")
        wo.start_back_x()
        pairs[1].start_z(lambda: ryp.at[1])
        pairs[0].start_back()
        small_hop()
        pairs[2].start_z(lambda: ryp.at[2])
        pairs[0].start_back_x()
        each(ff[1], "start_back_c")
        each(ff[2], "start_back1")
        pairs[1].start_back()
        wo.start_back_c()
        small_hop()
        pairs[2].start_back()
        each(ff[2], "start_back_x")
        pairs[1].start_back_x()
        pairs[0].start_back_c()
        small_hop()
        pairs[2].start_back_x()
        each(ff[2], "start_back_c")
        pairs[1].start_back_c()
        small_hop()
        pairs[2].start_back_c()
        while count < hops or hop is not None:
            small_hop()
        small[...] = sums[hops]
        y_away.wait_recv()
        gin_away.wait_recv()
        for unit in units:
            unit.end()
        for copy in [y_away, gin_away, wo_c, wo_y] + y3 + pair_c + pair_y + started:
            copy.wait_send()
        y_home.wait()
        gin_home.wait()


def backward(p, qt, kv, ot, dot, r, back, hot, x, gain, dh, ggf, wqkv, parts, gwo, y, n_dp, buckets):
    channels, tokens = qt.shape
    width = x.shape[1]
    n_pairs = channels // 128
    half = n_pairs // 2
    chunk = parts[0].shape[1]
    group = 3 * 128
    once = lambda shape: pl.BlockSpec(
        shape, lambda i: (0,) * len(shape), pipeline_mode=pl.Buffered(1)
    )
    pick = lambda i: lax.rem(i + half, n_pairs)
    side = lambda i: pick(i) // half
    place = lambda i: lax.rem(pick(i), half)
    turned = pl.BlockSpec((128, tokens), lambda i: (pick(i), 0))
    column = lambda rows, j, n: pl.BlockSpec(
        (rows, 128), lambda i: (0, side(i) * n * half + j * half + place(i))
    )
    shapes = []
    for k in range(3):
        shapes += [(width, chunk, True), (chunk, width, True)]
    shapes += [(width, group, False)] * 4
    units, far = [], []
    for n, w, deepest in shapes:
        units += [
            pltpu.VMEM((n // 4, w), BF),
            pltpu.VMEM((n // 16, w), BF),
            pltpu.VMEM((n // 8, w) if deepest else (3, n // 16, w), BF),
            pltpu.VMEM((n // 16, w), BF),
        ]
        far.append(pltpu.VMEM((max(n_dp // 16, 1), n // 16, w), BF))
    bits = n_dp.bit_length() - 1
    part_u, part_d = parts[0].shape, parts[1].shape
    copies = 160 + (10 * (n_dp // 16) if n_dp > 16 else 0)
    scratch = [
        pltpu.VMEM((tokens, 128), BF),
        pltpu.VMEM((128, tokens), BF),
        pltpu.VMEM((160, tokens), BF),
        pltpu.VMEM((width, tokens), BF),
        pltpu.VMEM((tokens, width), F32),
        pltpu.VMEM((3, 16, 128), F32),
        pltpu.VMEM((6, width, group), BF),
        pltpu.VMEM((6, width // 2, group), BF),
        pltpu.VMEM((3, width // 2, group), BF),
        pltpu.VMEM((tokens, width), BF),
        pltpu.VMEM(part_u, BF),
        pltpu.VMEM(part_d, BF),
        pltpu.VMEM(part_u, BF),
        pltpu.VMEM(part_d, BF),
        pltpu.VMEM(part_u, BF),
        pltpu.VMEM(part_d, BF),
        pltpu.VMEM(part_u, BF),
        pltpu.VMEM(part_d, BF),
        pltpu.VMEM((width // 2, width), BF),
        pltpu.VMEM((width // 2, width), BF),
        pltpu.VMEM((width // 2, width // 2), BF),
        pltpu.VMEM((bits + 2, 32, 128), F32),
        pltpu.VMEM((bits + 2, 32, 128), F32),
    ]
    scratch += units
    if n_dp > 16:
        scratch += far
    scratch += [pltpu.SemaphoreType.DMA((copies,))] * 2
    return pl.pallas_call(
        functools.partial(back_kernel, n_dp=n_dp, buckets=buckets),
        grid=(n_pairs,),
        in_specs=[
            pl.BlockSpec((2, tokens, tokens), lambda i: (pick(i), 0, 0)),
            turned,
            column(tokens, 0, 2),
            column(tokens, 1, 2),
            turned,
            turned,
            pl.BlockSpec((1, 2, tokens), lambda i: (pick(i), 0, 0)),
            once((96, tokens)),
            once((tokens, 128)),
            once((tokens, width)),
            once((1, width)),
            once((tokens, width)),
            once((1, width)),
            column(width, 0, 3),
            column(width, 1, 3),
            column(width, 2, 3),
        ]
        + [ANY] * 10,
        out_specs=[ANY] * 6 + [once((32, 128))],
        out_shape=[
            SHAPE((2, tokens // 2, width), BF),
            SHAPE((2, tokens // 2, width), BF),
            SHAPE((3, width, group), BF),
            SHAPE((width, group), BF),
            SHAPE((width, 3 * chunk), BF),
            SHAPE((3 * chunk, width), BF),
            SHAPE((32, 128), F32),
        ],
        scratch_shapes=scratch,
        compiler_params=params(60, collective_id=5, has_side_effects=True),
        name="backward",
    )(p, qt, kv, kv, ot, dot, r, back, hot, x, gain, dh, ggf, wqkv, wqkv, wqkv, *parts, gwo, y)


def local(
    n_dp, inputs, roi, cotangent, doc_lengths, live_mask, bucket_cells,
    gain_attn, gain_ffn, w_query, w_key, w_value, w_out, w_up, w_down, tables,
):
    rows, width = inputs.shape[1], inputs.shape[2]
    tokens = 2 * rows
    third = w_query.shape[1]
    heads = third // HDIM
    buckets = tables.shape[1]
    tab = jnp.pad(
        tables.transpose(2, 0, 1).reshape(heads, 3 * buckets), ((0, 2), (0, 128 - 3 * buckets))
    )
    ga, gf = gain_attn.reshape(1, width), gain_ffn.reshape(1, width)
    x, tabo, wqkv, qt, kv, upo = entry(
        inputs, roi, tab, ga, w_query, w_key, w_value, w_up
    )
    p, mixt, r, hot, back, dyo, woo, upo, dno = attend(
        doc_lengths, live_mask.reshape(2, 1, tokens), bucket_cells, tab, tabo, qt, kv,
        cotangent, w_out, w_up, w_down, upo, buckets,
    )
    y, gwo, dh, dmt, gain_f, *parts = middle(
        x, mixt, w_out, woo, cotangent, dyo, gf, w_up, upo, w_down, dno
    )
    yret, gret, fqkv, fwo, fup, fdn, small = backward(
        p, qt, kv, mixt, dmt, r, back, hot, x, ga, dh, gain_f, wqkv, parts, gwo, y, n_dp, buckets
    )
    lines = width // 128
    out = inputs.astype(F32) + roi.astype(F32) + yret.astype(F32)
    grad_in = cotangent.astype(F32) + gret.astype(F32)
    table_out = small[16 : 16 + heads, : 3 * buckets].reshape(heads, 3, buckets).transpose(1, 2, 0)
    gq, gk, gv = (
        jnp.concatenate([fqkv[k, :, j * 128 : (j + 1) * 128] for k in range(3)], axis=1).astype(F32)
        for j in range(3)
    )
    return (
        out,
        grad_in,
        small[0:lines].reshape(width),
        small[lines : 2 * lines].reshape(width),
        gq,
        gk,
        gv,
        fwo.T.astype(F32),
        fup.astype(F32),
        fdn.astype(F32),
        table_out,
    )


def solution(mesh):
    n_dp = mesh.shape["dp"]
    rows = P(None, ("dp", "mp"), None)
    columns, lines = P(None, "mp"), P("mp", None)
    tables = P(None, None, "mp")
    return jax.shard_map(
        functools.partial(local, n_dp),
        mesh=mesh,
        in_specs=(
            rows, rows, rows, P(None, "dp", None), P(None, "dp"), P(None, None, "dp"),
            P(), P(), columns, columns, columns, lines, columns, lines, tables,
        ),
        out_specs=(
            rows, rows, P(), P(), columns, columns, columns, lines, columns, lines, tables,
        ),
        check_vma=False,
    )
```

```python
import functools
import math

import jax
import jax.numpy as jnp
from jax import lax
from jax.experimental import pallas as pl
from jax.experimental.pallas import tpu as pltpu
from jax.sharding import PartitionSpec as P

BF = jnp.bfloat16
F32 = jnp.float32
HDIM = 64
EPS = 1e-06
MASKED = -1e30
MESH = pl.DeviceIdType.MESH
VMEM = pl.BlockSpec(memory_space=pltpu.VMEM)
ANY = pl.BlockSpec(memory_space=pltpu.HBM)
SHAPE = jax.ShapeDtypeStruct


def dg(a, b, ca, cb):
    return lax.dot_general(a, b, (((ca,), (cb,)), ((), ())), preferred_element_type=F32)


def params(limit=58, **more):
    return pltpu.CompilerParams(vmem_limit_bytes=limit << 20, **more)


class Copy:
    def __init__(self, make):
        self.make = make

    def start(self):
        self.make().start()

    def wait(self):
        self.make().wait()

    def wait_recv(self):
        self.make().wait_recv()

    def wait_send(self):
        self.make().wait_send()


def now(ref):
    return ref() if callable(ref) else ref


class Links:
    def __init__(self, send, recv):
        self.send, self.recv, self.count = send, recv, 0
        self.d, self.m = lax.axis_index("dp"), lax.axis_index("mp")

    def flipped(self, dp_flip, mp_flip):
        dp = self.d ^ dp_flip if dp_flip else self.d
        mp = self.m ^ mp_flip if mp_flip else self.m
        return dp, mp

    def remote(self, src, dst, dp_flip=0, mp_flip=0):
        i = self.count
        self.count += 1
        return Copy(
            lambda: pltpu.make_async_remote_copy(
                src_ref=now(src),
                dst_ref=now(dst),
                send_sem=self.send.at[i],
                recv_sem=self.recv.at[i],
                device_id=self.flipped(dp_flip, mp_flip),
                device_id_type=MESH,
            )
        )

    def local(self, src, dst):
        i = self.count
        self.count += 1
        return Copy(lambda: pltpu.make_async_copy(now(src), now(dst), self.send.at[i]))

    def barrier(self, flips):
        sem = pltpu.get_barrier_semaphore()
        for flip in flips:
            pl.semaphore_signal(
                sem, inc=1, device_id=self.flipped(*flip), device_id_type=MESH
            )
        pl.semaphore_wait(sem, len(flips))


def rows_at(start, size, unit):
    return pl.ds(pl.multiple_of(start, unit), size)


def entry_kernel(
    inp, roi, tab, gain, wq, wk, wv, wup,
    xf, tabo, wqkv, qt, kv, upo,
    sent, n1, send, recv,
):
    links = Links(send, recv)
    d, m = links.d, links.m
    rows = inp.shape[1]
    width, third = wq.shape
    piece = width // 8
    core, cross, deep = d & 1, (d >> 1) & 1, (d >> 2) & 1
    place = core * 4 + cross * 2 + deep
    links.barrier(((0, 1), (1, 0), (2, 0), (4, 0)))
    started = []

    def go(copy):
        copy.start()
        started.append(copy)
        return copy

    own_cols = [slice(j * third, (j + 1) * third) for j in range(3)]
    other_cols = [slice((3 + j) * third, (4 + j) * third) for j in range(3)]
    spot = rows_at(place * piece, piece, piece)
    first = [
        go(links.remote(w.at[spot], wqkv.at[spot, c], mp_flip=1))
        for w, c in zip((wq, wk, wv), other_cols)
    ]
    tab_copy = go(links.remote(tab, tabo, mp_flip=1))
    chunk = rows // 2
    row_copies = []
    for j in range(2):
        part = slice(j * chunk, (j + 1) * chunk)
        sent[part] = (inp[1 - m, part].astype(F32) + roi[1 - m, part].astype(F32)).astype(BF)
        here = rows_at(m * rows + j * chunk, chunk, chunk)
        row_copies.append(go(links.remote(sent.at[part], xf.at[here], mp_flip=1)))
    up_copy = go(links.remote(wup.at[spot], upo.at[spot], mp_flip=1))
    for w, c in zip((wq, wk, wv), own_cols):
        wqkv[:, c] = w[...]

    def normalise(where):
        x = xf[where].astype(F32)
        inverse = lax.rsqrt(jnp.mean(x * x, axis=-1, keepdims=True) + EPS)
        n1[where] = (x * inverse * gain[...]).astype(BF)

    own = rows_at(m * rows, rows, rows)
    xf[own] = (inp[m].astype(F32) + roi[m].astype(F32)).astype(BF)
    normalise(own)

    def project(where, side):
        rows_in = n1[where]
        base = side * 3 * third
        kv[where, side * 2 * third : (side + 1) * 2 * third] = dg(
            rows_in, wqkv[:, base + third : base + 3 * third], 1, 0
        ).astype(BF)
        qt[side * third : (side + 1) * third, where] = dg(
            wqkv[:, base : base + third], rows_in, 0, 1
        ).astype(BF)

    project(own, 0)
    stage = first
    for flip, begin, count in (
        (4, place, 1),
        (2, core * 4 + cross * 2, 2),
        (1, core * 4, 4),
    ):
        for copy in stage:
            copy.wait_recv()
        there = wqkv.at[rows_at(begin * piece, count * piece, piece), 3 * third : 6 * third]
        stage = [go(links.remote(there, there, dp_flip=flip))]
    for j in range(2):
        row_copies[j].wait_recv()
        here = rows_at((1 - m) * rows + j * chunk, chunk, chunk)
        normalise(here)
        project(here, 0)
    for copy in stage:
        copy.wait_recv()
    for j in range(2):
        project(slice(j * rows, (j + 1) * rows), 1)
    tab_copy.wait_recv()
    up_copy.wait_recv()
    for copy in started:
        copy.wait_send()


def entry(inputs, roi, tab, gain, wq, wk, wv, wup):
    rows, width = inputs.shape[1], inputs.shape[2]
    third = wq.shape[1]
    tokens = 2 * rows
    return pl.pallas_call(
        entry_kernel,
        out_shape=[
            SHAPE((tokens, width), BF),
            SHAPE(tab.shape, F32),
            SHAPE((width, 6 * third), BF),
            SHAPE((2 * third, tokens), BF),
            SHAPE((tokens, 4 * third), BF),
            SHAPE(wup.shape, BF),
        ],
        in_specs=[VMEM] * 7 + [ANY],
        out_specs=[VMEM] * 5 + [ANY],
        scratch_shapes=[
            pltpu.VMEM((rows, width), BF),
            pltpu.VMEM((tokens, width), BF),
            pltpu.SemaphoreType.DMA((12,)),
            pltpu.SemaphoreType.DMA((12,)),
        ],
        compiler_params=params(58, collective_id=1, has_side_effects=True),
        name="entry",
    )(inputs, roi, tab, gain, wq, wk, wv, wup)


def attend_kernel(
    lengths, live, cells, tab, tabo, qt_ref, k_ref, v_ref, cot, wo, wup, wdn, upo_in,
    p_ref, o_ref, r_ref, hot_ref, back_ref, dyo, woo, upo, dno,
    kx, qx, vx, mask, mats, hott_ref, send, recv, *, buckets,
):
    links = Links(send, recv)
    d, m = links.d, links.m
    tokens = k_ref.shape[0]
    rows = tokens // 2
    width, hidden = wup.shape
    inner = wo.shape[0]
    step = pl.program_id(0)
    core, cross, deep = d & 1, (d >> 1) & 1, (d >> 2) & 1
    place = core * 4 + cross * 2 + deep

    def block(full, begin, count):
        piece = full.shape[0] // 8
        return full.at[rows_at(begin * piece, count * piece, piece)]

    up = functools.partial(block, upo)
    down = functools.partial(block, dno)
    out = functools.partial(block, woo)
    dpiece, opiece = hidden // 8, inner // 8
    quarter = core * 4 + deep * 2
    down_y = links.remote(
        wdn.at[rows_at(quarter * dpiece, 2 * dpiece, dpiece)], down(quarter, 2), mp_flip=1
    )
    out_y = links.remote(wo.at[rows_at(place * opiece, opiece, opiece)], out(place, 1), mp_flip=1)
    dy_y = links.remote(cot.at[1 - m], dyo, mp_flip=1)
    up_z = links.remote(up(place, 1), up(place, 1), dp_flip=4)
    pair = core * 4 + cross * 2
    up_x = links.remote(up(pair, 2), up(pair, 2), dp_flip=2)
    up_c = links.remote(up(core * 4, 4), up(core * 4, 4), dp_flip=1)
    down_z = links.remote(down(quarter, 2), down(quarter, 2), dp_flip=4)
    down_c = links.remote(down(core * 4, 4), down(core * 4, 4), dp_flip=1)
    out_z = links.remote(out(place, 1), out(place, 1), dp_flip=4)
    out_x = links.remote(out(pair, 2), out(pair, 2), dp_flip=2)
    out_c = links.remote(out(core * 4, 4), out(core * 4, 4), dp_flip=1)

    def slot0():
        links.barrier(((0, 1), (1, 0), (2, 0), (4, 0)))
        up_z.start()
        down_y.start()
        out_y.start()
        dy_y.start()

    def slot4():
        up_z.wait_recv()
        up_x.start()

    def slot6():
        out_y.wait_recv()
        out_z.start()

    def slot7():
        down_y.wait_recv()
        down_z.start()

    def slot9():
        out_z.wait_recv()
        out_x.start()

    def slot11():
        up_x.wait_recv()
        up_c.start()
        out_x.wait_recv()
        out_c.start()

    def last():
        down_z.wait_recv()
        down_c.start()
        for copy in (dy_y, up_c, out_c, down_c):
            copy.wait_recv()
        for copy in (down_y, out_y, dy_y, up_z, up_x, up_c, down_z, down_c, out_z, out_x, out_c):
            copy.wait_send()

    slots = {0: slot0, 4: slot4, 6: slot6, 7: slot7, 9: slot9, 11: slot11}

    @pl.when(step == 0)
    def _():
        slot0()
        vx[64:80, :] = jnp.ones((16, tokens), BF)
        lane = lax.broadcasted_iota(jnp.int32, (buckets, tokens), 0)
        for t in range(3):
            row = cells[m, t : t + 1, :]
            hott_ref[t * buckets : (t + 1) * buckets, :] = jnp.where(row == lane, 1.0, 0.0).astype(BF)
            mirror = jnp.where(row == buckets - 1 - lane, 1.0, 0.0).astype(BF)
            back_ref[t * buckets : (t + 1) * buckets, :] = mirror
        hott_ref[96:128, :] = jnp.zeros((32, tokens), BF)
        wide_hot = hott_ref[...].T
        hot_ref[...] = wide_hot
        hot = wide_hot[:, 0:96]
        kx[:, 64:160] = hot
        kx[:, 160:256] = hot
        row_ids = lax.broadcasted_iota(jnp.int32, (1, tokens), 1)
        col_ids = lax.broadcasted_iota(jnp.int32, (tokens, 1), 0)
        seg_row = jnp.zeros((1, tokens), jnp.int32)
        seg_col = jnp.zeros((tokens, 1), jnp.int32)
        end = 0
        for i in range(lengths.shape[2]):
            end = end + lengths[m, 0, i]
            seg_row = seg_row + jnp.where(row_ids >= end, 1, 0)
            seg_col = seg_col + jnp.where(col_ids >= end, 1, 0)
        live_row = live[m].astype(F32)
        live_col = jnp.broadcast_to(live_row, (8, tokens)).T[:, 0:1]
        code = jnp.where(live_col == 1.0, seg_col, -1)
        allowed = (code == seg_row) | (col_ids == row_ids)
        mask[...] = jnp.where(allowed, 0.0, MASKED)
        line = lax.broadcasted_iota(jnp.int32, (128, 128), 0)
        lane = lax.broadcasted_iota(jnp.int32, (128, 128), 1)
        shift = jnp.where(lane < 64, lane, lane - 128)
        bucket = jnp.clip(-shift, -(buckets // 2), buckets // 2 - 1) + buckets // 2
        side = lax.broadcasted_iota(jnp.int32, (buckets, 128), 1)
        heads = mats.shape[0] // 2
        for part, table in enumerate((tab, tabo)):
            exact = table[...]
            upper = exact.astype(BF)
            lower = (exact - upper.astype(F32)).astype(BF)
            for t in range(3):
                pick = jnp.where(line == bucket + t * buckets, 1.0, 0.0).astype(BF)
                inside = (side >= t * buckets) & (side < (t + 1) * buckets)
                for level, source in enumerate((upper, lower)):
                    lines = dg(source, pick, 1, 0)
                    for h in range(heads):
                        wide = jnp.broadcast_to(lines[h : h + 1], (buckets, 128))
                        rolled = pltpu.roll(wide, t * buckets, 1, stride=1, stride_axis=0)
                        begin = level * 3 * buckets + t * buckets
                        mats[part * heads + h, begin : begin + buckets, :] = jnp.where(
                            inside, rolled, 0.0
                        ).astype(BF)

    vt = v_ref[...].T
    for h in range(2):
        for at, action in slots.items():
            if at % 2 == h and at > 0:
                pl.when(step == at // 2)(action)
        span = slice(64 * h, 64 * h + 64)
        kx[:, 0:64] = k_ref[:, span]
        qx[0:64, :] = qt_ref[span, :] * BF(0.125)
        qx[64:256, :] = dg(mats[2 * step + h], hott_ref[...], 1, 0).astype(BF)
        vx[0:64, :] = vt[span, :]
        s = dg(kx[...], qx[...], 1, 0) + mask[...]
        top = jnp.max(s, axis=0, keepdims=True)
        p = jnp.exp(s - top).astype(BF)
        p_ref[h] = p
        o = dg(vx[...], p, 1, 0)
        r = 1.0 / o[64:65, :]
        o_ref[span, :] = (o[0:64] * r).astype(BF)
        r_ref[0, h : h + 1, :] = r
    pl.when(step == pl.num_programs(0) - 1)(last)


def attend(lengths, live, cells, tab, tabo, qt, kv, cot, wo, wup, wdn, upo, buckets):
    channels, tokens = qt.shape
    width, hidden = wup.shape
    inner = wo.shape[0]
    pairs = channels // 128
    half = pairs // 2
    whole = lambda shape: pl.BlockSpec(shape, lambda i: (0,) * len(shape))
    return pl.pallas_call(
        functools.partial(attend_kernel, buckets=buckets),
        grid=(pairs,),
        in_specs=[
            pl.BlockSpec(memory_space=pltpu.SMEM),
            whole(live.shape),
            whole(cells.shape),
            whole(tab.shape),
            whole(tabo.shape),
            pl.BlockSpec((128, tokens), lambda i: (i, 0)),
            pl.BlockSpec((tokens, 128), lambda i: (0, (i // half) * 2 * half + i % half)),
            pl.BlockSpec((tokens, 128), lambda i: (0, (i // half) * 2 * half + half + i % half)),
            ANY, ANY, ANY, ANY, ANY,
        ],
        out_specs=[
            pl.BlockSpec((2, tokens, tokens), lambda i: (i, 0, 0)),
            pl.BlockSpec((128, tokens), lambda i: (i, 0)),
            pl.BlockSpec((1, 2, tokens), lambda i: (i, 0, 0)),
            whole((tokens, 128)),
            whole((96, tokens)),
            ANY, ANY, ANY, ANY,
        ],
        out_shape=[
            SHAPE((2 * pairs, tokens, tokens), BF),
            SHAPE((channels, tokens), BF),
            SHAPE((pairs, 2, tokens), F32),
            SHAPE((tokens, 128), BF),
            SHAPE((96, tokens), BF),
            SHAPE((tokens // 2, width), BF),
            SHAPE((inner, width), BF),
            SHAPE((width, hidden), BF),
            SHAPE((hidden, width), BF),
        ],
        input_output_aliases={12: 7},
        scratch_shapes=[
            pltpu.VMEM((tokens, 256), BF),
            pltpu.VMEM((256, tokens), BF),
            pltpu.VMEM((80, tokens), BF),
            pltpu.VMEM((tokens, tokens), F32),
            pltpu.VMEM((2 * pairs, 192, 128), BF),
            pltpu.VMEM((128, tokens), BF),
            pltpu.SemaphoreType.DMA((20,)),
            pltpu.SemaphoreType.DMA((20,)),
        ],
        compiler_params=params(58, collective_id=3, has_side_effects=True),
        name="attend",
    )(lengths, live, cells, tab, tabo, qt, kv, kv, cot, wo, wup, wdn, upo)


def middle_kernel(
    x_ref, mixt_ref, wo_in, woo_in, cot, dyo, gain_ref, wup_in, upo_in, wdn_in, dno_in,
    y_ref, gwo_ref, dh_ref, dmt_ref, gg_ref,
    sum1u, sum1d, sum2u, sum2d, own3u, own3d, far3u, far3d,
    h1, n2, n2t, yacc, dn, wo_ref, dy_ref, gu, gd, rcu, rcd, ryu, ryd, send, recv,
):
    links = Links(send, recv)
    core = links.d & 1
    step = pl.program_id(0)
    last = pl.num_programs(0) - 1
    half_steps = pl.num_programs(0) // 2
    early = step < half_steps
    width, chunk = gu.shape[1:]
    keep_u, give_u = (rows_at(c * (width // 2), width // 2, 16) for c in (core, 1 - core))
    keep_d, give_d = (rows_at(c * (chunk // 2), chunk // 2, 16) for c in (core, 1 - core))

    def core_copies(i):
        return (
            pltpu.make_async_remote_copy(
                gu.at[i % 2, give_u], rcu.at[i], send.at[0, i], recv.at[0, i],
                device_id=(links.d ^ 1, links.m), device_id_type=MESH,
            ),
            pltpu.make_async_remote_copy(
                gd.at[i % 2, give_d], rcd.at[i], send.at[1, i], recv.at[1, i],
                device_id=(links.d ^ 1, links.m), device_id_type=MESH,
            ),
        )

    def pair_copies(i):
        return (
            pltpu.make_async_remote_copy(
                rcu.at[i], ryu.at[i], send.at[2, i], recv.at[2, i],
                device_id=(links.d, 1 - links.m), device_id_type=MESH,
            ),
            pltpu.make_async_remote_copy(
                rcd.at[i], ryd.at[i], send.at[3, i], recv.at[3, i],
                device_id=(links.d, 1 - links.m), device_id_type=MESH,
            ),
        )

    def settle(i):
        for copy in core_copies(i):
            copy.wait_recv()
        for copy in core_copies(i):
            copy.wait_send()
        rcu[i] = (rcu[i].astype(F32) + gu[i % 2, keep_u].astype(F32)).astype(BF)
        rcd[i] = (rcd[i].astype(F32) + gd[i % 2, keep_d].astype(F32)).astype(BF)

    @pl.when(step == 0)
    def _():
        links.barrier(((0, 1), (1, 0)))
        m = links.m
        rows = dyo.shape[0]
        dy_ref[rows_at(m * rows, rows, rows)] = cot[m]
        dy_ref[rows_at((1 - m) * rows, rows, rows)] = dyo[...]
        inner = wo_in.shape[0]
        wo_ref[0:inner] = wo_in[...]
        wo_ref[inner:] = woo_in[...]
        added = dg(mixt_ref[...], wo_ref[...], 0, 0)
        h = x_ref[...].astype(F32) + added
        h1[...] = h
        yacc[...] = added
        inverse = lax.rsqrt(jnp.mean(h * h, axis=-1, keepdims=True) + EPS)
        normed = (h * inverse * gain_ref[...]).astype(BF)
        n2[...] = normed
        n2t[...] = normed.T
        dn[...] = jnp.zeros_like(dn)

    wup = jnp.where(early, upo_in[...], wup_in[...])
    wdn = jnp.where(early, dno_in[...], wdn_in[...])
    dy = dy_ref[...]
    u = dg(n2[...], wup, 1, 0)
    cdf = 0.5 * (1.0 + lax.erf(u * 0.7071067811865476))
    act = (u * cdf).astype(BF)
    grad_act = dg(dy, wdn, 1, 1)
    density = jnp.exp(u * u * (-0.5)) * 0.3989422804014327
    du = (grad_act * (cdf + u * density)).astype(BF)
    yacc[...] += dg(act, wdn, 1, 0)

    @pl.when(step > 0)
    def _():
        settle(step - 1)

    @pl.when((step > 0) & (step < half_steps))
    def _():
        for copy in pair_copies(step - 1):
            copy.start()

    dn[...] += dg(du, wup, 1, 1)
    gu[step % 2] = dg(n2t[...], du, 1, 0).astype(BF)
    gd[step % 2] = dg(act, dy, 0, 0).astype(BF)
    for copy in core_copies(step):
        copy.start()

    @pl.when(step == last)
    def _():
        h = h1[...]
        inverse = lax.rsqrt(jnp.mean(h * h, axis=-1, keepdims=True) + EPS)
        normed = h * inverse
        grad = dn[...]
        gg_ref[...] = jnp.sum(grad * normed, axis=0, keepdims=True)
        inner = grad * gain_ref[...]
        added = inverse * (inner - normed * jnp.mean(inner * normed, axis=-1, keepdims=True))
        dh_ref[...] = added
        y_ref[...] = yacc[...].astype(BF)
        low = (dy_ref[...].astype(F32) + added).astype(BF)
        gwo_ref[...] = dg(low, mixt_ref[...], 0, 1).astype(BF)
        dmt_ref[...] = dg(wo_ref[...], low, 1, 1).astype(BF)
        settle(last)
        n = rcu.shape[0] // 2
        for k, (out_u, out_d) in enumerate(((sum1u, sum1d), (sum2u, sum2d))):
            for copy in pair_copies(k):
                copy.wait_recv()
            out_u[...] = (rcu[n + k].astype(F32) + ryu[k].astype(F32)).astype(BF)
            out_d[...] = (rcd[n + k].astype(F32) + ryd[k].astype(F32)).astype(BF)
        own3u[...] = rcu[n + 2]
        own3d[...] = rcd[n + 2]
        far3u[...] = rcu[2]
        far3d[...] = rcd[2]
        for k in range(2):
            for copy in pair_copies(k):
                copy.wait_send()


def middle(x, mixt, wo, woo, cot, dyo, gain, wup, upo, wdn, dno):
    tokens, width = x.shape
    half = wup.shape[1]
    chunk = half // 3
    n = 6
    once = lambda shape: pl.BlockSpec(
        shape, lambda i: (0,) * len(shape), pipeline_mode=pl.Buffered(1)
    )
    late = lambda i: jnp.maximum(i - n // 2, 0)
    early = lambda i: jnp.minimum(i, n // 2 - 1)
    part_u, part_d = (width // 2, chunk), (chunk // 2, width)
    outs = [
        ((tokens, width), BF),
        ((width, width), BF),
        ((tokens, width), F32),
        ((width, tokens), BF),
        ((1, width), F32),
    ] + [(part_u, BF), (part_d, BF)] * 4
    return pl.pallas_call(
        middle_kernel,
        grid=(n,),
        in_specs=[
            once((tokens, width)),
            once((width, tokens)),
            once(wo.shape),
            once(woo.shape),
            once(cot.shape),
            once(dyo.shape),
            once((1, width)),
            pl.BlockSpec((width, chunk), lambda i: (0, late(i))),
            pl.BlockSpec((width, chunk), lambda i: (0, early(i))),
            pl.BlockSpec((chunk, width), lambda i: (late(i), 0)),
            pl.BlockSpec((chunk, width), lambda i: (early(i), 0)),
        ],
        out_specs=[once(shape) for shape, _ in outs],
        out_shape=[SHAPE(*entry) for entry in outs],
        scratch_shapes=[
            pltpu.VMEM((tokens, width), F32),
            pltpu.VMEM((tokens, width), BF),
            pltpu.VMEM((width, tokens), BF),
            pltpu.VMEM((tokens, width), F32),
            pltpu.VMEM((tokens, width), F32),
            pltpu.VMEM((width, width), BF),
            pltpu.VMEM((tokens, width), BF),
            pltpu.VMEM((2, width, chunk), BF),
            pltpu.VMEM((2, chunk, width), BF),
            pltpu.VMEM((n,) + part_u, BF),
            pltpu.VMEM((n,) + part_d, BF),
            pltpu.VMEM((2,) + part_u, BF),
            pltpu.VMEM((2,) + part_d, BF),
            pltpu.SemaphoreType.DMA((4, n)),
            pltpu.SemaphoreType.DMA((4, n)),
        ],
        compiler_params=params(60, collective_id=4, has_side_effects=True),
        name="middle",
    )(x, mixt, wo, woo, cot, dyo, gain, wup, upo, wdn, dno)


class Unit:
    def __init__(self, links, n, w, rx, rz, zp, final, far, n_dp, deepest):
        self.links, self.n, self.w = links, n, w
        self.rx, self.rz, self.zp, self.final, self.far = rx, rz, zp, final, far
        self.n_dp, self.stepwise = n_dp, deepest
        d = links.d
        self.core, self.cross = d & 1, (d >> 1) & 1
        self.b0, self.b1 = (d >> 2) & 1, (d >> 3) & 1
        q = n // 16
        self.q = q
        self.xr = links.remote(lambda: self.xr.make_source(), rx, dp_flip=2)
        spot = self.core * 8 + self.cross * 4 + self.b0 * 2 + self.b1
        self.piece = lambda: final(spot * q, q)
        self.home = links.local(zp, self.piece)
        if deepest:
            keep = self.b0 * 2
            give = (1 - self.b0) * 2
            self.z1 = links.remote(lambda: rx.at[rows_at(give * q, 2 * q, 16)], rz[0], dp_flip=4)
            self.z2 = links.remote(
                lambda: rz[0].at[rows_at((1 - self.b1) * q, q, 16)], rz[1], dp_flip=8
            )
            self.g2 = links.remote(zp, self.piece, dp_flip=8)
            both = lambda: final((self.core * 8 + self.cross * 4 + keep) * q, 2 * q)
            self.g1 = links.remote(both, both, dp_flip=4)
        else:
            self.zs, self.gs = [], []
            for r in range(1, 4):
                p0, p1 = self.b0 ^ (r & 1), self.b1 ^ (r >> 1)
                src = lambda p=p0 * 2 + p1: rx.at[rows_at(p * q, q, 16)]
                dst = lambda r=r: rz[0].at[r - 1]
                self.zs.append(links.remote(src, dst, dp_flip=r << 2))
                self.gs.append(links.remote(zp, self.piece, dp_flip=r << 2))
        quad = lambda: final((self.core * 8 + self.cross * 4) * q, 4 * q)
        self.gx = links.remote(quad, quad, dp_flip=2)
        side = lambda: final(self.core * 8 * q, 8 * q)
        self.gc = links.remote(side, side, dp_flip=1)
        if far is not None:
            self.others = [
                links.remote(lambda: far.at[0], lambda r=r: far.at[r], dp_flip=r << 4)
                for r in range(1, n_dp // 16)
            ]

    def start_x(self, source):
        half = self.n // 4
        self.xr.make_source = lambda: now(source).at[rows_at((1 - self.cross) * half, half, 16)]
        self.xr.start()

    def add_x(self, kept):
        half = self.n // 4
        self.xr.wait_recv()
        mine = now(kept)[rows_at(self.cross * half, half, 16)]
        self.rx[...] = (self.rx[...].astype(F32) + mine.astype(F32)).astype(BF)

    def start_z(self, kept):
        self.add_x(kept)
        for copy in [self.z1] if self.stepwise else self.zs:
            copy.start()

    def start_z2(self):
        self.z1.wait_recv()
        mine = self.rx[rows_at(self.b0 * 2 * self.q, 2 * self.q, 16)]
        self.rz[0][...] = (self.rz[0][...].astype(F32) + mine.astype(F32)).astype(BF)
        self.z2.start()

    def start_back(self):
        q = self.q
        if self.stepwise:
            self.z2.wait_recv()
            total = self.rz[0][rows_at(self.b1 * q, q, 16)].astype(F32)
            total = total + self.rz[1][...].astype(F32)
        else:
            for copy in self.zs:
                copy.wait_recv()
            total = self.rx[rows_at((self.b0 * 2 + self.b1) * q, q, 16)].astype(F32)
            for r in range(3):
                total = total + self.rz[0][r].astype(F32)
        if self.far is not None:
            self.far[0] = total.astype(BF)
            for copy in self.others:
                copy.start()
            for r, copy in enumerate(self.others):
                copy.wait_recv()
                total = total + self.far[r + 1].astype(F32)
        self.zp[...] = total.astype(BF)
        self.home.start()
        for copy in [self.g2] if self.stepwise else self.gs:
            copy.start()

    def start_back1(self):
        self.home.wait()
        self.g2.wait_recv()
        self.g1.start()

    def start_back_x(self):
        if self.stepwise:
            self.g1.wait_recv()
        else:
            self.home.wait()
            for copy in self.gs:
                copy.wait_recv()
        self.gx.start()

    def start_back_c(self):
        self.gx.wait_recv()
        self.gc.start()

    def end(self):
        self.gc.wait_recv()
        sent = [self.xr, self.gx, self.gc]
        sent += [self.z1, self.z2, self.g2, self.g1] if self.stepwise else self.zs + self.gs
        if self.far is not None:
            sent += self.others
        for copy in sent:
            copy.wait_send()


def back_kernel(
    p_ref, qt_ref, k_ref, v_ref, ot_ref, dot_ref, r_ref, back_ref, hot_ref,
    x_ref, gain_ref, dh_ref, ggf_ref, wq_ref, wk_ref, wv_ref,
    sum1u, sum1d, sum2u, sum2d, own3u, own3d, far3u, far3d, gwo, y,
    yret, gret, fqkv, fwo, fup, fdn, small,
    vx, dox, kht, n1t, dn, gtab, gp, rcp, ryp, gin,
    k1u, k1d, k2u, k2d, k3u, k3d, ry3u, ry3d, kw, rcw, ryw,
    sums, got, *rest, n_dp, buckets,
):
    units_scratch, rest = rest[: 4 * 10], rest[4 * 10 :]
    far = rest[:10] if n_dp > 16 else [None] * 10
    send, recv = rest[-2:]
    links = Links(send, recv)
    d, m = links.d, links.m
    core = d & 1
    step = pl.program_id(0)
    tokens, width = x_ref.shape
    rows = tokens // 2
    chunk = far3u.shape[1]
    group = gp.shape[2]
    bits = n_dp.bit_length() - 1

    def region(ref, row0, col0, w, lead=None):
        def at(start, count):
            where = rows_at(row0 + start, count, 16)
            if lead is not None:
                return ref.at[lead, where]
            return ref.at[where, col0 : col0 + w]

        return at

    finals = []
    for k in range(3):
        finals.append((width, chunk, region(fup, 0, k * chunk, chunk), True))
        finals.append((chunk, width, region(fdn, k * chunk, 0, width), True))
    finals.append((width, group, region(fwo, 0, 0, group), False))
    for k in range(3):
        finals.append((width, group, region(fqkv, 0, 0, group, lead=k), False))
    units = []
    for i, (n, w, final, deepest) in enumerate(finals):
        rx, zp = units_scratch[4 * i], units_scratch[4 * i + 1]
        rz = units_scratch[4 * i + 2 : 4 * i + 4]
        units.append(Unit(links, n, w, rx, rz, zp, final, far[i], n_dp, deepest))
    ff = (units[0:2], units[2:4], units[4:6])
    wo, pairs = units[6], units[7:10]
    kept = ((k1u, k1d), (k2u, k2d), (ry3u, ry3d))
    heads_half = width // 2

    mine = rows_at(m * rows, rows, rows)
    theirs = rows_at((1 - m) * rows, rows, rows)
    y_home = links.local(lambda: y.at[mine], lambda: yret.at[m])
    y_away = links.remote(lambda: y.at[theirs], lambda: yret.at[m], mp_flip=1)
    gin_home = links.local(lambda: gin.at[mine], lambda: gret.at[m])
    gin_away = links.remote(lambda: gin.at[theirs], lambda: gret.at[m], mp_flip=1)
    loads = [
        links.local(src, dst)
        for src, dst in ((sum1u, k1u), (sum1d, k1d), (sum2u, k2u), (sum2d, k2d), (own3u, k3u), (own3d, k3d))
    ]
    keep = rows_at(core * (width // 2), width // 2, 16)
    give = rows_at((1 - core) * (width // 2), width // 2, 16)
    load_w = links.local(lambda: gwo.at[keep], kw)
    y3 = [links.remote(far3u, ry3u, mp_flip=1), links.remote(far3d, ry3d, mp_flip=1)]
    wo_c = links.remote(lambda: gwo.at[give], rcw, dp_flip=1)
    wo_y = links.remote(lambda: rcw.at[:, heads_half:], ryw, mp_flip=1)
    pair_c = [
        links.remote(lambda i=i: gp.at[i, give], lambda i=i: rcp.at[i], dp_flip=1) for i in range(6)
    ]
    pair_y = [
        links.remote(lambda i=i: rcp.at[i], lambda i=i: ryp.at[i], mp_flip=1) for i in range(3)
    ]

    def settle(i):
        pair_c[i].wait_recv()
        rcp[i] = (rcp[i].astype(F32) + gp[i, keep].astype(F32)).astype(BF)

    def send_other(i):
        settle(i)
        pair_y[i].start()

    def join_own(k):
        settle(3 + k)
        pair_y[k].wait_recv()
        ryp[k] = (ryp[k].astype(F32) + rcp[3 + k].astype(F32)).astype(BF)
        pairs[k].start_x(lambda: ryp.at[k])

    def each(group_of, name, *args):
        for unit in group_of:
            getattr(unit, name)(*args)

    def ff_z(k):
        for unit, held in zip(ff[k], kept[k]):
            unit.start_z(held)

    def slot_start():
        links.barrier(
            [(0, 1)]
            + [(1 << b, 0) for b in range(bits)]
            + [(12, 0)]
            + [(r << 4, 0) for r in range(1, n_dp // 16) if r & (r - 1)]
        )
        for copy in loads:
            copy.start()
        load_w.start()
        wo_c.start()
        for copy in y3:
            copy.start()
        for unit, source in zip(ff[0], (sum1u, sum1d)):
            unit.start_x(source)
        for unit, source in zip(ff[1], (sum2u, sum2d)):
            unit.start_x(source)
        y_home.start()

    def slot_end(i):
        pair_c[i].start()
        if i == 0:
            load_w.wait()
            wo_c.wait_recv()
            rcw[...] = (rcw[...].astype(F32) + kw[...].astype(F32)).astype(BF)
            wo_y.start()
            for copy in loads:
                copy.wait()
        if i == 1:
            ff_z(0)
            send_other(0)
        if i == 2:
            each(ff[0], "start_z2")
            ff_z(1)
            send_other(1)
            for unit, copy, held, own in zip(ff[2], y3, kept[2], (k3u, k3d)):
                copy.wait_recv()
                held[...] = (held[...].astype(F32) + own[...].astype(F32)).astype(BF)
                unit.start_x(held)
        if i == 3:
            each(ff[0], "start_back")
            each(ff[1], "start_z2")
            send_other(2)
            y_away.start()
            wo_y.wait_recv()
            ryw[...] = (ryw[...].astype(F32) + rcw[:, 0:heads_half].astype(F32)).astype(BF)
            wo.start_x(ryw)
        if i == 4:
            each(ff[0], "start_back1")
            each(ff[1], "start_back")
            ff_z(2)
            join_own(0)
            wo.start_z(ryw)
        if i == 5:
            each(ff[0], "start_back_x")
            each(ff[1], "start_back1")
            each(ff[2], "start_z2")
            join_own(1)
            wo.start_back()
            pairs[0].start_z(lambda: ryp.at[0])

    @pl.when(step == 0)
    def _():
        slot_start()
        kht[64:160, :] = back_ref[...]
        lanes = lax.broadcasted_iota(jnp.int32, (tokens, 64), 1)
        vx[:, 64:128] = jnp.where(lanes < 2, -1.0, 0.0).astype(BF)
        dox[64:128, :] = jnp.zeros((64, tokens), BF)
        x = x_ref[...].astype(F32)
        inverse = lax.rsqrt(jnp.mean(x * x, axis=-1, keepdims=True) + EPS)
        n1t[...] = (x * inverse * gain_ref[...]).astype(BF).T
        dn[...] = jnp.zeros_like(dn)
        gtab[...] = jnp.zeros_like(gtab)

    side = lax.broadcasted_iota(jnp.int32, (buckets, 128), 1)
    first_row = jnp.where(step < 3, 8 + 2 * step, 2 * (step - 3))
    dqs, dks, dvs = [], [], []
    for h in range(2):
        span = slice(64 * h, 64 * h + 64)
        scaled = dot_ref[span, :].astype(F32) * r_ref[0, h : h + 1, :]
        inner = jnp.sum(scaled * ot_ref[span, :].astype(F32), axis=0, keepdims=True)
        upper = inner.astype(BF)
        lower = (inner - upper.astype(F32)).astype(BF)
        dox[0:64, :] = scaled.astype(BF)
        dox[64:66, :] = jnp.concatenate([upper, lower], 0)
        vx[:, 0:64] = v_ref[:, span]
        kht[0:64, :] = k_ref[:, span].T
        dp = dg(vx[...], dox[...], 1, 0)
        p = p_ref[h]
        ds = (p.astype(F32) * dp).astype(BF)
        dvs.append(dg(p, dox[0:64, :], 1, 1).astype(BF))
        dks.append((dg(ds, qt_ref[span, :], 1, 1) * 0.125).astype(BF))
        both = dg(kht[...], ds, 1, 0)
        dqs.append((both[0:64] * 0.125).astype(BF).T)
        left = both[64:160]
        left_hi = left.astype(BF)
        left_lo = (left - left_hi.astype(F32)).astype(BF)
        hot = hot_ref[...]
        blocks = dg(left_hi, hot, 1, 0) + dg(left_lo, hot, 1, 0)
        for t in range(3):
            inside = (side >= t * buckets) & (side < (t + 1) * buckets)
            block = jnp.where(inside, blocks[t * buckets : (t + 1) * buckets], 0.0)
            rolled = pltpu.roll(block, (129 - (t + 1) * buckets) % 128, 1, stride=1, stride_axis=0)
            gtab[t, pl.ds(first_row + h, 1), :] = jnp.sum(rolled, axis=0, keepdims=True)
    grads = jnp.concatenate(dqs + dks + dvs, axis=1)
    weights = jnp.concatenate([wq_ref[...], wk_ref[...], wv_ref[...]], axis=1)
    dn[...] += dg(grads, weights, 1, 1)
    gp[step] = dg(n1t[...], grads, 1, 0).astype(BF)
    for i in range(6):
        pl.when(step == i)(functools.partial(slot_end, i))

    @pl.when(step == pl.num_programs(0) - 1)
    def _():
        x = x_ref[...].astype(F32)
        inverse = lax.rsqrt(jnp.mean(x * x, axis=-1, keepdims=True) + EPS)
        normed = x * inverse
        total = dn[...]
        grad_gain = jnp.sum(total * normed, axis=0, keepdims=True)
        inner = total * gain_ref[...]
        added = inverse * (inner - normed * jnp.mean(inner * normed, axis=-1, keepdims=True))
        gin[...] = (dh_ref[...] + added).astype(BF)
        lines = width // 128
        for j in range(lines):
            lane = slice(j * 128, (j + 1) * 128)
            sums[0, j : j + 1, :] = grad_gain[:, lane]
            sums[0, lines + j : lines + j + 1, :] = ggf_ref[:, lane]
        sums[0, 2 * lines : 16, :] = jnp.zeros((16 - 2 * lines, 128), F32)
        line = lax.broadcasted_iota(jnp.int32, (128, 128), 0)
        lane = lax.broadcasted_iota(jnp.int32, (128, 128), 1)
        shift = jnp.where(lane < 64, lane, lane - 128)
        bucket = jnp.clip(-shift, -(buckets // 2), buckets // 2 - 1) + buckets // 2
        table = jnp.zeros((16, 128), F32)
        for t in range(3):
            pick = jnp.where(line == bucket + t * buckets, 1.0, 0.0)
            table = table + lax.dot_general(
                gtab[t], pick, (((1,), (1,)), ((), ())),
                precision=lax.Precision.HIGHEST, preferred_element_type=F32,
            )
        sums[0, 16:32, :] = table
        hops = bits + 1
        hop = None
        count = 0

        def small_hop():
            nonlocal hop, count
            if hop is not None:
                hop.wait_recv()
                k = count
                if k == 1:
                    sums[1, 0:16] = sums[0, 0:16] + got[0, 0:16]
                    sums[1, 16:24] = sums[0, 16:24] + got[0, 24:32]
                    sums[1, 24:32] = jnp.zeros((8, 128), F32)
                else:
                    sums[k] = sums[k - 1] + got[k - 1]
                hop = None
            if count < hops:
                flips = dict(mp_flip=1) if count == 0 else dict(dp_flip=1 << (count - 1))
                k = count
                hop = links.remote(lambda: sums.at[k], lambda: got.at[k], **flips)
                hop.start()
                started.append(hop)
                count += 1

        started = []
        small_hop()
        gin_away.start()
        gin_home.start()
        join_own(2)
        each(ff[0], "start_back_c")
        each(ff[1], "start_back_x")
        each(ff[2], "start_back")
        wo.start_back_x()
        pairs[1].start_z(lambda: ryp.at[1])
        pairs[0].start_back()
        small_hop()
        pairs[2].start_z(lambda: ryp.at[2])
        pairs[0].start_back_x()
        each(ff[1], "start_back_c")
        each(ff[2], "start_back1")
        pairs[1].start_back()
        wo.start_back_c()
        small_hop()
        pairs[2].start_back()
        each(ff[2], "start_back_x")
        pairs[1].start_back_x()
        pairs[0].start_back_c()
        small_hop()
        pairs[2].start_back_x()
        each(ff[2], "start_back_c")
        pairs[1].start_back_c()
        small_hop()
        pairs[2].start_back_c()
        while count < hops or hop is not None:
            small_hop()
        small[...] = sums[hops]
        y_away.wait_recv()
        gin_away.wait_recv()
        for unit in units:
            unit.end()
        for copy in [y_away, gin_away, wo_c, wo_y] + y3 + pair_c + pair_y + started:
            copy.wait_send()
        y_home.wait()
        gin_home.wait()


def backward(p, qt, kv, ot, dot, r, back, hot, x, gain, dh, ggf, wqkv, parts, gwo, y, n_dp, buckets):
    channels, tokens = qt.shape
    width = x.shape[1]
    n_pairs = channels // 128
    half = n_pairs // 2
    chunk = parts[0].shape[1]
    group = 3 * 128
    once = lambda shape: pl.BlockSpec(
        shape, lambda i: (0,) * len(shape), pipeline_mode=pl.Buffered(1)
    )
    pick = lambda i: lax.rem(i + half, n_pairs)
    side = lambda i: pick(i) // half
    place = lambda i: lax.rem(pick(i), half)
    turned = pl.BlockSpec((128, tokens), lambda i: (pick(i), 0))
    column = lambda rows, j, n: pl.BlockSpec(
        (rows, 128), lambda i: (0, side(i) * n * half + j * half + place(i))
    )
    shapes = []
    for k in range(3):
        shapes += [(width, chunk, True), (chunk, width, True)]
    shapes += [(width, group, False)] * 4
    units, far = [], []
    for n, w, deepest in shapes:
        units += [
            pltpu.VMEM((n // 4, w), BF),
            pltpu.VMEM((n // 16, w), BF),
            pltpu.VMEM((n // 8, w) if deepest else (3, n // 16, w), BF),
            pltpu.VMEM((n // 16, w), BF),
        ]
        far.append(pltpu.VMEM((max(n_dp // 16, 1), n // 16, w), BF))
    bits = n_dp.bit_length() - 1
    part_u, part_d = parts[0].shape, parts[1].shape
    copies = 160 + (10 * (n_dp // 16) if n_dp > 16 else 0)
    scratch = [
        pltpu.VMEM((tokens, 128), BF),
        pltpu.VMEM((128, tokens), BF),
        pltpu.VMEM((160, tokens), BF),
        pltpu.VMEM((width, tokens), BF),
        pltpu.VMEM((tokens, width), F32),
        pltpu.VMEM((3, 16, 128), F32),
        pltpu.VMEM((6, width, group), BF),
        pltpu.VMEM((6, width // 2, group), BF),
        pltpu.VMEM((3, width // 2, group), BF),
        pltpu.VMEM((tokens, width), BF),
        pltpu.VMEM(part_u, BF),
        pltpu.VMEM(part_d, BF),
        pltpu.VMEM(part_u, BF),
        pltpu.VMEM(part_d, BF),
        pltpu.VMEM(part_u, BF),
        pltpu.VMEM(part_d, BF),
        pltpu.VMEM(part_u, BF),
        pltpu.VMEM(part_d, BF),
        pltpu.VMEM((width // 2, width), BF),
        pltpu.VMEM((width // 2, width), BF),
        pltpu.VMEM((width // 2, width // 2), BF),
        pltpu.VMEM((bits + 2, 32, 128), F32),
        pltpu.VMEM((bits + 2, 32, 128), F32),
    ]
    scratch += units
    if n_dp > 16:
        scratch += far
    scratch += [pltpu.SemaphoreType.DMA((copies,))] * 2
    return pl.pallas_call(
        functools.partial(back_kernel, n_dp=n_dp, buckets=buckets),
        grid=(n_pairs,),
        in_specs=[
            pl.BlockSpec((2, tokens, tokens), lambda i: (pick(i), 0, 0)),
            turned,
            column(tokens, 0, 2),
            column(tokens, 1, 2),
            turned,
            turned,
            pl.BlockSpec((1, 2, tokens), lambda i: (pick(i), 0, 0)),
            once((96, tokens)),
            once((tokens, 128)),
            once((tokens, width)),
            once((1, width)),
            once((tokens, width)),
            once((1, width)),
            column(width, 0, 3),
            column(width, 1, 3),
            column(width, 2, 3),
        ]
        + [ANY] * 10,
        out_specs=[ANY] * 6 + [once((32, 128))],
        out_shape=[
            SHAPE((2, tokens // 2, width), BF),
            SHAPE((2, tokens // 2, width), BF),
            SHAPE((3, width, group), BF),
            SHAPE((width, group), BF),
            SHAPE((width, 3 * chunk), BF),
            SHAPE((3 * chunk, width), BF),
            SHAPE((32, 128), F32),
        ],
        scratch_shapes=scratch,
        compiler_params=params(60, collective_id=5, has_side_effects=True),
        name="backward",
    )(p, qt, kv, kv, ot, dot, r, back, hot, x, gain, dh, ggf, wqkv, wqkv, wqkv, *parts, gwo, y)


def local(
    n_dp, inputs, roi, cotangent, doc_lengths, live_mask, bucket_cells,
    gain_attn, gain_ffn, w_query, w_key, w_value, w_out, w_up, w_down, tables,
):
    rows, width = inputs.shape[1], inputs.shape[2]
    tokens = 2 * rows
    third = w_query.shape[1]
    heads = third // HDIM
    buckets = tables.shape[1]
    tab = jnp.pad(
        tables.transpose(2, 0, 1).reshape(heads, 3 * buckets), ((0, 2), (0, 128 - 3 * buckets))
    )
    ga, gf = gain_attn.reshape(1, width), gain_ffn.reshape(1, width)
    x, tabo, wqkv, qt, kv, upo = entry(
        inputs, roi, tab, ga, w_query, w_key, w_value, w_up
    )
    p, mixt, r, hot, back, dyo, woo, upo, dno = attend(
        doc_lengths, live_mask.reshape(2, 1, tokens), bucket_cells, tab, tabo, qt, kv,
        cotangent, w_out, w_up, w_down, upo, buckets,
    )
    y, gwo, dh, dmt, gain_f, *parts = middle(
        x, mixt, w_out, woo, cotangent, dyo, gf, w_up, upo, w_down, dno
    )
    yret, gret, fqkv, fwo, fup, fdn, small = backward(
        p, qt, kv, mixt, dmt, r, back, hot, x, ga, dh, gain_f, wqkv, parts, gwo, y, n_dp, buckets
    )
    lines = width // 128
    out = inputs.astype(F32) + roi.astype(F32) + yret.astype(F32)
    grad_in = cotangent.astype(F32) + gret.astype(F32)
    table_out = small[16 : 16 + heads, : 3 * buckets].reshape(heads, 3, buckets).transpose(1, 2, 0)
    gq, gk, gv = (
        jnp.concatenate([fqkv[k, :, j * 128 : (j + 1) * 128] for k in range(3)], axis=1).astype(F32)
        for j in range(3)
    )
    return (
        out,
        grad_in,
        small[0:lines].reshape(width),
        small[lines : 2 * lines].reshape(width),
        gq,
        gk,
        gv,
        fwo.T.astype(F32),
        fup.astype(F32),
        fdn.astype(F32),
        table_out,
    )


def solution(mesh):
    n_dp = mesh.shape["dp"]
    rows = P(None, ("dp", "mp"), None)
    columns, lines = P(None, "mp"), P("mp", None)
    tables = P(None, None, "mp")
    return jax.shard_map(
        functools.partial(local, n_dp),
        mesh=mesh,
        in_specs=(
            rows, rows, rows, P(None, "dp", None), P(None, "dp"), P(None, None, "dp"),
            P(), P(), columns, columns, columns, lines, columns, lines, tables,
        ),
        out_specs=(
            rows, rows, P(), P(), columns, columns, columns, lines, columns, lines, tables,
        ),
        check_vma=False,
    )
```

```python
import functools
import math

import jax
import jax.numpy as jnp
from jax import lax
from jax.experimental import pallas as pl
from jax.experimental.pallas import tpu as pltpu
from jax.sharding import PartitionSpec as P

BF = jnp.bfloat16
F32 = jnp.float32
HDIM = 64
EPS = 1e-06
MASKED = -1e30
MESH = pl.DeviceIdType.MESH
VMEM = pl.BlockSpec(memory_space=pltpu.VMEM)
ANY = pl.BlockSpec(memory_space=pltpu.HBM)
SHAPE = jax.ShapeDtypeStruct


def dg(a, b, ca, cb):
    return lax.dot_general(a, b, (((ca,), (cb,)), ((), ())), preferred_element_type=F32)


def params(limit=58, **more):
    return pltpu.CompilerParams(vmem_limit_bytes=limit << 20, **more)


class Copy:
    def __init__(self, make):
        self.make = make

    def start(self):
        self.make().start()

    def wait(self):
        self.make().wait()

    def wait_recv(self):
        self.make().wait_recv()

    def wait_send(self):
        self.make().wait_send()


def now(ref):
    return ref() if callable(ref) else ref


class Links:
    def __init__(self, send, recv):
        self.send, self.recv, self.count = send, recv, 0
        self.d, self.m = lax.axis_index("dp"), lax.axis_index("mp")

    def flipped(self, dp_flip, mp_flip):
        dp = self.d ^ dp_flip if dp_flip else self.d
        mp = self.m ^ mp_flip if mp_flip else self.m
        return dp, mp

    def remote(self, src, dst, dp_flip=0, mp_flip=0):
        i = self.count
        self.count += 1
        return Copy(
            lambda: pltpu.make_async_remote_copy(
                src_ref=now(src),
                dst_ref=now(dst),
                send_sem=self.send.at[i],
                recv_sem=self.recv.at[i],
                device_id=self.flipped(dp_flip, mp_flip),
                device_id_type=MESH,
            )
        )

    def local(self, src, dst):
        i = self.count
        self.count += 1
        return Copy(lambda: pltpu.make_async_copy(now(src), now(dst), self.send.at[i]))

    def barrier(self, flips):
        sem = pltpu.get_barrier_semaphore()
        for flip in flips:
            pl.semaphore_signal(
                sem, inc=1, device_id=self.flipped(*flip), device_id_type=MESH
            )
        pl.semaphore_wait(sem, len(flips))


def rows_at(start, size, unit):
    return pl.ds(pl.multiple_of(start, unit), size)


def accumulate(into, other, start=0):
    n = into.shape[0]
    unit = 48 if n % 48 == 0 else 32

    def body(i, carry):
        here = rows_at(i * unit, unit, 16)
        there = rows_at(start + i * unit, unit, 16)
        into[here] = (into[here].astype(F32) + other[there].astype(F32)).astype(BF)
        return carry

    lax.fori_loop(0, n // unit, body, 0)


def carry_over(into, source, start=0):
    n = into.shape[0]
    unit = 48 if n % 48 == 0 else 32

    def body(i, carry):
        into[rows_at(i * unit, unit, 16)] = source[rows_at(start + i * unit, unit, 16)]
        return carry

    lax.fori_loop(0, n // unit, body, 0)


def entry_kernel(
    inp, roi, tab, gain, wq, wk, wv, wup,
    xf, tabo, wqkv, qt, kv, upo,
    sent, n1, send, recv,
):
    links = Links(send, recv)
    d, m = links.d, links.m
    rows = inp.shape[1]
    width, third = wq.shape
    piece = width // 8
    core, cross, deep = d & 1, (d >> 1) & 1, (d >> 2) & 1
    place = core * 4 + cross * 2 + deep
    links.barrier(((0, 1), (1, 0), (2, 0), (4, 0)))
    started = []

    def go(copy):
        copy.start()
        started.append(copy)
        return copy

    own_cols = [slice(j * third, (j + 1) * third) for j in range(3)]
    other_cols = [slice((3 + j) * third, (4 + j) * third) for j in range(3)]
    spot = rows_at(place * piece, piece, piece)
    first = [
        go(links.remote(w.at[spot], wqkv.at[spot, c], mp_flip=1))
        for w, c in zip((wq, wk, wv), other_cols)
    ]
    tab_copy = go(links.remote(tab, tabo, mp_flip=1))
    chunk = rows // 2
    row_copies = []
    for j in range(2):
        part = slice(j * chunk, (j + 1) * chunk)
        sent[part] = (inp[1 - m, part].astype(F32) + roi[1 - m, part].astype(F32)).astype(BF)
        here = rows_at(m * rows + j * chunk, chunk, chunk)
        row_copies.append(go(links.remote(sent.at[part], xf.at[here], mp_flip=1)))
    up_copy = go(links.remote(wup.at[spot], upo.at[spot], mp_flip=1))
    for w, c in zip((wq, wk, wv), own_cols):
        wqkv[:, c] = w[...]

    def normalise(where):
        x = xf[where].astype(F32)
        inverse = lax.rsqrt(jnp.mean(x * x, axis=-1, keepdims=True) + EPS)
        n1[where] = (x * inverse * gain[...]).astype(BF)

    own = rows_at(m * rows, rows, rows)
    xf[own] = (inp[m].astype(F32) + roi[m].astype(F32)).astype(BF)
    normalise(own)

    def project(where, side):
        rows_in = n1[where]
        base = side * 3 * third
        kv[where, side * 2 * third : (side + 1) * 2 * third] = dg(
            rows_in, wqkv[:, base + third : base + 3 * third], 1, 0
        ).astype(BF)
        qt[side * third : (side + 1) * third, where] = dg(
            wqkv[:, base : base + third], rows_in, 0, 1
        ).astype(BF)

    project(own, 0)
    stage = first
    for flip, begin, count in (
        (4, place, 1),
        (2, core * 4 + cross * 2, 2),
        (1, core * 4, 4),
    ):
        for copy in stage:
            copy.wait_recv()
        there = wqkv.at[rows_at(begin * piece, count * piece, piece), 3 * third : 6 * third]
        stage = [go(links.remote(there, there, dp_flip=flip))]
    for j in range(2):
        row_copies[j].wait_recv()
        here = rows_at((1 - m) * rows + j * chunk, chunk, chunk)
        normalise(here)
        project(here, 0)
    for copy in stage:
        copy.wait_recv()
    for j in range(2):
        project(slice(j * rows, (j + 1) * rows), 1)
    tab_copy.wait_recv()
    up_copy.wait_recv()
    for copy in started:
        copy.wait_send()


def entry(inputs, roi, tab, gain, wq, wk, wv, wup):
    rows, width = inputs.shape[1], inputs.shape[2]
    third = wq.shape[1]
    tokens = 2 * rows
    return pl.pallas_call(
        entry_kernel,
        out_shape=[
            SHAPE((tokens, width), BF),
            SHAPE(tab.shape, F32),
            SHAPE((width, 6 * third), BF),
            SHAPE((2 * third, tokens), BF),
            SHAPE((tokens, 4 * third), BF),
            SHAPE(wup.shape, BF),
        ],
        in_specs=[VMEM] * 7 + [ANY],
        out_specs=[VMEM] * 5 + [ANY],
        scratch_shapes=[
            pltpu.VMEM((rows, width), BF),
            pltpu.VMEM((tokens, width), BF),
            pltpu.SemaphoreType.DMA((12,)),
            pltpu.SemaphoreType.DMA((12,)),
        ],
        compiler_params=params(58, collective_id=1, has_side_effects=True),
        name="entry",
    )(inputs, roi, tab, gain, wq, wk, wv, wup)


def attend_kernel(
    lengths, live, cells, tab, tabo, qt_ref, k_ref, v_ref, cot, wo, wup, wdn, upo_in,
    p_ref, o_ref, r_ref, hot_ref, back_ref, dyo, woo, upo, dno,
    kx, qx, vx, mask, mats, hott_ref, send, recv, *, buckets,
):
    links = Links(send, recv)
    d, m = links.d, links.m
    tokens = k_ref.shape[0]
    rows = tokens // 2
    width, hidden = wup.shape
    inner = wo.shape[0]
    step = pl.program_id(0)
    core, cross, deep = d & 1, (d >> 1) & 1, (d >> 2) & 1
    place = core * 4 + cross * 2 + deep

    def block(full, begin, count):
        piece = full.shape[0] // 8
        return full.at[rows_at(begin * piece, count * piece, piece)]

    up = functools.partial(block, upo)
    down = functools.partial(block, dno)
    out = functools.partial(block, woo)
    dpiece, opiece = hidden // 8, inner // 8
    quarter = core * 4 + deep * 2
    down_y = links.remote(
        wdn.at[rows_at(quarter * dpiece, 2 * dpiece, dpiece)], down(quarter, 2), mp_flip=1
    )
    out_y = links.remote(wo.at[rows_at(place * opiece, opiece, opiece)], out(place, 1), mp_flip=1)
    dy_y = links.remote(cot.at[1 - m], dyo, mp_flip=1)
    up_z = links.remote(up(place, 1), up(place, 1), dp_flip=4)
    pair = core * 4 + cross * 2
    up_x = links.remote(up(pair, 2), up(pair, 2), dp_flip=2)
    up_c = links.remote(up(core * 4, 4), up(core * 4, 4), dp_flip=1)
    down_z = links.remote(down(quarter, 2), down(quarter, 2), dp_flip=4)
    down_c = links.remote(down(core * 4, 4), down(core * 4, 4), dp_flip=1)
    out_z = links.remote(out(place, 1), out(place, 1), dp_flip=4)
    out_x = links.remote(out(pair, 2), out(pair, 2), dp_flip=2)
    out_c = links.remote(out(core * 4, 4), out(core * 4, 4), dp_flip=1)

    def slot0():
        links.barrier(((0, 1), (1, 0), (2, 0), (4, 0)))
        up_z.start()
        down_y.start()
        out_y.start()
        dy_y.start()

    def slot4():
        up_z.wait_recv()
        up_x.start()

    def slot6():
        out_y.wait_recv()
        out_z.start()

    def slot7():
        down_y.wait_recv()
        down_z.start()

    def slot9():
        out_z.wait_recv()
        out_x.start()

    def slot11():
        up_x.wait_recv()
        up_c.start()
        out_x.wait_recv()
        out_c.start()

    def last():
        down_z.wait_recv()
        down_c.start()
        for copy in (dy_y, up_c, out_c, down_c):
            copy.wait_recv()
        for copy in (down_y, out_y, dy_y, up_z, up_x, up_c, down_z, down_c, out_z, out_x, out_c):
            copy.wait_send()

    slots = {0: slot0, 4: slot4, 6: slot6, 7: slot7, 9: slot9, 11: slot11}

    @pl.when(step == 0)
    def _():
        slot0()
        vx[64:80, :] = jnp.ones((16, tokens), BF)
        lane = lax.broadcasted_iota(jnp.int32, (buckets, tokens), 0)
        for t in range(3):
            row = cells[m, t : t + 1, :]
            hott_ref[t * buckets : (t + 1) * buckets, :] = jnp.where(row == lane, 1.0, 0.0).astype(BF)
            mirror = jnp.where(row == buckets - 1 - lane, 1.0, 0.0).astype(BF)
            back_ref[t * buckets : (t + 1) * buckets, :] = mirror
        hott_ref[96:128, :] = jnp.zeros((32, tokens), BF)
        wide_hot = hott_ref[...].T
        hot_ref[...] = wide_hot
        hot = wide_hot[:, 0:96]
        kx[:, 64:160] = hot
        kx[:, 160:256] = hot
        row_ids = lax.broadcasted_iota(jnp.int32, (1, tokens), 1)
        col_ids = lax.broadcasted_iota(jnp.int32, (tokens, 1), 0)
        seg_row = jnp.zeros((1, tokens), jnp.int32)
        seg_col = jnp.zeros((tokens, 1), jnp.int32)
        end = 0
        for i in range(lengths.shape[2]):
            end = end + lengths[m, 0, i]
            seg_row = seg_row + jnp.where(row_ids >= end, 1, 0)
            seg_col = seg_col + jnp.where(col_ids >= end, 1, 0)
        live_row = live[m].astype(F32)
        live_col = jnp.broadcast_to(live_row, (8, tokens)).T[:, 0:1]
        code = jnp.where(live_col == 1.0, seg_col, -1)
        allowed = (code == seg_row) | (col_ids == row_ids)
        mask[...] = jnp.where(allowed, 0.0, MASKED)
        line = lax.broadcasted_iota(jnp.int32, (128, 128), 0)
        lane = lax.broadcasted_iota(jnp.int32, (128, 128), 1)
        shift = jnp.where(lane < 64, lane, lane - 128)
        bucket = jnp.clip(-shift, -(buckets // 2), buckets // 2 - 1) + buckets // 2
        side = lax.broadcasted_iota(jnp.int32, (buckets, 128), 1)
        heads = mats.shape[0] // 2
        for part, table in enumerate((tab, tabo)):
            exact = table[...]
            upper = exact.astype(BF)
            lower = (exact - upper.astype(F32)).astype(BF)
            for t in range(3):
                pick = jnp.where(line == bucket + t * buckets, 1.0, 0.0).astype(BF)
                inside = (side >= t * buckets) & (side < (t + 1) * buckets)
                for level, source in enumerate((upper, lower)):
                    lines = dg(source, pick, 1, 0)
                    for h in range(heads):
                        wide = jnp.broadcast_to(lines[h : h + 1], (buckets, 128))
                        rolled = pltpu.roll(wide, t * buckets, 1, stride=1, stride_axis=0)
                        begin = level * 3 * buckets + t * buckets
                        mats[part * heads + h, begin : begin + buckets, :] = jnp.where(
                            inside, rolled, 0.0
                        ).astype(BF)

    vt = v_ref[...].T
    for h in range(2):
        for at, action in slots.items():
            if at % 2 == h and at > 0:
                pl.when(step == at // 2)(action)
        span = slice(64 * h, 64 * h + 64)
        kx[:, 0:64] = k_ref[:, span]
        qx[0:64, :] = qt_ref[span, :] * BF(0.125)
        qx[64:256, :] = dg(mats[2 * step + h], hott_ref[...], 1, 0).astype(BF)
        vx[0:64, :] = vt[span, :]
        s = dg(kx[...], qx[...], 1, 0) + mask[...]
        top = jnp.max(s, axis=0, keepdims=True)
        p = jnp.exp(s - top).astype(BF)
        p_ref[h] = p
        o = dg(vx[...], p, 1, 0)
        r = 1.0 / o[64:65, :]
        o_ref[span, :] = (o[0:64] * r).astype(BF)
        r_ref[0, h : h + 1, :] = r
    pl.when(step == pl.num_programs(0) - 1)(last)


def attend(lengths, live, cells, tab, tabo, qt, kv, cot, wo, wup, wdn, upo, buckets):
    channels, tokens = qt.shape
    width, hidden = wup.shape
    inner = wo.shape[0]
    pairs = channels // 128
    half = pairs // 2
    whole = lambda shape: pl.BlockSpec(shape, lambda i: (0,) * len(shape))
    return pl.pallas_call(
        functools.partial(attend_kernel, buckets=buckets),
        grid=(pairs,),
        in_specs=[
            pl.BlockSpec(memory_space=pltpu.SMEM),
            whole(live.shape),
            whole(cells.shape),
            whole(tab.shape),
            whole(tabo.shape),
            pl.BlockSpec((128, tokens), lambda i: (i, 0)),
            pl.BlockSpec((tokens, 128), lambda i: (0, (i // half) * 2 * half + i % half)),
            pl.BlockSpec((tokens, 128), lambda i: (0, (i // half) * 2 * half + half + i % half)),
            ANY, ANY, ANY, ANY, ANY,
        ],
        out_specs=[
            pl.BlockSpec((2, tokens, tokens), lambda i: (i, 0, 0)),
            pl.BlockSpec((128, tokens), lambda i: (i, 0)),
            pl.BlockSpec((1, 2, tokens), lambda i: (i, 0, 0)),
            whole((tokens, 128)),
            whole((96, tokens)),
            ANY, ANY, ANY, ANY,
        ],
        out_shape=[
            SHAPE((2 * pairs, tokens, tokens), BF),
            SHAPE((channels, tokens), BF),
            SHAPE((pairs, 2, tokens), F32),
            SHAPE((tokens, 128), BF),
            SHAPE((96, tokens), BF),
            SHAPE((tokens // 2, width), BF),
            SHAPE((inner, width), BF),
            SHAPE((width, hidden), BF),
            SHAPE((hidden, width), BF),
        ],
        input_output_aliases={12: 7},
        scratch_shapes=[
            pltpu.VMEM((tokens, 256), BF),
            pltpu.VMEM((256, tokens), BF),
            pltpu.VMEM((80, tokens), BF),
            pltpu.VMEM((tokens, tokens), F32),
            pltpu.VMEM((2 * pairs, 192, 128), BF),
            pltpu.VMEM((128, tokens), BF),
            pltpu.SemaphoreType.DMA((20,)),
            pltpu.SemaphoreType.DMA((20,)),
        ],
        compiler_params=params(58, collective_id=3, has_side_effects=True),
        name="attend",
    )(lengths, live, cells, tab, tabo, qt, kv, kv, cot, wo, wup, wdn, upo)


def middle_kernel(
    x_ref, mixt_ref, wo_in, woo_in, cot, dyo, gain_ref, wup_in, upo_in, wdn_in, dno_in,
    y_ref, gwo_ref, dh_ref, dmt_ref, gg_ref,
    sum1u, sum1d, sum2u, sum2d, own3u, own3d, far3u, far3d,
    h1, n2, n2t, yacc, dn, wo_ref, dy_ref, gu, gd, rcu, rcd, ryu, ryd, send, recv,
):
    links = Links(send, recv)
    core = links.d & 1
    step = pl.program_id(0)
    last = pl.num_programs(0) - 1
    half_steps = pl.num_programs(0) // 2
    early = step < half_steps
    width, chunk = gu.shape[1:]
    keep_u, give_u = (rows_at(c * (width // 2), width // 2, 16) for c in (core, 1 - core))
    keep_d, give_d = (rows_at(c * (chunk // 2), chunk // 2, 16) for c in (core, 1 - core))

    def core_copies(i):
        return (
            pltpu.make_async_remote_copy(
                gu.at[i % 2, give_u], rcu.at[i], send.at[0, i], recv.at[0, i],
                device_id=(links.d ^ 1, links.m), device_id_type=MESH,
            ),
            pltpu.make_async_remote_copy(
                gd.at[i % 2, give_d], rcd.at[i], send.at[1, i], recv.at[1, i],
                device_id=(links.d ^ 1, links.m), device_id_type=MESH,
            ),
        )

    def pair_copies(i):
        return (
            pltpu.make_async_remote_copy(
                rcu.at[i], ryu.at[i], send.at[2, i], recv.at[2, i],
                device_id=(links.d, 1 - links.m), device_id_type=MESH,
            ),
            pltpu.make_async_remote_copy(
                rcd.at[i], ryd.at[i], send.at[3, i], recv.at[3, i],
                device_id=(links.d, 1 - links.m), device_id_type=MESH,
            ),
        )

    def settle(i):
        for copy in core_copies(i):
            copy.wait_recv()
        for copy in core_copies(i):
            copy.wait_send()
        accumulate(rcu.at[i], gu.at[i % 2], core * (width // 2))
        accumulate(rcd.at[i], gd.at[i % 2], core * (chunk // 2))

    @pl.when(step == 0)
    def _():
        links.barrier(((0, 1), (1, 0)))
        m = links.m
        rows = dyo.shape[0]
        dy_ref[rows_at(m * rows, rows, rows)] = cot[m]
        dy_ref[rows_at((1 - m) * rows, rows, rows)] = dyo[...]
        inner = wo_in.shape[0]
        wo_ref[0:inner] = wo_in[...]
        wo_ref[inner:] = woo_in[...]
        added = dg(mixt_ref[...], wo_ref[...], 0, 0)
        h = x_ref[...].astype(F32) + added
        h1[...] = h
        yacc[...] = added
        inverse = lax.rsqrt(jnp.mean(h * h, axis=-1, keepdims=True) + EPS)
        normed = (h * inverse * gain_ref[...]).astype(BF)
        n2[...] = normed
        n2t[...] = normed.T
        dn[...] = jnp.zeros_like(dn)

    wup = jnp.where(early, upo_in[...], wup_in[...])
    wdn = jnp.where(early, dno_in[...], wdn_in[...])
    dy = dy_ref[...]
    u = dg(n2[...], wup, 1, 0)
    cdf = 0.5 * (1.0 + lax.erf(u * 0.7071067811865476))
    act = (u * cdf).astype(BF)
    grad_act = dg(dy, wdn, 1, 1)
    density = jnp.exp(u * u * (-0.5)) * 0.3989422804014327
    du = (grad_act * (cdf + u * density)).astype(BF)
    yacc[...] += dg(act, wdn, 1, 0)

    @pl.when(step > 0)
    def _():
        settle(step - 1)

    @pl.when((step > 0) & (step < half_steps))
    def _():
        for copy in pair_copies(step - 1):
            copy.start()

    dn[...] += dg(du, wup, 1, 1)
    gu[step % 2] = dg(n2t[...], du, 1, 0).astype(BF)
    gd[step % 2] = dg(act, dy, 0, 0).astype(BF)
    for copy in core_copies(step):
        copy.start()

    @pl.when(step == last)
    def _():
        h = h1[...]
        inverse = lax.rsqrt(jnp.mean(h * h, axis=-1, keepdims=True) + EPS)
        normed = h * inverse
        grad = dn[...]
        gg_ref[...] = jnp.sum(grad * normed, axis=0, keepdims=True)
        inner = grad * gain_ref[...]
        added = inverse * (inner - normed * jnp.mean(inner * normed, axis=-1, keepdims=True))
        dh_ref[...] = added
        y_ref[...] = yacc[...].astype(BF)
        low = (dy_ref[...].astype(F32) + added).astype(BF)
        gwo_ref[...] = dg(low, mixt_ref[...], 0, 1).astype(BF)
        dmt_ref[...] = dg(wo_ref[...], low, 1, 1).astype(BF)
        settle(last)
        n = rcu.shape[0] // 2
        for k, (out_u, out_d) in enumerate(((sum1u, sum1d), (sum2u, sum2d))):
            for copy in pair_copies(k):
                copy.wait_recv()
            accumulate(rcu.at[n + k], ryu.at[k])
            accumulate(rcd.at[n + k], ryd.at[k])
            carry_over(out_u, rcu.at[n + k])
            carry_over(out_d, rcd.at[n + k])
        carry_over(own3u, rcu.at[n + 2])
        carry_over(own3d, rcd.at[n + 2])
        carry_over(far3u, rcu.at[2])
        carry_over(far3d, rcd.at[2])
        for k in range(2):
            for copy in pair_copies(k):
                copy.wait_send()


def middle(x, mixt, wo, woo, cot, dyo, gain, wup, upo, wdn, dno):
    tokens, width = x.shape
    half = wup.shape[1]
    chunk = half // 3
    n = 6
    once = lambda shape: pl.BlockSpec(
        shape, lambda i: (0,) * len(shape), pipeline_mode=pl.Buffered(1)
    )
    late = lambda i: jnp.maximum(i - n // 2, 0)
    early = lambda i: jnp.minimum(i, n // 2 - 1)
    part_u, part_d = (width // 2, chunk), (chunk // 2, width)
    outs = [
        ((tokens, width), BF),
        ((width, width), BF),
        ((tokens, width), F32),
        ((width, tokens), BF),
        ((1, width), F32),
    ] + [(part_u, BF), (part_d, BF)] * 4
    return pl.pallas_call(
        middle_kernel,
        grid=(n,),
        in_specs=[
            once((tokens, width)),
            once((width, tokens)),
            once(wo.shape),
            once(woo.shape),
            once(cot.shape),
            once(dyo.shape),
            once((1, width)),
            pl.BlockSpec((width, chunk), lambda i: (0, late(i))),
            pl.BlockSpec((width, chunk), lambda i: (0, early(i))),
            pl.BlockSpec((chunk, width), lambda i: (late(i), 0)),
            pl.BlockSpec((chunk, width), lambda i: (early(i), 0)),
        ],
        out_specs=[once(shape) for shape, _ in outs],
        out_shape=[SHAPE(*entry) for entry in outs],
        scratch_shapes=[
            pltpu.VMEM((tokens, width), F32),
            pltpu.VMEM((tokens, width), BF),
            pltpu.VMEM((width, tokens), BF),
            pltpu.VMEM((tokens, width), F32),
            pltpu.VMEM((tokens, width), F32),
            pltpu.VMEM((width, width), BF),
            pltpu.VMEM((tokens, width), BF),
            pltpu.VMEM((2, width, chunk), BF),
            pltpu.VMEM((2, chunk, width), BF),
            pltpu.VMEM((n,) + part_u, BF),
            pltpu.VMEM((n,) + part_d, BF),
            pltpu.VMEM((2,) + part_u, BF),
            pltpu.VMEM((2,) + part_d, BF),
            pltpu.SemaphoreType.DMA((4, n)),
            pltpu.SemaphoreType.DMA((4, n)),
        ],
        compiler_params=params(60, collective_id=4, has_side_effects=True),
        name="middle",
    )(x, mixt, wo, woo, cot, dyo, gain, wup, upo, wdn, dno)


class Unit:
    def __init__(self, links, n, w, rx, rz, zp, final, far, n_dp, deepest):
        self.links, self.n, self.w = links, n, w
        self.rx, self.rz, self.zp, self.final, self.far = rx, rz, zp, final, far
        self.n_dp, self.stepwise = n_dp, deepest
        d = links.d
        self.core, self.cross = d & 1, (d >> 1) & 1
        self.b0, self.b1 = (d >> 2) & 1, (d >> 3) & 1
        q = n // 16
        self.q = q
        self.xr = links.remote(lambda: self.xr.make_source(), rx, dp_flip=2)
        spot = self.core * 8 + self.cross * 4 + self.b0 * 2 + self.b1
        self.piece = lambda: final(spot * q, q)
        self.home = links.local(zp, self.piece)
        if deepest:
            keep = self.b0 * 2
            give = (1 - self.b0) * 2
            self.z1 = links.remote(lambda: rx.at[rows_at(give * q, 2 * q, 16)], rz[0], dp_flip=4)
            self.z2 = links.remote(
                lambda: rz[0].at[rows_at((1 - self.b1) * q, q, 16)], rz[1], dp_flip=8
            )
            self.g2 = links.remote(zp, self.piece, dp_flip=8)
            both = lambda: final((self.core * 8 + self.cross * 4 + keep) * q, 2 * q)
            self.g1 = links.remote(both, both, dp_flip=4)
        else:
            self.zs, self.gs = [], []
            for r in range(1, 4):
                p0, p1 = self.b0 ^ (r & 1), self.b1 ^ (r >> 1)
                src = lambda p=p0 * 2 + p1: rx.at[rows_at(p * q, q, 16)]
                dst = lambda r=r: rz[0].at[r - 1]
                self.zs.append(links.remote(src, dst, dp_flip=r << 2))
                self.gs.append(links.remote(zp, self.piece, dp_flip=r << 2))
        quad = lambda: final((self.core * 8 + self.cross * 4) * q, 4 * q)
        self.gx = links.remote(quad, quad, dp_flip=2)
        side = lambda: final(self.core * 8 * q, 8 * q)
        self.gc = links.remote(side, side, dp_flip=1)
        if far is not None:
            self.others = [
                links.remote(lambda: far.at[0], lambda r=r: far.at[r], dp_flip=r << 4)
                for r in range(1, n_dp // 16)
            ]

    def start_x(self, source):
        half = self.n // 4
        self.xr.make_source = lambda: now(source).at[rows_at((1 - self.cross) * half, half, 16)]
        self.xr.start()

    def add_x(self, kept):
        half = self.n // 4
        self.xr.wait_recv()
        accumulate(self.rx, now(kept), self.cross * half)

    def start_z(self, kept):
        self.add_x(kept)
        for copy in [self.z1] if self.stepwise else self.zs:
            copy.start()

    def start_z2(self):
        self.z1.wait_recv()
        accumulate(self.rz[0], self.rx, self.b0 * 2 * self.q)
        self.z2.start()

    def start_back(self):
        q = self.q
        if self.stepwise:
            self.z2.wait_recv()
            total = self.rz[0][rows_at(self.b1 * q, q, 16)].astype(F32)
            total = total + self.rz[1][...].astype(F32)
        else:
            for copy in self.zs:
                copy.wait_recv()
            total = self.rx[rows_at((self.b0 * 2 + self.b1) * q, q, 16)].astype(F32)
            for r in range(3):
                total = total + self.rz[0][r].astype(F32)
        if self.far is not None:
            self.far[0] = total.astype(BF)
            for copy in self.others:
                copy.start()
            for r, copy in enumerate(self.others):
                copy.wait_recv()
                total = total + self.far[r + 1].astype(F32)
        self.zp[...] = total.astype(BF)
        self.home.start()
        for copy in [self.g2] if self.stepwise else self.gs:
            copy.start()

    def start_back1(self):
        self.home.wait()
        self.g2.wait_recv()
        self.g1.start()

    def start_back_x(self):
        if self.stepwise:
            self.g1.wait_recv()
        else:
            self.home.wait()
            for copy in self.gs:
                copy.wait_recv()
        self.gx.start()

    def start_back_c(self):
        self.gx.wait_recv()
        self.gc.start()

    def end(self):
        self.gc.wait_recv()
        sent = [self.xr, self.gx, self.gc]
        sent += [self.z1, self.z2, self.g2, self.g1] if self.stepwise else self.zs + self.gs
        if self.far is not None:
            sent += self.others
        for copy in sent:
            copy.wait_send()


def back_kernel(
    p_ref, qt_ref, k_ref, v_ref, ot_ref, dot_ref, r_ref, back_ref, hot_ref,
    x_ref, gain_ref, dh_ref, ggf_ref, wq_ref, wk_ref, wv_ref,
    sum1u, sum1d, sum2u, sum2d, own3u, own3d, far3u, far3d, gwo, y,
    yret, gret, fqkv, fwo, fup, fdn, small,
    vx, dox, kht, n1t, dn, gtab, gp, rcp, ryp, gin,
    k1u, k1d, k2u, k2d, k3u, k3d, ry3u, ry3d, kw, rcw, ryw,
    sums, got, *rest, n_dp, buckets,
):
    units_scratch, rest = rest[: 4 * 10], rest[4 * 10 :]
    far = rest[:10] if n_dp > 16 else [None] * 10
    send, recv = rest[-2:]
    links = Links(send, recv)
    d, m = links.d, links.m
    core = d & 1
    step = pl.program_id(0)
    tokens, width = x_ref.shape
    rows = tokens // 2
    chunk = far3u.shape[1]
    group = gp.shape[2]
    bits = n_dp.bit_length() - 1

    def region(ref, row0, col0, w, lead=None):
        def at(start, count):
            where = rows_at(row0 + start, count, 16)
            if lead is not None:
                return ref.at[lead, where]
            return ref.at[where, col0 : col0 + w]

        return at

    finals = []
    for k in range(3):
        finals.append((width, chunk, region(fup, 0, k * chunk, chunk), True))
        finals.append((chunk, width, region(fdn, k * chunk, 0, width), True))
    finals.append((width, group, region(fwo, 0, 0, group), False))
    for k in range(3):
        finals.append((width, group, region(fqkv, 0, 0, group, lead=k), False))
    units = []
    for i, (n, w, final, deepest) in enumerate(finals):
        rx, zp = units_scratch[4 * i], units_scratch[4 * i + 1]
        rz = units_scratch[4 * i + 2 : 4 * i + 4]
        units.append(Unit(links, n, w, rx, rz, zp, final, far[i], n_dp, deepest))
    ff = (units[0:2], units[2:4], units[4:6])
    wo, pairs = units[6], units[7:10]
    kept = ((k1u, k1d), (k2u, k2d), (ry3u, ry3d))
    heads_half = width // 2

    mine = rows_at(m * rows, rows, rows)
    theirs = rows_at((1 - m) * rows, rows, rows)
    y_home = links.local(lambda: y.at[mine], lambda: yret.at[m])
    y_away = links.remote(lambda: y.at[theirs], lambda: yret.at[m], mp_flip=1)
    gin_home = links.local(lambda: gin.at[mine], lambda: gret.at[m])
    gin_away = links.remote(lambda: gin.at[theirs], lambda: gret.at[m], mp_flip=1)
    loads = [
        links.local(src, dst)
        for src, dst in ((sum1u, k1u), (sum1d, k1d), (sum2u, k2u), (sum2d, k2d), (own3u, k3u), (own3d, k3d))
    ]
    keep = rows_at(core * (width // 2), width // 2, 16)
    give = rows_at((1 - core) * (width // 2), width // 2, 16)
    load_w = links.local(lambda: gwo.at[keep], kw)
    y3 = [links.remote(far3u, ry3u, mp_flip=1), links.remote(far3d, ry3d, mp_flip=1)]
    wo_c = links.remote(lambda: gwo.at[give], rcw, dp_flip=1)
    wo_y = links.remote(lambda: rcw.at[:, heads_half:], ryw, mp_flip=1)
    pair_c = [
        links.remote(lambda i=i: gp.at[i, give], lambda i=i: rcp.at[i], dp_flip=1) for i in range(6)
    ]
    pair_y = [
        links.remote(lambda i=i: rcp.at[i], lambda i=i: ryp.at[i], mp_flip=1) for i in range(3)
    ]

    def settle(i):
        pair_c[i].wait_recv()
        accumulate(rcp.at[i], gp.at[i], core * (width // 2))

    def send_other(i):
        settle(i)
        pair_y[i].start()

    def join_own(k):
        settle(3 + k)
        pair_y[k].wait_recv()
        accumulate(ryp.at[k], rcp.at[3 + k])
        pairs[k].start_x(lambda: ryp.at[k])

    def each(group_of, name, *args):
        for unit in group_of:
            getattr(unit, name)(*args)

    def ff_z(k):
        for unit, held in zip(ff[k], kept[k]):
            unit.start_z(held)

    def slot_start():
        links.barrier(
            [(0, 1)]
            + [(1 << b, 0) for b in range(bits)]
            + [(12, 0)]
            + [(r << 4, 0) for r in range(1, n_dp // 16) if r & (r - 1)]
        )
        for copy in loads:
            copy.start()
        load_w.start()
        wo_c.start()
        for copy in y3:
            copy.start()
        for unit, source in zip(ff[0], (sum1u, sum1d)):
            unit.start_x(source)
        for unit, source in zip(ff[1], (sum2u, sum2d)):
            unit.start_x(source)
        y_home.start()

    def slot_end(i):
        pair_c[i].start()
        if i == 0:
            load_w.wait()
            wo_c.wait_recv()
            accumulate(rcw, kw)
            wo_y.start()
            for copy in loads:
                copy.wait()
        if i == 1:
            ff_z(0)
            send_other(0)
        if i == 2:
            each(ff[0], "start_z2")
            ff_z(1)
            send_other(1)
            for unit, copy, held, own in zip(ff[2], y3, kept[2], (k3u, k3d)):
                copy.wait_recv()
                accumulate(held, own)
                unit.start_x(held)
        if i == 3:
            each(ff[0], "start_back")
            each(ff[1], "start_z2")
            send_other(2)
            y_away.start()
            wo_y.wait_recv()
            accumulate(ryw, rcw.at[:, 0:heads_half])
            wo.start_x(ryw)
        if i == 4:
            each(ff[0], "start_back1")
            each(ff[1], "start_back")
            ff_z(2)
            join_own(0)
            wo.start_z(ryw)
        if i == 5:
            each(ff[0], "start_back_x")
            each(ff[1], "start_back1")
            each(ff[2], "start_z2")
            join_own(1)
            wo.start_back()
            pairs[0].start_z(lambda: ryp.at[0])

    @pl.when(step == 0)
    def _():
        slot_start()
        kht[64:160, :] = back_ref[...]
        lanes = lax.broadcasted_iota(jnp.int32, (tokens, 64), 1)
        vx[:, 64:128] = jnp.where(lanes < 2, -1.0, 0.0).astype(BF)
        dox[64:128, :] = jnp.zeros((64, tokens), BF)
        x = x_ref[...].astype(F32)
        inverse = lax.rsqrt(jnp.mean(x * x, axis=-1, keepdims=True) + EPS)
        n1t[...] = (x * inverse * gain_ref[...]).astype(BF).T
        dn[...] = jnp.zeros_like(dn)
        gtab[...] = jnp.zeros_like(gtab)

    side = lax.broadcasted_iota(jnp.int32, (buckets, 128), 1)
    first_row = jnp.where(step < 3, 8 + 2 * step, 2 * (step - 3))
    dqs, dks, dvs = [], [], []
    for h in range(2):
        span = slice(64 * h, 64 * h + 64)
        scaled = dot_ref[span, :].astype(F32) * r_ref[0, h : h + 1, :]
        inner = jnp.sum(scaled * ot_ref[span, :].astype(F32), axis=0, keepdims=True)
        upper = inner.astype(BF)
        lower = (inner - upper.astype(F32)).astype(BF)
        dox[0:64, :] = scaled.astype(BF)
        dox[64:66, :] = jnp.concatenate([upper, lower], 0)
        vx[:, 0:64] = v_ref[:, span]
        kht[0:64, :] = k_ref[:, span].T
        dp = dg(vx[...], dox[...], 1, 0)
        p = p_ref[h]
        ds = (p.astype(F32) * dp).astype(BF)
        dvs.append(dg(p, dox[0:64, :], 1, 1).astype(BF))
        dks.append((dg(ds, qt_ref[span, :], 1, 1) * 0.125).astype(BF))
        both = dg(kht[...], ds, 1, 0)
        dqs.append((both[0:64] * 0.125).astype(BF).T)
        left = both[64:160]
        left_hi = left.astype(BF)
        left_lo = (left - left_hi.astype(F32)).astype(BF)
        hot = hot_ref[...]
        blocks = dg(left_hi, hot, 1, 0) + dg(left_lo, hot, 1, 0)
        for t in range(3):
            inside = (side >= t * buckets) & (side < (t + 1) * buckets)
            block = jnp.where(inside, blocks[t * buckets : (t + 1) * buckets], 0.0)
            rolled = pltpu.roll(block, (129 - (t + 1) * buckets) % 128, 1, stride=1, stride_axis=0)
            gtab[t, pl.ds(first_row + h, 1), :] = jnp.sum(rolled, axis=0, keepdims=True)
    grads = jnp.concatenate(dqs + dks + dvs, axis=1)
    weights = jnp.concatenate([wq_ref[...], wk_ref[...], wv_ref[...]], axis=1)
    dn[...] += dg(grads, weights, 1, 1)
    gp[step] = dg(n1t[...], grads, 1, 0).astype(BF)
    for i in range(6):
        pl.when(step == i)(functools.partial(slot_end, i))

    @pl.when(step == pl.num_programs(0) - 1)
    def _():
        x = x_ref[...].astype(F32)
        inverse = lax.rsqrt(jnp.mean(x * x, axis=-1, keepdims=True) + EPS)
        normed = x * inverse
        total = dn[...]
        grad_gain = jnp.sum(total * normed, axis=0, keepdims=True)
        inner = total * gain_ref[...]
        added = inverse * (inner - normed * jnp.mean(inner * normed, axis=-1, keepdims=True))
        gin[...] = (dh_ref[...] + added).astype(BF)
        lines = width // 128
        for j in range(lines):
            lane = slice(j * 128, (j + 1) * 128)
            sums[0, j : j + 1, :] = grad_gain[:, lane]
            sums[0, lines + j : lines + j + 1, :] = ggf_ref[:, lane]
        sums[0, 2 * lines : 16, :] = jnp.zeros((16 - 2 * lines, 128), F32)
        line = lax.broadcasted_iota(jnp.int32, (128, 128), 0)
        lane = lax.broadcasted_iota(jnp.int32, (128, 128), 1)
        shift = jnp.where(lane < 64, lane, lane - 128)
        bucket = jnp.clip(-shift, -(buckets // 2), buckets // 2 - 1) + buckets // 2
        table = jnp.zeros((16, 128), F32)
        for t in range(3):
            pick = jnp.where(line == bucket + t * buckets, 1.0, 0.0)
            table = table + lax.dot_general(
                gtab[t], pick, (((1,), (1,)), ((), ())),
                precision=lax.Precision.HIGHEST, preferred_element_type=F32,
            )
        sums[0, 16:32, :] = table
        hops = bits + 1
        hop = None
        count = 0

        def small_hop():
            nonlocal hop, count
            if hop is not None:
                hop.wait_recv()
                k = count
                if k == 1:
                    sums[1, 0:16] = sums[0, 0:16] + got[0, 0:16]
                    sums[1, 16:24] = sums[0, 16:24] + got[0, 24:32]
                    sums[1, 24:32] = jnp.zeros((8, 128), F32)
                else:
                    sums[k] = sums[k - 1] + got[k - 1]
                hop = None
            if count < hops:
                flips = dict(mp_flip=1) if count == 0 else dict(dp_flip=1 << (count - 1))
                k = count
                hop = links.remote(lambda: sums.at[k], lambda: got.at[k], **flips)
                hop.start()
                started.append(hop)
                count += 1

        started = []
        small_hop()
        gin_away.start()
        gin_home.start()
        join_own(2)
        each(ff[0], "start_back_c")
        each(ff[1], "start_back_x")
        each(ff[2], "start_back")
        wo.start_back_x()
        pairs[1].start_z(lambda: ryp.at[1])
        pairs[0].start_back()
        small_hop()
        pairs[2].start_z(lambda: ryp.at[2])
        pairs[0].start_back_x()
        each(ff[1], "start_back_c")
        each(ff[2], "start_back1")
        pairs[1].start_back()
        wo.start_back_c()
        small_hop()
        pairs[2].start_back()
        each(ff[2], "start_back_x")
        pairs[1].start_back_x()
        pairs[0].start_back_c()
        small_hop()
        pairs[2].start_back_x()
        each(ff[2], "start_back_c")
        pairs[1].start_back_c()
        small_hop()
        pairs[2].start_back_c()
        while count < hops or hop is not None:
            small_hop()
        small[...] = sums[hops]
        y_away.wait_recv()
        gin_away.wait_recv()
        for unit in units:
            unit.end()
        for copy in [y_away, gin_away, wo_c, wo_y] + y3 + pair_c + pair_y + started:
            copy.wait_send()
        y_home.wait()
        gin_home.wait()


def backward(p, qt, kv, ot, dot, r, back, hot, x, gain, dh, ggf, wqkv, parts, gwo, y, n_dp, buckets):
    channels, tokens = qt.shape
    width = x.shape[1]
    n_pairs = channels // 128
    half = n_pairs // 2
    chunk = parts[0].shape[1]
    group = 3 * 128
    once = lambda shape: pl.BlockSpec(
        shape, lambda i: (0,) * len(shape), pipeline_mode=pl.Buffered(1)
    )
    pick = lambda i: lax.rem(i + half, n_pairs)
    side = lambda i: pick(i) // half
    place = lambda i: lax.rem(pick(i), half)
    turned = pl.BlockSpec((128, tokens), lambda i: (pick(i), 0))
    column = lambda rows, j, n: pl.BlockSpec(
        (rows, 128), lambda i: (0, side(i) * n * half + j * half + place(i))
    )
    shapes = []
    for k in range(3):
        shapes += [(width, chunk, True), (chunk, width, True)]
    shapes += [(width, group, False)] * 4
    units, far = [], []
    for n, w, deepest in shapes:
        units += [
            pltpu.VMEM((n // 4, w), BF),
            pltpu.VMEM((n // 16, w), BF),
            pltpu.VMEM((n // 8, w) if deepest else (3, n // 16, w), BF),
            pltpu.VMEM((n // 16, w), BF),
        ]
        far.append(pltpu.VMEM((max(n_dp // 16, 1), n // 16, w), BF))
    bits = n_dp.bit_length() - 1
    part_u, part_d = parts[0].shape, parts[1].shape
    copies = 160 + (10 * (n_dp // 16) if n_dp > 16 else 0)
    scratch = [
        pltpu.VMEM((tokens, 128), BF),
        pltpu.VMEM((128, tokens), BF),
        pltpu.VMEM((160, tokens), BF),
        pltpu.VMEM((width, tokens), BF),
        pltpu.VMEM((tokens, width), F32),
        pltpu.VMEM((3, 16, 128), F32),
        pltpu.VMEM((6, width, group), BF),
        pltpu.VMEM((6, width // 2, group), BF),
        pltpu.VMEM((3, width // 2, group), BF),
        pltpu.VMEM((tokens, width), BF),
        pltpu.VMEM(part_u, BF),
        pltpu.VMEM(part_d, BF),
        pltpu.VMEM(part_u, BF),
        pltpu.VMEM(part_d, BF),
        pltpu.VMEM(part_u, BF),
        pltpu.VMEM(part_d, BF),
        pltpu.VMEM(part_u, BF),
        pltpu.VMEM(part_d, BF),
        pltpu.VMEM((width // 2, width), BF),
        pltpu.VMEM((width // 2, width), BF),
        pltpu.VMEM((width // 2, width // 2), BF),
        pltpu.VMEM((bits + 2, 32, 128), F32),
        pltpu.VMEM((bits + 2, 32, 128), F32),
    ]
    scratch += units
    if n_dp > 16:
        scratch += far
    scratch += [pltpu.SemaphoreType.DMA((copies,))] * 2
    return pl.pallas_call(
        functools.partial(back_kernel, n_dp=n_dp, buckets=buckets),
        grid=(n_pairs,),
        in_specs=[
            pl.BlockSpec((2, tokens, tokens), lambda i: (pick(i), 0, 0)),
            turned,
            column(tokens, 0, 2),
            column(tokens, 1, 2),
            turned,
            turned,
            pl.BlockSpec((1, 2, tokens), lambda i: (pick(i), 0, 0)),
            once((96, tokens)),
            once((tokens, 128)),
            once((tokens, width)),
            once((1, width)),
            once((tokens, width)),
            once((1, width)),
            column(width, 0, 3),
            column(width, 1, 3),
            column(width, 2, 3),
        ]
        + [ANY] * 10,
        out_specs=[ANY] * 6 + [once((32, 128))],
        out_shape=[
            SHAPE((2, tokens // 2, width), BF),
            SHAPE((2, tokens // 2, width), BF),
            SHAPE((3, width, group), BF),
            SHAPE((width, group), BF),
            SHAPE((width, 3 * chunk), BF),
            SHAPE((3 * chunk, width), BF),
            SHAPE((32, 128), F32),
        ],
        scratch_shapes=scratch,
        compiler_params=params(60, collective_id=5, has_side_effects=True),
        name="backward",
    )(p, qt, kv, kv, ot, dot, r, back, hot, x, gain, dh, ggf, wqkv, wqkv, wqkv, *parts, gwo, y)


def local(
    n_dp, inputs, roi, cotangent, doc_lengths, live_mask, bucket_cells,
    gain_attn, gain_ffn, w_query, w_key, w_value, w_out, w_up, w_down, tables,
):
    rows, width = inputs.shape[1], inputs.shape[2]
    tokens = 2 * rows
    third = w_query.shape[1]
    heads = third // HDIM
    buckets = tables.shape[1]
    tab = jnp.pad(
        tables.transpose(2, 0, 1).reshape(heads, 3 * buckets), ((0, 2), (0, 128 - 3 * buckets))
    )
    ga, gf = gain_attn.reshape(1, width), gain_ffn.reshape(1, width)
    x, tabo, wqkv, qt, kv, upo = entry(
        inputs, roi, tab, ga, w_query, w_key, w_value, w_up
    )
    p, mixt, r, hot, back, dyo, woo, upo, dno = attend(
        doc_lengths, live_mask.reshape(2, 1, tokens), bucket_cells, tab, tabo, qt, kv,
        cotangent, w_out, w_up, w_down, upo, buckets,
    )
    y, gwo, dh, dmt, gain_f, *parts = middle(
        x, mixt, w_out, woo, cotangent, dyo, gf, w_up, upo, w_down, dno
    )
    yret, gret, fqkv, fwo, fup, fdn, small = backward(
        p, qt, kv, mixt, dmt, r, back, hot, x, ga, dh, gain_f, wqkv, parts, gwo, y, n_dp, buckets
    )
    lines = width // 128
    out = inputs.astype(F32) + roi.astype(F32) + yret.astype(F32)
    grad_in = cotangent.astype(F32) + gret.astype(F32)
    table_out = small[16 : 16 + heads, : 3 * buckets].reshape(heads, 3, buckets).transpose(1, 2, 0)
    gq, gk, gv = (
        jnp.concatenate([fqkv[k, :, j * 128 : (j + 1) * 128] for k in range(3)], axis=1).astype(F32)
        for j in range(3)
    )
    return (
        out,
        grad_in,
        small[0:lines].reshape(width),
        small[lines : 2 * lines].reshape(width),
        gq,
        gk,
        gv,
        fwo.T.astype(F32),
        fup.astype(F32),
        fdn.astype(F32),
        table_out,
    )


def solution(mesh):
    n_dp = mesh.shape["dp"]
    rows = P(None, ("dp", "mp"), None)
    columns, lines = P(None, "mp"), P("mp", None)
    tables = P(None, None, "mp")
    return jax.shard_map(
        functools.partial(local, n_dp),
        mesh=mesh,
        in_specs=(
            rows, rows, rows, P(None, "dp", None), P(None, "dp"), P(None, None, "dp"),
            P(), P(), columns, columns, columns, lines, columns, lines, tables,
        ),
        out_specs=(
            rows, rows, P(), P(), columns, columns, columns, lines, columns, lines, tables,
        ),
        check_vma=False,
    )
```

```python
import functools
import math

import jax
import jax.numpy as jnp
from jax import lax
from jax.experimental import pallas as pl
from jax.experimental.pallas import tpu as pltpu
from jax.sharding import PartitionSpec as P

BF = jnp.bfloat16
F32 = jnp.float32
HDIM = 64
EPS = 1e-06
MASKED = -1e30
MESH = pl.DeviceIdType.MESH
VMEM = pl.BlockSpec(memory_space=pltpu.VMEM)
ANY = pl.BlockSpec(memory_space=pltpu.HBM)
SHAPE = jax.ShapeDtypeStruct


def dg(a, b, ca, cb):
    return lax.dot_general(a, b, (((ca,), (cb,)), ((), ())), preferred_element_type=F32)


def params(limit=58, **more):
    return pltpu.CompilerParams(vmem_limit_bytes=limit << 20, **more)


class Copy:
    def __init__(self, make):
        self.make = make

    def start(self):
        self.make().start()

    def wait(self):
        self.make().wait()

    def wait_recv(self):
        self.make().wait_recv()

    def wait_send(self):
        self.make().wait_send()


def now(ref):
    return ref() if callable(ref) else ref


class Links:
    def __init__(self, send, recv):
        self.send, self.recv, self.count = send, recv, 0
        self.d, self.m = lax.axis_index("dp"), lax.axis_index("mp")

    def flipped(self, dp_flip, mp_flip):
        dp = self.d ^ dp_flip if dp_flip else self.d
        mp = self.m ^ mp_flip if mp_flip else self.m
        return dp, mp

    def remote(self, src, dst, dp_flip=0, mp_flip=0):
        i = self.count
        self.count += 1
        return Copy(
            lambda: pltpu.make_async_remote_copy(
                src_ref=now(src),
                dst_ref=now(dst),
                send_sem=self.send.at[i],
                recv_sem=self.recv.at[i],
                device_id=self.flipped(dp_flip, mp_flip),
                device_id_type=MESH,
            )
        )

    def local(self, src, dst):
        i = self.count
        self.count += 1
        return Copy(lambda: pltpu.make_async_copy(now(src), now(dst), self.send.at[i]))

    def barrier(self, flips):
        sem = pltpu.get_barrier_semaphore()
        for flip in flips:
            pl.semaphore_signal(
                sem, inc=1, device_id=self.flipped(*flip), device_id_type=MESH
            )
        pl.semaphore_wait(sem, len(flips))


def rows_at(start, size, unit):
    return pl.ds(pl.multiple_of(start, unit), size)


def accumulate(into, other, start=0):
    n = into.shape[0]
    unit = 48 if n % 48 == 0 else 32

    def body(i, carry):
        here = rows_at(i * unit, unit, 16)
        there = rows_at(start + i * unit, unit, 16)
        into[here] = (into[here].astype(F32) + other[there].astype(F32)).astype(BF)
        return carry

    lax.fori_loop(0, n // unit, body, 0)


def carry_over(into, source, start=0):
    n = into.shape[0]
    unit = 48 if n % 48 == 0 else 32

    def body(i, carry):
        into[rows_at(i * unit, unit, 16)] = source[rows_at(start + i * unit, unit, 16)]
        return carry

    lax.fori_loop(0, n // unit, body, 0)


def entry_kernel(
    inp, roi, tab, gains, wq, wk, wv, wup,
    xf, tabo, wqkv, qt, kv, upo,
    sent, n1, send, recv,
):
    links = Links(send, recv)
    d, m = links.d, links.m
    rows = inp.shape[1]
    width, third = wq.shape
    piece = width // 8
    core, cross, deep = d & 1, (d >> 1) & 1, (d >> 2) & 1
    place = core * 4 + cross * 2 + deep
    links.barrier(((0, 1), (1, 0), (2, 0), (4, 0)))
    started = []

    def go(copy):
        copy.start()
        started.append(copy)
        return copy

    own_cols = [slice(j * third, (j + 1) * third) for j in range(3)]
    other_cols = [slice((3 + j) * third, (4 + j) * third) for j in range(3)]
    spot = rows_at(place * piece, piece, piece)
    first = [
        go(links.remote(w.at[spot], wqkv.at[spot, c], mp_flip=1))
        for w, c in zip((wq, wk, wv), other_cols)
    ]
    tab_copy = go(links.remote(tab, tabo, mp_flip=1))
    chunk = rows // 2
    row_copies = []
    for j in range(2):
        part = slice(j * chunk, (j + 1) * chunk)
        sent[part] = (inp[1 - m, part].astype(F32) + roi[1 - m, part].astype(F32)).astype(BF)
        here = rows_at(m * rows + j * chunk, chunk, chunk)
        row_copies.append(go(links.remote(sent.at[part], xf.at[here], mp_flip=1)))
    up_copy = go(links.remote(wup.at[spot], upo.at[spot], mp_flip=1))
    for w, c in zip((wq, wk, wv), own_cols):
        wqkv[:, c] = w[...]

    def normalise(where):
        x = xf[where].astype(F32)
        inverse = lax.rsqrt(jnp.mean(x * x, axis=-1, keepdims=True) + EPS)
        n1[where] = (x * inverse * gains[0:1]).astype(BF)

    own = rows_at(m * rows, rows, rows)
    xf[own] = (inp[m].astype(F32) + roi[m].astype(F32)).astype(BF)
    normalise(own)

    def project(where, side):
        rows_in = n1[where]
        base = side * 3 * third
        kv[where, side * 2 * third : (side + 1) * 2 * third] = dg(
            rows_in, wqkv[:, base + third : base + 3 * third], 1, 0
        ).astype(BF)
        qt[side * third : (side + 1) * third, where] = dg(
            wqkv[:, base : base + third], rows_in, 0, 1
        ).astype(BF)

    project(own, 0)
    stage = first
    for flip, begin, count in (
        (4, place, 1),
        (2, core * 4 + cross * 2, 2),
        (1, core * 4, 4),
    ):
        for copy in stage:
            copy.wait_recv()
        there = wqkv.at[rows_at(begin * piece, count * piece, piece), 3 * third : 6 * third]
        stage = [go(links.remote(there, there, dp_flip=flip))]
    for j in range(2):
        row_copies[j].wait_recv()
        here = rows_at((1 - m) * rows + j * chunk, chunk, chunk)
        normalise(here)
        project(here, 0)
    for copy in stage:
        copy.wait_recv()
    for j in range(2):
        project(slice(j * rows, (j + 1) * rows), 1)
    tab_copy.wait_recv()
    up_copy.wait_recv()
    for copy in started:
        copy.wait_send()


def entry(inputs, roi, tab, gain, wq, wk, wv, wup):
    rows, width = inputs.shape[1], inputs.shape[2]
    third = wq.shape[1]
    tokens = 2 * rows
    return pl.pallas_call(
        entry_kernel,
        out_shape=[
            SHAPE((tokens, width), BF),
            SHAPE(tab.shape, F32),
            SHAPE((width, 6 * third), BF),
            SHAPE((2 * third, tokens), BF),
            SHAPE((tokens, 4 * third), BF),
            SHAPE(wup.shape, BF),
        ],
        in_specs=[VMEM] * 7 + [ANY],
        out_specs=[VMEM] * 5 + [ANY],
        scratch_shapes=[
            pltpu.VMEM((rows, width), BF),
            pltpu.VMEM((tokens, width), BF),
            pltpu.SemaphoreType.DMA((12,)),
            pltpu.SemaphoreType.DMA((12,)),
        ],
        compiler_params=params(58, collective_id=1, has_side_effects=True),
        name="entry",
    )(inputs, roi, tab, gain, wq, wk, wv, wup)


def attend_kernel(
    lengths, marks, tab, tabo, qt_ref, k_ref, v_ref, cot, wo, wup, wdn, upo_in,
    p_ref, o_ref, r_ref, hot_ref, back_ref, dyo, woo, upo, dno,
    kx, qx, vx, mask, mats, hott_ref, send, recv, *, buckets,
):
    links = Links(send, recv)
    d, m = links.d, links.m
    tokens = k_ref.shape[0]
    rows = tokens // 2
    width, hidden = wup.shape
    inner = wo.shape[0]
    step = pl.program_id(0)
    core, cross, deep = d & 1, (d >> 1) & 1, (d >> 2) & 1
    place = core * 4 + cross * 2 + deep

    def block(full, begin, count):
        piece = full.shape[0] // 8
        return full.at[rows_at(begin * piece, count * piece, piece)]

    up = functools.partial(block, upo)
    down = functools.partial(block, dno)
    out = functools.partial(block, woo)
    dpiece, opiece = hidden // 8, inner // 8
    quarter = core * 4 + deep * 2
    down_y = [
        links.remote(
            wdn.at[rows_at((quarter + j) * dpiece, dpiece, dpiece)], down(quarter + j, 1), mp_flip=1
        )
        for j in range(2)
    ]
    out_y = links.remote(wo.at[rows_at(place * opiece, opiece, opiece)], out(place, 1), mp_flip=1)
    dy_y = links.remote(cot.at[1 - m], dyo, mp_flip=1)
    up_z = links.remote(up(place, 1), up(place, 1), dp_flip=4)
    pair = core * 4 + cross * 2
    up_x = links.remote(up(pair, 2), up(pair, 2), dp_flip=2)
    up_c = links.remote(up(core * 4, 4), up(core * 4, 4), dp_flip=1)
    down_z = [
        links.remote(down(quarter + j, 1), down(quarter + j, 1), dp_flip=4) for j in range(2)
    ]
    down_c = links.remote(down(core * 4, 4), down(core * 4, 4), dp_flip=1)
    out_z = links.remote(out(place, 1), out(place, 1), dp_flip=4)
    out_x = links.remote(out(pair, 2), out(pair, 2), dp_flip=2)
    out_c = links.remote(out(core * 4, 4), out(core * 4, 4), dp_flip=1)

    def slot0():
        links.barrier(((0, 1), (1, 0), (2, 0), (4, 0)))
        up_z.start()
        down_y[0].start()
        out_y.start()

    def slot4():
        up_z.wait_recv()
        up_x.start()

    def slot2():
        down_y[1].start()

    def slot5():
        down_y[0].wait_recv()
        down_z[0].start()

    def slot6():
        dy_y.start()
        out_y.wait_recv()
        out_z.start()

    def slot7():
        down_y[1].wait_recv()
        down_z[1].start()

    def slot9():
        out_z.wait_recv()
        out_x.start()

    def slot11():
        up_x.wait_recv()
        up_c.start()
        out_x.wait_recv()
        out_c.start()

    def last():
        down_z[0].wait_recv()
        down_z[1].wait_recv()
        down_c.start()
        for copy in (dy_y, up_c, out_c, down_c):
            copy.wait_recv()
        for copy in (*down_y, out_y, dy_y, up_z, up_x, up_c, *down_z, down_c, out_z, out_x, out_c):
            copy.wait_send()

    slots = {0: slot0, 1: slot2, 4: slot4, 5: slot5, 6: slot6, 7: slot7, 9: slot9, 11: slot11}

    @pl.when(step == 0)
    def _():
        slot0()
        vx[64:80, :] = jnp.ones((16, tokens), BF)
        lane = lax.broadcasted_iota(jnp.int32, (buckets, tokens), 0)
        for t in range(3):
            row = marks[m, t + 1 : t + 2, :]
            hott_ref[t * buckets : (t + 1) * buckets, :] = jnp.where(row == lane, 1.0, 0.0).astype(BF)
            mirror = jnp.where(row == buckets - 1 - lane, 1.0, 0.0).astype(BF)
            back_ref[t * buckets : (t + 1) * buckets, :] = mirror
        hott_ref[96:128, :] = jnp.zeros((32, tokens), BF)
        wide_hot = hott_ref[...].T
        hot_ref[...] = wide_hot
        hot = wide_hot[:, 0:96]
        kx[:, 64:160] = hot
        kx[:, 160:256] = hot
        row_ids = lax.broadcasted_iota(jnp.int32, (1, tokens), 1)
        col_ids = lax.broadcasted_iota(jnp.int32, (tokens, 1), 0)
        seg_row = jnp.zeros((1, tokens), jnp.int32)
        seg_col = jnp.zeros((tokens, 1), jnp.int32)
        end = 0
        for i in range(lengths.shape[2]):
            end = end + lengths[m, 0, i]
            seg_row = seg_row + jnp.where(row_ids >= end, 1, 0)
            seg_col = seg_col + jnp.where(col_ids >= end, 1, 0)
        live_row = marks[m, 0:1, :].astype(F32)
        live_col = jnp.broadcast_to(live_row, (8, tokens)).T[:, 0:1]
        code = jnp.where(live_col == 1.0, seg_col, -1)
        allowed = (code == seg_row) | (col_ids == row_ids)
        mask[...] = jnp.where(allowed, 0.0, MASKED)
        line = lax.broadcasted_iota(jnp.int32, (128, 128), 0)
        lane = lax.broadcasted_iota(jnp.int32, (128, 128), 1)
        shift = jnp.where(lane < 64, lane, lane - 128)
        bucket = jnp.clip(-shift, -(buckets // 2), buckets // 2 - 1) + buckets // 2
        side = lax.broadcasted_iota(jnp.int32, (buckets, 128), 1)
        heads = mats.shape[0] // 2
        for part, table in enumerate((tab, tabo)):
            exact = table[...]
            upper = exact.astype(BF)
            lower = (exact - upper.astype(F32)).astype(BF)
            for t in range(3):
                pick = jnp.where(line == bucket + t * buckets, 1.0, 0.0).astype(BF)
                inside = (side >= t * buckets) & (side < (t + 1) * buckets)
                for level, source in enumerate((upper, lower)):
                    lines = dg(source, pick, 1, 0)
                    for h in range(heads):
                        wide = jnp.broadcast_to(lines[h : h + 1], (buckets, 128))
                        rolled = pltpu.roll(wide, t * buckets, 1, stride=1, stride_axis=0)
                        begin = level * 3 * buckets + t * buckets
                        mats[part * heads + h, begin : begin + buckets, :] = jnp.where(
                            inside, rolled, 0.0
                        ).astype(BF)

    vt = v_ref[...].T
    for h in range(2):
        for at, action in slots.items():
            if at % 2 == h and at > 0:
                pl.when(step == at // 2)(action)
        span = slice(64 * h, 64 * h + 64)
        kx[:, 0:64] = k_ref[:, span]
        qx[0:64, :] = qt_ref[span, :] * BF(0.125)
        qx[64:256, :] = dg(mats[2 * step + h], hott_ref[...], 1, 0).astype(BF)
        vx[0:64, :] = vt[span, :]
        s = dg(kx[...], qx[...], 1, 0) + mask[...]
        top = jnp.max(s, axis=0, keepdims=True)
        p = jnp.exp(s - top).astype(BF)
        p_ref[h] = p
        o = dg(vx[...], p, 1, 0)
        r = 1.0 / o[64:65, :]
        o_ref[span, :] = (o[0:64] * r).astype(BF)
        r_ref[0, h : h + 1, :] = r
    pl.when(step == pl.num_programs(0) - 1)(last)


def attend(lengths, marks, tab, tabo, qt, kv, cot, wo, wup, wdn, upo, buckets):
    channels, tokens = qt.shape
    width, hidden = wup.shape
    inner = wo.shape[0]
    pairs = channels // 128
    half = pairs // 2
    whole = lambda shape: pl.BlockSpec(shape, lambda i: (0,) * len(shape))
    return pl.pallas_call(
        functools.partial(attend_kernel, buckets=buckets),
        grid=(pairs,),
        in_specs=[
            pl.BlockSpec(memory_space=pltpu.SMEM),
            whole(marks.shape),
            whole(tab.shape),
            whole(tabo.shape),
            pl.BlockSpec((128, tokens), lambda i: (i, 0)),
            pl.BlockSpec((tokens, 128), lambda i: (0, (i // half) * 2 * half + i % half)),
            pl.BlockSpec((tokens, 128), lambda i: (0, (i // half) * 2 * half + half + i % half)),
            ANY, ANY, ANY, ANY, ANY,
        ],
        out_specs=[
            pl.BlockSpec((2, tokens, tokens), lambda i: (i, 0, 0)),
            pl.BlockSpec((128, tokens), lambda i: (i, 0)),
            pl.BlockSpec((1, 2, tokens), lambda i: (i, 0, 0)),
            whole((tokens, 128)),
            whole((96, tokens)),
            ANY, ANY, ANY, ANY,
        ],
        out_shape=[
            SHAPE((2 * pairs, tokens, tokens), BF),
            SHAPE((channels, tokens), BF),
            SHAPE((pairs, 2, tokens), F32),
            SHAPE((tokens, 128), BF),
            SHAPE((96, tokens), BF),
            SHAPE((tokens // 2, width), BF),
            SHAPE((inner, width), BF),
            SHAPE((width, hidden), BF),
            SHAPE((hidden, width), BF),
        ],
        input_output_aliases={11: 7},
        scratch_shapes=[
            pltpu.VMEM((tokens, 256), BF),
            pltpu.VMEM((256, tokens), BF),
            pltpu.VMEM((80, tokens), BF),
            pltpu.VMEM((tokens, tokens), F32),
            pltpu.VMEM((2 * pairs, 192, 128), BF),
            pltpu.VMEM((128, tokens), BF),
            pltpu.SemaphoreType.DMA((20,)),
            pltpu.SemaphoreType.DMA((20,)),
        ],
        compiler_params=params(58, collective_id=3, has_side_effects=True),
        name="attend",
    )(lengths, marks, tab, tabo, qt, kv, kv, cot, wo, wup, wdn, upo)


def middle_kernel(
    x_ref, mixt_ref, wo_in, woo_in, cot, dyo, gains, wup_in, upo_in, wdn_in, dno_in,
    y_ref, gwo_ref, dh_ref, dmt_ref, gg_ref,
    sum1u, sum1d, sum2u, sum2d, own3u, own3d, far3u, far3d,
    h1, n2, n2t, yacc, dn, wo_ref, dy_ref, gu, gd, rcu, rcd, ryu, ryd, send, recv,
):
    links = Links(send, recv)
    core = links.d & 1
    step = pl.program_id(0)
    last = pl.num_programs(0) - 1
    half_steps = pl.num_programs(0) // 2
    early = step < half_steps
    width, chunk = gu.shape[1:]
    keep_u, give_u = (rows_at(c * (width // 2), width // 2, 16) for c in (core, 1 - core))
    keep_d, give_d = (rows_at(c * (chunk // 2), chunk // 2, 16) for c in (core, 1 - core))

    def core_copies(i):
        return (
            pltpu.make_async_remote_copy(
                gu.at[i % 2, give_u], rcu.at[i], send.at[0, i], recv.at[0, i],
                device_id=(links.d ^ 1, links.m), device_id_type=MESH,
            ),
            pltpu.make_async_remote_copy(
                gd.at[i % 2, give_d], rcd.at[i], send.at[1, i], recv.at[1, i],
                device_id=(links.d ^ 1, links.m), device_id_type=MESH,
            ),
        )

    def pair_copies(i):
        return (
            pltpu.make_async_remote_copy(
                rcu.at[i], ryu.at[i], send.at[2, i], recv.at[2, i],
                device_id=(links.d, 1 - links.m), device_id_type=MESH,
            ),
            pltpu.make_async_remote_copy(
                rcd.at[i], ryd.at[i], send.at[3, i], recv.at[3, i],
                device_id=(links.d, 1 - links.m), device_id_type=MESH,
            ),
        )

    def settle(i):
        for copy in core_copies(i):
            copy.wait_recv()
        for copy in core_copies(i):
            copy.wait_send()
        accumulate(rcu.at[i], gu.at[i % 2], core * (width // 2))
        accumulate(rcd.at[i], gd.at[i % 2], core * (chunk // 2))

    @pl.when(step == 0)
    def _():
        links.barrier(((0, 1), (1, 0)))
        m = links.m
        rows = dyo.shape[0]
        dy_ref[rows_at(m * rows, rows, rows)] = cot[m]
        dy_ref[rows_at((1 - m) * rows, rows, rows)] = dyo[...]
        inner = wo_in.shape[0]
        wo_ref[0:inner] = wo_in[...]
        wo_ref[inner:] = woo_in[...]
        added = dg(mixt_ref[...], wo_ref[...], 0, 0)
        h = x_ref[...].astype(F32) + added
        h1[...] = h
        yacc[...] = added
        inverse = lax.rsqrt(jnp.mean(h * h, axis=-1, keepdims=True) + EPS)
        normed = (h * inverse * gains[1:2]).astype(BF)
        n2[...] = normed
        n2t[...] = normed.T
        dn[...] = jnp.zeros_like(dn)

    wup = jnp.where(early, upo_in[...], wup_in[...])
    wdn = jnp.where(early, dno_in[...], wdn_in[...])
    dy = dy_ref[...]
    u = dg(n2[...], wup, 1, 0)
    cdf = 0.5 * (1.0 + lax.erf(u * 0.7071067811865476))
    act = (u * cdf).astype(BF)
    grad_act = dg(dy, wdn, 1, 1)
    density = jnp.exp(u * u * (-0.5)) * 0.3989422804014327
    du = (grad_act * (cdf + u * density)).astype(BF)
    yacc[...] += dg(act, wdn, 1, 0)

    @pl.when(step > 0)
    def _():
        settle(step - 1)

    @pl.when((step > 0) & (step < half_steps))
    def _():
        for copy in pair_copies(step - 1):
            copy.start()

    dn[...] += dg(du, wup, 1, 1)
    gu[step % 2] = dg(n2t[...], du, 1, 0).astype(BF)
    gd[step % 2] = dg(act, dy, 0, 0).astype(BF)
    for copy in core_copies(step):
        copy.start()

    @pl.when(step == last)
    def _():
        h = h1[...]
        inverse = lax.rsqrt(jnp.mean(h * h, axis=-1, keepdims=True) + EPS)
        normed = h * inverse
        grad = dn[...]
        gg_ref[...] = jnp.sum(grad * normed, axis=0, keepdims=True)
        inner = grad * gains[1:2]
        added = inverse * (inner - normed * jnp.mean(inner * normed, axis=-1, keepdims=True))
        dh_ref[...] = added
        y_ref[...] = yacc[...].astype(BF)
        low = (dy_ref[...].astype(F32) + added).astype(BF)
        gwo_ref[...] = dg(low, mixt_ref[...], 0, 1).astype(BF)
        dmt_ref[...] = dg(wo_ref[...], low, 1, 1).astype(BF)
        settle(last)
        n = rcu.shape[0] // 2
        for k, (out_u, out_d) in enumerate(((sum1u, sum1d), (sum2u, sum2d))):
            for copy in pair_copies(k):
                copy.wait_recv()
            accumulate(rcu.at[n + k], ryu.at[k])
            accumulate(rcd.at[n + k], ryd.at[k])
            carry_over(out_u, rcu.at[n + k])
            carry_over(out_d, rcd.at[n + k])
        carry_over(own3u, rcu.at[n + 2])
        carry_over(own3d, rcd.at[n + 2])
        carry_over(far3u, rcu.at[2])
        carry_over(far3d, rcd.at[2])
        for k in range(2):
            for copy in pair_copies(k):
                copy.wait_send()


def middle(x, mixt, wo, woo, cot, dyo, gain, wup, upo, wdn, dno):
    tokens, width = x.shape
    half = wup.shape[1]
    chunk = half // 3
    n = 6
    once = lambda shape: pl.BlockSpec(
        shape, lambda i: (0,) * len(shape), pipeline_mode=pl.Buffered(1)
    )
    late = lambda i: jnp.maximum(i - n // 2, 0)
    early = lambda i: jnp.minimum(i, n // 2 - 1)
    part_u, part_d = (width // 2, chunk), (chunk // 2, width)
    outs = [
        ((tokens, width), BF),
        ((width, width), BF),
        ((tokens, width), F32),
        ((width, tokens), BF),
        ((1, width), F32),
    ] + [(part_u, BF), (part_d, BF)] * 4
    return pl.pallas_call(
        middle_kernel,
        grid=(n,),
        in_specs=[
            once((tokens, width)),
            once((width, tokens)),
            once(wo.shape),
            once(woo.shape),
            once(cot.shape),
            once(dyo.shape),
            once((2, width)),
            pl.BlockSpec((width, chunk), lambda i: (0, late(i))),
            pl.BlockSpec((width, chunk), lambda i: (0, early(i))),
            pl.BlockSpec((chunk, width), lambda i: (late(i), 0)),
            pl.BlockSpec((chunk, width), lambda i: (early(i), 0)),
        ],
        out_specs=[once(shape) for shape, _ in outs],
        out_shape=[SHAPE(*entry) for entry in outs],
        scratch_shapes=[
            pltpu.VMEM((tokens, width), F32),
            pltpu.VMEM((tokens, width), BF),
            pltpu.VMEM((width, tokens), BF),
            pltpu.VMEM((tokens, width), F32),
            pltpu.VMEM((tokens, width), F32),
            pltpu.VMEM((width, width), BF),
            pltpu.VMEM((tokens, width), BF),
            pltpu.VMEM((2, width, chunk), BF),
            pltpu.VMEM((2, chunk, width), BF),
            pltpu.VMEM((n,) + part_u, BF),
            pltpu.VMEM((n,) + part_d, BF),
            pltpu.VMEM((2,) + part_u, BF),
            pltpu.VMEM((2,) + part_d, BF),
            pltpu.SemaphoreType.DMA((4, n)),
            pltpu.SemaphoreType.DMA((4, n)),
        ],
        compiler_params=params(60, collective_id=4, has_side_effects=True),
        name="middle",
    )(x, mixt, wo, woo, cot, dyo, gain, wup, upo, wdn, dno)


class Unit:
    def __init__(self, links, n, w, rx, rz, zp, final, far, n_dp, deepest):
        self.links, self.n, self.w = links, n, w
        self.rx, self.rz, self.zp, self.final, self.far = rx, rz, zp, final, far
        self.n_dp, self.stepwise = n_dp, deepest
        d = links.d
        self.core, self.cross = d & 1, (d >> 1) & 1
        self.b0, self.b1 = (d >> 2) & 1, (d >> 3) & 1
        q = n // 16
        self.q = q
        self.xr = links.remote(lambda: self.xr.make_source(), rx, dp_flip=2)
        spot = self.core * 8 + self.cross * 4 + self.b0 * 2 + self.b1
        self.piece = lambda: final(spot * q, q)
        self.home = links.local(zp, self.piece)
        if deepest:
            keep = self.b0 * 2
            give = (1 - self.b0) * 2
            self.z1 = links.remote(lambda: rx.at[rows_at(give * q, 2 * q, 16)], rz[0], dp_flip=4)
            self.z2 = links.remote(
                lambda: rz[0].at[rows_at((1 - self.b1) * q, q, 16)], rz[1], dp_flip=8
            )
            self.g2 = links.remote(zp, self.piece, dp_flip=8)
            both = lambda: final((self.core * 8 + self.cross * 4 + keep) * q, 2 * q)
            self.g1 = links.remote(both, both, dp_flip=4)
        else:
            self.zs, self.gs = [], []
            for r in range(1, 4):
                p0, p1 = self.b0 ^ (r & 1), self.b1 ^ (r >> 1)
                src = lambda p=p0 * 2 + p1: rx.at[rows_at(p * q, q, 16)]
                dst = lambda r=r: rz[0].at[r - 1]
                self.zs.append(links.remote(src, dst, dp_flip=r << 2))
                self.gs.append(links.remote(zp, self.piece, dp_flip=r << 2))
        quad = lambda: final((self.core * 8 + self.cross * 4) * q, 4 * q)
        self.gx = links.remote(quad, quad, dp_flip=2)
        side = lambda: final(self.core * 8 * q, 8 * q)
        self.gc = links.remote(side, side, dp_flip=1)
        if far is not None:
            self.others = [
                links.remote(lambda: far.at[0], lambda r=r: far.at[r], dp_flip=r << 4)
                for r in range(1, n_dp // 16)
            ]

    def start_x(self, source):
        half = self.n // 4
        self.xr.make_source = lambda: now(source).at[rows_at((1 - self.cross) * half, half, 16)]
        self.xr.start()

    def add_x(self, kept):
        half = self.n // 4
        self.xr.wait_recv()
        accumulate(self.rx, now(kept), self.cross * half)

    def start_z(self, kept):
        self.add_x(kept)
        for copy in [self.z1] if self.stepwise else self.zs:
            copy.start()

    def start_z2(self):
        self.z1.wait_recv()
        accumulate(self.rz[0], self.rx, self.b0 * 2 * self.q)
        self.z2.start()

    def start_back(self):
        q = self.q
        if self.stepwise:
            self.z2.wait_recv()
            total = self.rz[0][rows_at(self.b1 * q, q, 16)].astype(F32)
            total = total + self.rz[1][...].astype(F32)
        else:
            for copy in self.zs:
                copy.wait_recv()
            total = self.rx[rows_at((self.b0 * 2 + self.b1) * q, q, 16)].astype(F32)
            for r in range(3):
                total = total + self.rz[0][r].astype(F32)
        if self.far is not None:
            self.far[0] = total.astype(BF)
            for copy in self.others:
                copy.start()
            for r, copy in enumerate(self.others):
                copy.wait_recv()
                total = total + self.far[r + 1].astype(F32)
        self.zp[...] = total.astype(BF)
        self.home.start()
        for copy in [self.g2] if self.stepwise else self.gs:
            copy.start()

    def start_back1(self):
        self.home.wait()
        self.g2.wait_recv()
        self.g1.start()

    def start_back_x(self):
        if self.stepwise:
            self.g1.wait_recv()
        else:
            self.home.wait()
            for copy in self.gs:
                copy.wait_recv()
        self.gx.start()

    def start_back_c(self):
        self.gx.wait_recv()
        self.gc.start()

    def end(self):
        self.gc.wait_recv()
        sent = [self.xr, self.gx, self.gc]
        sent += [self.z1, self.z2, self.g2, self.g1] if self.stepwise else self.zs + self.gs
        if self.far is not None:
            sent += self.others
        for copy in sent:
            copy.wait_send()


def back_kernel(
    p_ref, qt_ref, k_ref, v_ref, ot_ref, dot_ref, r_ref, back_ref, hot_ref,
    x_ref, gains, dh_ref, ggf_ref, wq_ref, wk_ref, wv_ref,
    sum1u, sum1d, sum2u, sum2d, own3u, own3d, far3u, far3d, gwo, y,
    yret, gret, fqkv, fwo, fup, fdn, small,
    vx, dox, kht, n1t, dn, gtab, gp, rcp, ryp, gin,
    k1u, k1d, k2u, k2d, k3u, k3d, ry3u, ry3d, kw, rcw, ryw,
    sums, got, *rest, n_dp, buckets,
):
    units_scratch, rest = rest[: 4 * 10], rest[4 * 10 :]
    far = rest[:10] if n_dp > 16 else [None] * 10
    send, recv = rest[-2:]
    links = Links(send, recv)
    d, m = links.d, links.m
    core = d & 1
    step = pl.program_id(0)
    tokens, width = x_ref.shape
    rows = tokens // 2
    chunk = far3u.shape[1]
    group = gp.shape[2]
    bits = n_dp.bit_length() - 1

    def region(ref, row0, col0, w, lead=None):
        def at(start, count):
            where = rows_at(row0 + start, count, 16)
            if lead is not None:
                return ref.at[lead, where]
            return ref.at[where, col0 : col0 + w]

        return at

    finals = []
    for k in range(3):
        finals.append((width, chunk, region(fup, 0, k * chunk, chunk), True))
        finals.append((chunk, width, region(fdn, k * chunk, 0, width), True))
    finals.append((width, group, region(fwo, 0, 0, group), False))
    for k in range(3):
        finals.append((width, group, region(fqkv, 0, 0, group, lead=k), False))
    units = []
    for i, (n, w, final, deepest) in enumerate(finals):
        rx, zp = units_scratch[4 * i], units_scratch[4 * i + 1]
        rz = units_scratch[4 * i + 2 : 4 * i + 4]
        units.append(Unit(links, n, w, rx, rz, zp, final, far[i], n_dp, deepest))
    ff = (units[0:2], units[2:4], units[4:6])
    wo, pairs = units[6], units[7:10]
    kept = ((k1u, k1d), (k2u, k2d), (ry3u, ry3d))
    heads_half = width // 2

    mine = rows_at(m * rows, rows, rows)
    theirs = rows_at((1 - m) * rows, rows, rows)
    y_home = links.local(lambda: y.at[mine], lambda: yret.at[m])
    y_away = links.remote(lambda: y.at[theirs], lambda: yret.at[m], mp_flip=1)
    gin_home = links.local(lambda: gin.at[mine], lambda: gret.at[m])
    gin_away = links.remote(lambda: gin.at[theirs], lambda: gret.at[m], mp_flip=1)
    loads = [
        links.local(src, dst)
        for src, dst in ((sum1u, k1u), (sum1d, k1d), (sum2u, k2u), (sum2d, k2d), (own3u, k3u), (own3d, k3d))
    ]
    keep = rows_at(core * (width // 2), width // 2, 16)
    give = rows_at((1 - core) * (width // 2), width // 2, 16)
    load_w = links.local(lambda: gwo.at[keep], kw)
    y3 = [links.remote(far3u, ry3u, mp_flip=1), links.remote(far3d, ry3d, mp_flip=1)]
    wo_c = links.remote(lambda: gwo.at[give], rcw, dp_flip=1)
    wo_y = links.remote(lambda: rcw.at[:, heads_half:], ryw, mp_flip=1)
    pair_c = [
        links.remote(lambda i=i: gp.at[i, give], lambda i=i: rcp.at[i], dp_flip=1) for i in range(6)
    ]
    pair_y = [
        links.remote(lambda i=i: rcp.at[i], lambda i=i: ryp.at[i], mp_flip=1) for i in range(3)
    ]

    def settle(i):
        pair_c[i].wait_recv()
        accumulate(rcp.at[i], gp.at[i], core * (width // 2))

    def send_other(i):
        settle(i)
        pair_y[i].start()

    def join_own(k):
        settle(3 + k)
        pair_y[k].wait_recv()
        accumulate(ryp.at[k], rcp.at[3 + k])
        pairs[k].start_x(lambda: ryp.at[k])

    def each(group_of, name, *args):
        for unit in group_of:
            getattr(unit, name)(*args)

    def ff_z(k):
        for unit, held in zip(ff[k], kept[k]):
            unit.start_z(held)

    def slot_start():
        links.barrier(
            [(0, 1)]
            + [(1 << b, 0) for b in range(bits)]
            + [(12, 0)]
            + [(r << 4, 0) for r in range(1, n_dp // 16) if r & (r - 1)]
        )
        for copy in loads:
            copy.start()
        load_w.start()
        wo_c.start()
        for copy in y3:
            copy.start()
        for unit, source in zip(ff[0], (sum1u, sum1d)):
            unit.start_x(source)
        for unit, source in zip(ff[1], (sum2u, sum2d)):
            unit.start_x(source)
        y_home.start()

    def slot_end(i):
        pair_c[i].start()
        if i == 0:
            load_w.wait()
            wo_c.wait_recv()
            accumulate(rcw, kw)
            wo_y.start()
            for copy in loads:
                copy.wait()
        if i == 1:
            ff_z(0)
            send_other(0)
        if i == 2:
            each(ff[0], "start_z2")
            ff_z(1)
            send_other(1)
            for unit, copy, held, own in zip(ff[2], y3, kept[2], (k3u, k3d)):
                copy.wait_recv()
                accumulate(held, own)
                unit.start_x(held)
        if i == 3:
            each(ff[0], "start_back")
            each(ff[1], "start_z2")
            send_other(2)
            y_away.start()
            wo_y.wait_recv()
            accumulate(ryw, rcw.at[:, 0:heads_half])
            wo.start_x(ryw)
        if i == 4:
            each(ff[0], "start_back1")
            each(ff[1], "start_back")
            ff_z(2)
            join_own(0)
            wo.start_z(ryw)
        if i == 5:
            each(ff[0], "start_back_x")
            each(ff[1], "start_back1")
            each(ff[2], "start_z2")
            join_own(1)
            wo.start_back()
            pairs[0].start_z(lambda: ryp.at[0])

    @pl.when(step == 0)
    def _():
        slot_start()
        kht[64:160, :] = back_ref[...]
        lanes = lax.broadcasted_iota(jnp.int32, (tokens, 64), 1)
        vx[:, 64:128] = jnp.where(lanes < 2, -1.0, 0.0).astype(BF)
        dox[64:128, :] = jnp.zeros((64, tokens), BF)
        x = x_ref[...].astype(F32)
        inverse = lax.rsqrt(jnp.mean(x * x, axis=-1, keepdims=True) + EPS)
        n1t[...] = (x * inverse * gains[0:1]).astype(BF).T
        dn[...] = jnp.zeros_like(dn)
        gtab[...] = jnp.zeros_like(gtab)

    side = lax.broadcasted_iota(jnp.int32, (buckets, 128), 1)
    first_row = jnp.where(step < 3, 8 + 2 * step, 2 * (step - 3))
    dqs, dks, dvs = [], [], []
    for h in range(2):
        span = slice(64 * h, 64 * h + 64)
        scaled = dot_ref[span, :].astype(F32) * r_ref[0, h : h + 1, :]
        inner = jnp.sum(scaled * ot_ref[span, :].astype(F32), axis=0, keepdims=True)
        upper = inner.astype(BF)
        lower = (inner - upper.astype(F32)).astype(BF)
        dox[0:64, :] = scaled.astype(BF)
        dox[64:66, :] = jnp.concatenate([upper, lower], 0)
        vx[:, 0:64] = v_ref[:, span]
        kht[0:64, :] = k_ref[:, span].T
        dp = dg(vx[...], dox[...], 1, 0)
        p = p_ref[h]
        ds = (p.astype(F32) * dp).astype(BF)
        dvs.append(dg(p, dox[0:64, :], 1, 1).astype(BF))
        dks.append((dg(ds, qt_ref[span, :], 1, 1) * 0.125).astype(BF))
        both = dg(kht[...], ds, 1, 0)
        dqs.append((both[0:64] * 0.125).astype(BF).T)
        left = both[64:160]
        left_hi = left.astype(BF)
        left_lo = (left - left_hi.astype(F32)).astype(BF)
        hot = hot_ref[...]
        blocks = dg(left_hi, hot, 1, 0) + dg(left_lo, hot, 1, 0)
        for t in range(3):
            inside = (side >= t * buckets) & (side < (t + 1) * buckets)
            block = jnp.where(inside, blocks[t * buckets : (t + 1) * buckets], 0.0)
            rolled = pltpu.roll(block, (129 - (t + 1) * buckets) % 128, 1, stride=1, stride_axis=0)
            gtab[t, pl.ds(first_row + h, 1), :] = jnp.sum(rolled, axis=0, keepdims=True)
    grads = jnp.concatenate(dqs + dks + dvs, axis=1)
    weights = jnp.concatenate([wq_ref[...], wk_ref[...], wv_ref[...]], axis=1)
    dn[...] += dg(grads, weights, 1, 1)
    gp[step] = dg(n1t[...], grads, 1, 0).astype(BF)
    for i in range(6):
        pl.when(step == i)(functools.partial(slot_end, i))

    @pl.when(step == pl.num_programs(0) - 1)
    def _():
        x = x_ref[...].astype(F32)
        inverse = lax.rsqrt(jnp.mean(x * x, axis=-1, keepdims=True) + EPS)
        normed = x * inverse
        total = dn[...]
        grad_gain = jnp.sum(total * normed, axis=0, keepdims=True)
        inner = total * gains[0:1]
        added = inverse * (inner - normed * jnp.mean(inner * normed, axis=-1, keepdims=True))
        gin[...] = (dh_ref[...] + added).astype(BF)
        lines = width // 128
        for j in range(lines):
            lane = slice(j * 128, (j + 1) * 128)
            sums[0, j : j + 1, :] = grad_gain[:, lane]
            sums[0, lines + j : lines + j + 1, :] = ggf_ref[:, lane]
        sums[0, 2 * lines : 16, :] = jnp.zeros((16 - 2 * lines, 128), F32)
        line = lax.broadcasted_iota(jnp.int32, (128, 128), 0)
        lane = lax.broadcasted_iota(jnp.int32, (128, 128), 1)
        shift = jnp.where(lane < 64, lane, lane - 128)
        bucket = jnp.clip(-shift, -(buckets // 2), buckets // 2 - 1) + buckets // 2
        table = jnp.zeros((16, 128), F32)
        for t in range(3):
            pick = jnp.where(line == bucket + t * buckets, 1.0, 0.0)
            table = table + lax.dot_general(
                gtab[t], pick, (((1,), (1,)), ((), ())),
                precision=lax.Precision.HIGHEST, preferred_element_type=F32,
            )
        sums[0, 16:32, :] = table
        hops = bits + 1
        hop = None
        count = 0

        def small_hop():
            nonlocal hop, count
            if hop is not None:
                hop.wait_recv()
                k = count
                if k == 1:
                    sums[1, 0:16] = sums[0, 0:16] + got[0, 0:16]
                    sums[1, 16:24] = sums[0, 16:24] + got[0, 24:32]
                    sums[1, 24:32] = jnp.zeros((8, 128), F32)
                else:
                    sums[k] = sums[k - 1] + got[k - 1]
                hop = None
            if count < hops:
                flips = dict(mp_flip=1) if count == 0 else dict(dp_flip=1 << (count - 1))
                k = count
                hop = links.remote(lambda: sums.at[k], lambda: got.at[k], **flips)
                hop.start()
                started.append(hop)
                count += 1

        started = []
        small_hop()
        gin_away.start()
        gin_home.start()
        join_own(2)
        each(ff[0], "start_back_c")
        each(ff[1], "start_back_x")
        each(ff[2], "start_back")
        wo.start_back_x()
        pairs[1].start_z(lambda: ryp.at[1])
        pairs[0].start_back()
        small_hop()
        pairs[2].start_z(lambda: ryp.at[2])
        pairs[0].start_back_x()
        each(ff[1], "start_back_c")
        each(ff[2], "start_back1")
        pairs[1].start_back()
        wo.start_back_c()
        small_hop()
        pairs[2].start_back()
        each(ff[2], "start_back_x")
        pairs[1].start_back_x()
        pairs[0].start_back_c()
        small_hop()
        pairs[2].start_back_x()
        each(ff[2], "start_back_c")
        pairs[1].start_back_c()
        small_hop()
        pairs[2].start_back_c()
        while count < hops or hop is not None:
            small_hop()
        small[...] = sums[hops]
        y_away.wait_recv()
        gin_away.wait_recv()
        for unit in units:
            unit.end()
        for copy in [y_away, gin_away, wo_c, wo_y] + y3 + pair_c + pair_y + started:
            copy.wait_send()
        y_home.wait()
        gin_home.wait()


def backward(p, qt, kv, ot, dot, r, back, hot, x, gain, dh, ggf, wqkv, parts, gwo, y, n_dp, buckets):
    channels, tokens = qt.shape
    width = x.shape[1]
    n_pairs = channels // 128
    half = n_pairs // 2
    chunk = parts[0].shape[1]
    group = 3 * 128
    once = lambda shape: pl.BlockSpec(
        shape, lambda i: (0,) * len(shape), pipeline_mode=pl.Buffered(1)
    )
    pick = lambda i: lax.rem(i + half, n_pairs)
    side = lambda i: pick(i) // half
    place = lambda i: lax.rem(pick(i), half)
    turned = pl.BlockSpec((128, tokens), lambda i: (pick(i), 0))
    column = lambda rows, j, n: pl.BlockSpec(
        (rows, 128), lambda i: (0, side(i) * n * half + j * half + place(i))
    )
    shapes = []
    for k in range(3):
        shapes += [(width, chunk, True), (chunk, width, True)]
    shapes += [(width, group, False)] * 4
    units, far = [], []
    for n, w, deepest in shapes:
        units += [
            pltpu.VMEM((n // 4, w), BF),
            pltpu.VMEM((n // 16, w), BF),
            pltpu.VMEM((n // 8, w) if deepest else (3, n // 16, w), BF),
            pltpu.VMEM((n // 16, w), BF),
        ]
        far.append(pltpu.VMEM((max(n_dp // 16, 1), n // 16, w), BF))
    bits = n_dp.bit_length() - 1
    part_u, part_d = parts[0].shape, parts[1].shape
    copies = 160 + (10 * (n_dp // 16) if n_dp > 16 else 0)
    scratch = [
        pltpu.VMEM((tokens, 128), BF),
        pltpu.VMEM((128, tokens), BF),
        pltpu.VMEM((160, tokens), BF),
        pltpu.VMEM((width, tokens), BF),
        pltpu.VMEM((tokens, width), F32),
        pltpu.VMEM((3, 16, 128), F32),
        pltpu.VMEM((6, width, group), BF),
        pltpu.VMEM((6, width // 2, group), BF),
        pltpu.VMEM((3, width // 2, group), BF),
        pltpu.VMEM((tokens, width), BF),
        pltpu.VMEM(part_u, BF),
        pltpu.VMEM(part_d, BF),
        pltpu.VMEM(part_u, BF),
        pltpu.VMEM(part_d, BF),
        pltpu.VMEM(part_u, BF),
        pltpu.VMEM(part_d, BF),
        pltpu.VMEM(part_u, BF),
        pltpu.VMEM(part_d, BF),
        pltpu.VMEM((width // 2, width), BF),
        pltpu.VMEM((width // 2, width), BF),
        pltpu.VMEM((width // 2, width // 2), BF),
        pltpu.VMEM((bits + 2, 32, 128), F32),
        pltpu.VMEM((bits + 2, 32, 128), F32),
    ]
    scratch += units
    if n_dp > 16:
        scratch += far
    scratch += [pltpu.SemaphoreType.DMA((copies,))] * 2
    return pl.pallas_call(
        functools.partial(back_kernel, n_dp=n_dp, buckets=buckets),
        grid=(n_pairs,),
        in_specs=[
            pl.BlockSpec((2, tokens, tokens), lambda i: (pick(i), 0, 0)),
            turned,
            column(tokens, 0, 2),
            column(tokens, 1, 2),
            turned,
            turned,
            pl.BlockSpec((1, 2, tokens), lambda i: (pick(i), 0, 0)),
            once((96, tokens)),
            once((tokens, 128)),
            once((tokens, width)),
            once((2, width)),
            once((tokens, width)),
            once((1, width)),
            column(width, 0, 3),
            column(width, 1, 3),
            column(width, 2, 3),
        ]
        + [ANY] * 10,
        out_specs=[ANY] * 6 + [once((32, 128))],
        out_shape=[
            SHAPE((2, tokens // 2, width), BF),
            SHAPE((2, tokens // 2, width), BF),
            SHAPE((3, width, group), BF),
            SHAPE((width, group), BF),
            SHAPE((width, 3 * chunk), BF),
            SHAPE((3 * chunk, width), BF),
            SHAPE((32, 128), F32),
        ],
        scratch_shapes=scratch,
        compiler_params=params(60, collective_id=5, has_side_effects=True),
        name="backward",
    )(p, qt, kv, kv, ot, dot, r, back, hot, x, gain, dh, ggf, wqkv, wqkv, wqkv, *parts, gwo, y)


def local(
    n_dp, inputs, roi, cotangent, doc_lengths, live_mask, bucket_cells,
    gain_attn, gain_ffn, w_query, w_key, w_value, w_out, w_up, w_down, tables,
):
    rows, width = inputs.shape[1], inputs.shape[2]
    tokens = 2 * rows
    third = w_query.shape[1]
    heads = third // HDIM
    buckets = tables.shape[1]
    tab = jnp.pad(
        tables.transpose(2, 0, 1).reshape(heads, 3 * buckets), ((0, 2), (0, 128 - 3 * buckets))
    )
    marks = jnp.concatenate([live_mask[:, None, :], bucket_cells], axis=1)
    gains = jnp.stack([gain_attn, gain_ffn])
    x, tabo, wqkv, qt, kv, upo = entry(
        inputs, roi, tab, gains, w_query, w_key, w_value, w_up
    )
    p, mixt, r, hot, back, dyo, woo, upo, dno = attend(
        doc_lengths, marks, tab, tabo, qt, kv,
        cotangent, w_out, w_up, w_down, upo, buckets,
    )
    y, gwo, dh, dmt, gain_f, *parts = middle(
        x, mixt, w_out, woo, cotangent, dyo, gains, w_up, upo, w_down, dno
    )
    yret, gret, fqkv, fwo, fup, fdn, small = backward(
        p, qt, kv, mixt, dmt, r, back, hot, x, gains, dh, gain_f, wqkv, parts, gwo, y, n_dp, buckets
    )
    lines = width // 128
    out = inputs.astype(F32) + roi.astype(F32) + yret.astype(F32)
    grad_in = cotangent.astype(F32) + gret.astype(F32)
    table_out = small[16 : 16 + heads, : 3 * buckets].reshape(heads, 3, buckets).transpose(1, 2, 0)
    gq, gk, gv = (
        jnp.concatenate([fqkv[k, :, j * 128 : (j + 1) * 128] for k in range(3)], axis=1).astype(F32)
        for j in range(3)
    )
    return (
        out,
        grad_in,
        small[0:lines].reshape(width),
        small[lines : 2 * lines].reshape(width),
        gq,
        gk,
        gv,
        fwo.T.astype(F32),
        fup.astype(F32),
        fdn.astype(F32),
        table_out,
    )


def solution(mesh):
    n_dp = mesh.shape["dp"]
    rows = P(None, ("dp", "mp"), None)
    columns, lines = P(None, "mp"), P("mp", None)
    tables = P(None, None, "mp")
    return jax.shard_map(
        functools.partial(local, n_dp),
        mesh=mesh,
        in_specs=(
            rows, rows, rows, P(None, "dp", None), P(None, "dp"), P(None, None, "dp"),
            P(), P(), columns, columns, columns, lines, columns, lines, tables,
        ),
        out_specs=(
            rows, rows, P(), P(), columns, columns, columns, lines, columns, lines, tables,
        ),
        check_vma=False,
    )
```

```python
import functools
import math

import jax
import jax.numpy as jnp
from jax import lax
from jax.experimental import pallas as pl
from jax.experimental.pallas import tpu as pltpu
from jax.sharding import PartitionSpec as P

BF = jnp.bfloat16
F32 = jnp.float32
HDIM = 64
EPS = 1e-06
MASKED = -1e30
MESH = pl.DeviceIdType.MESH
VMEM = pl.BlockSpec(memory_space=pltpu.VMEM)
ANY = pl.BlockSpec(memory_space=pltpu.HBM)
SHAPE = jax.ShapeDtypeStruct


def dg(a, b, ca, cb):
    return lax.dot_general(a, b, (((ca,), (cb,)), ((), ())), preferred_element_type=F32)


def params(limit=58, **more):
    return pltpu.CompilerParams(vmem_limit_bytes=limit << 20, **more)


class Copy:
    def __init__(self, make):
        self.make = make

    def start(self):
        self.make().start()

    def wait(self):
        self.make().wait()

    def wait_recv(self):
        self.make().wait_recv()

    def wait_send(self):
        self.make().wait_send()


def now(ref):
    return ref() if callable(ref) else ref


class Links:
    def __init__(self, send, recv):
        self.send, self.recv, self.count = send, recv, 0
        self.d, self.m = lax.axis_index("dp"), lax.axis_index("mp")

    def flipped(self, dp_flip, mp_flip):
        dp = self.d ^ dp_flip if dp_flip else self.d
        mp = self.m ^ mp_flip if mp_flip else self.m
        return dp, mp

    def remote(self, src, dst, dp_flip=0, mp_flip=0):
        i = self.count
        self.count += 1
        return Copy(
            lambda: pltpu.make_async_remote_copy(
                src_ref=now(src),
                dst_ref=now(dst),
                send_sem=self.send.at[i],
                recv_sem=self.recv.at[i],
                device_id=self.flipped(dp_flip, mp_flip),
                device_id_type=MESH,
            )
        )

    def local(self, src, dst):
        i = self.count
        self.count += 1
        return Copy(lambda: pltpu.make_async_copy(now(src), now(dst), self.send.at[i]))

    def barrier(self, flips):
        sem = pltpu.get_barrier_semaphore()
        for flip in flips:
            pl.semaphore_signal(
                sem, inc=1, device_id=self.flipped(*flip), device_id_type=MESH
            )
        pl.semaphore_wait(sem, len(flips))


def rows_at(start, size, unit):
    return pl.ds(pl.multiple_of(start, unit), size)


def accumulate(into, other, start=0):
    n = into.shape[0]
    unit = 48 if n % 48 == 0 else 32

    def body(i, carry):
        here = rows_at(i * unit, unit, 16)
        there = rows_at(start + i * unit, unit, 16)
        into[here] = (into[here].astype(F32) + other[there].astype(F32)).astype(BF)
        return carry

    lax.fori_loop(0, n // unit, body, 0)


def carry_over(into, source, start=0):
    n = into.shape[0]
    unit = 48 if n % 48 == 0 else 32

    def body(i, carry):
        into[rows_at(i * unit, unit, 16)] = source[rows_at(start + i * unit, unit, 16)]
        return carry

    lax.fori_loop(0, n // unit, body, 0)


def entry_kernel(
    inp, roi, tab, gains, wq, wk, wv, wup,
    xf, tabo, wqkv, qt, kv, upo,
    sent, n1, send, recv,
):
    links = Links(send, recv)
    d, m = links.d, links.m
    rows = inp.shape[1]
    width, third = wq.shape
    piece = width // 8
    core, cross, deep = d & 1, (d >> 1) & 1, (d >> 2) & 1
    place = core * 4 + cross * 2 + deep
    links.barrier(((0, 1), (1, 0), (2, 0), (4, 0)))
    started = []

    def go(copy):
        copy.start()
        started.append(copy)
        return copy

    own_cols = [slice(j * third, (j + 1) * third) for j in range(3)]
    other_cols = [slice((3 + j) * third, (4 + j) * third) for j in range(3)]
    spot = rows_at(place * piece, piece, piece)
    first = [
        go(links.remote(w.at[spot], wqkv.at[spot, c], mp_flip=1))
        for w, c in zip((wq, wk, wv), other_cols)
    ]
    tab_copy = go(links.remote(tab, tabo, mp_flip=1))
    chunk = rows // 2
    row_copies = []
    for j in range(2):
        part = slice(j * chunk, (j + 1) * chunk)
        sent[part] = (inp[1 - m, part].astype(F32) + roi[1 - m, part].astype(F32)).astype(BF)
        here = rows_at(m * rows + j * chunk, chunk, chunk)
        row_copies.append(go(links.remote(sent.at[part], xf.at[here], mp_flip=1)))
    up_copy = go(links.remote(wup.at[spot], upo.at[spot], mp_flip=1))
    for w, c in zip((wq, wk, wv), own_cols):
        wqkv[:, c] = w[...]

    def normalise(where):
        x = xf[where].astype(F32)
        inverse = lax.rsqrt(jnp.mean(x * x, axis=-1, keepdims=True) + EPS)
        n1[where] = (x * inverse * gains[0:1]).astype(BF)

    own = rows_at(m * rows, rows, rows)
    xf[own] = (inp[m].astype(F32) + roi[m].astype(F32)).astype(BF)
    normalise(own)

    def project(where, side):
        rows_in = n1[where]
        base = side * 3 * third
        kv[where, side * 2 * third : (side + 1) * 2 * third] = dg(
            rows_in, wqkv[:, base + third : base + 3 * third], 1, 0
        ).astype(BF)
        qt[side * third : (side + 1) * third, where] = dg(
            wqkv[:, base : base + third], rows_in, 0, 1
        ).astype(BF)

    project(own, 0)
    stage = first
    for flip, begin, count in (
        (4, place, 1),
        (2, core * 4 + cross * 2, 2),
        (1, core * 4, 4),
    ):
        for copy in stage:
            copy.wait_recv()
        there = wqkv.at[rows_at(begin * piece, count * piece, piece), 3 * third : 6 * third]
        stage = [go(links.remote(there, there, dp_flip=flip))]
    for j in range(2):
        row_copies[j].wait_recv()
        here = rows_at((1 - m) * rows + j * chunk, chunk, chunk)
        normalise(here)
        project(here, 0)
    for copy in stage:
        copy.wait_recv()
    for j in range(2):
        project(slice(j * rows, (j + 1) * rows), 1)
    tab_copy.wait_recv()
    up_copy.wait_recv()
    for copy in started:
        copy.wait_send()


def entry(inputs, roi, tab, gain, wq, wk, wv, wup):
    rows, width = inputs.shape[1], inputs.shape[2]
    third = wq.shape[1]
    tokens = 2 * rows
    return pl.pallas_call(
        entry_kernel,
        out_shape=[
            SHAPE((tokens, width), BF),
            SHAPE(tab.shape, F32),
            SHAPE((width, 6 * third), BF),
            SHAPE((2 * third, tokens), BF),
            SHAPE((tokens, 4 * third), BF),
            SHAPE(wup.shape, BF),
        ],
        in_specs=[VMEM] * 7 + [ANY],
        out_specs=[VMEM] * 5 + [ANY],
        scratch_shapes=[
            pltpu.VMEM((rows, width), BF),
            pltpu.VMEM((tokens, width), BF),
            pltpu.SemaphoreType.DMA((12,)),
            pltpu.SemaphoreType.DMA((12,)),
        ],
        compiler_params=params(58, collective_id=1, has_side_effects=True),
        name="entry",
    )(inputs, roi, tab, gain, wq, wk, wv, wup)


def attend_kernel(
    lengths, marks, tab, tabo, qt_ref, k_ref, v_ref, cot, wo, wup, wdn, upo_in,
    p_ref, o_ref, r_ref, hot_ref, back_ref, dyo, woo, upo, dno,
    kx, qx, vx, mask, mats, hott_ref, send, recv, *, buckets,
):
    links = Links(send, recv)
    d, m = links.d, links.m
    tokens = k_ref.shape[0]
    rows = tokens // 2
    width, hidden = wup.shape
    inner = wo.shape[0]
    step = pl.program_id(0)
    core, cross, deep = d & 1, (d >> 1) & 1, (d >> 2) & 1
    place = core * 4 + cross * 2 + deep

    def block(full, begin, count):
        piece = full.shape[0] // 8
        return full.at[rows_at(begin * piece, count * piece, piece)]

    up = functools.partial(block, upo)
    down = functools.partial(block, dno)
    out = functools.partial(block, woo)
    dpiece, opiece = hidden // 8, inner // 8
    quarter = core * 4 + deep * 2
    down_y = [
        links.remote(
            wdn.at[rows_at((quarter + j) * dpiece, dpiece, dpiece)], down(quarter + j, 1), mp_flip=1
        )
        for j in range(2)
    ]
    out_y = links.remote(wo.at[rows_at(place * opiece, opiece, opiece)], out(place, 1), mp_flip=1)
    dy_y = links.remote(cot.at[1 - m], dyo, mp_flip=1)
    up_z = links.remote(up(place, 1), up(place, 1), dp_flip=4)
    pair = core * 4 + cross * 2
    up_x = links.remote(up(pair, 2), up(pair, 2), dp_flip=2)
    up_c = links.remote(up(core * 4, 4), up(core * 4, 4), dp_flip=1)
    down_z = [
        links.remote(down(quarter + j, 1), down(quarter + j, 1), dp_flip=4) for j in range(2)
    ]
    down_c = links.remote(down(core * 4, 4), down(core * 4, 4), dp_flip=1)
    out_z = links.remote(out(place, 1), out(place, 1), dp_flip=4)
    out_x = links.remote(out(pair, 2), out(pair, 2), dp_flip=2)
    out_c = links.remote(out(core * 4, 4), out(core * 4, 4), dp_flip=1)

    def slot0():
        links.barrier(((0, 1), (1, 0), (2, 0), (4, 0)))
        up_z.start()
        down_y[0].start()
        out_y.start()

    def slot4():
        up_z.wait_recv()
        up_x.start()

    def slot2():
        down_y[1].start()

    def slot5():
        down_y[0].wait_recv()
        down_z[0].start()

    def slot6():
        dy_y.start()
        out_y.wait_recv()
        out_z.start()

    def slot7():
        down_y[1].wait_recv()
        down_z[1].start()

    def slot9():
        out_z.wait_recv()
        out_x.start()

    def slot11():
        up_x.wait_recv()
        up_c.start()
        out_x.wait_recv()
        out_c.start()

    def last():
        down_z[0].wait_recv()
        down_z[1].wait_recv()
        down_c.start()
        for copy in (dy_y, up_c, out_c, down_c):
            copy.wait_recv()
        for copy in (*down_y, out_y, dy_y, up_z, up_x, up_c, *down_z, down_c, out_z, out_x, out_c):
            copy.wait_send()

    slots = {0: slot0, 1: slot2, 4: slot4, 5: slot5, 6: slot6, 7: slot7, 9: slot9, 11: slot11}

    @pl.when(step == 0)
    def _():
        slot0()
        vx[64:80, :] = jnp.ones((16, tokens), BF)
        lane = lax.broadcasted_iota(jnp.int32, (buckets, tokens), 0)
        for t in range(3):
            row = marks[m, t + 1 : t + 2, :]
            hott_ref[t * buckets : (t + 1) * buckets, :] = jnp.where(row == lane, 1.0, 0.0).astype(BF)
            mirror = jnp.where(row == buckets - 1 - lane, 1.0, 0.0).astype(BF)
            back_ref[t * buckets : (t + 1) * buckets, :] = mirror
        hott_ref[96:128, :] = jnp.zeros((32, tokens), BF)
        wide_hot = hott_ref[...].T
        hot_ref[...] = wide_hot
        hot = wide_hot[:, 0:96]
        kx[:, 64:160] = hot
        kx[:, 160:256] = hot
        row_ids = lax.broadcasted_iota(jnp.int32, (1, tokens), 1)
        col_ids = lax.broadcasted_iota(jnp.int32, (tokens, 1), 0)
        seg_row = jnp.zeros((1, tokens), jnp.int32)
        seg_col = jnp.zeros((tokens, 1), jnp.int32)
        end = 0
        for i in range(lengths.shape[2]):
            end = end + lengths[m, 0, i]
            seg_row = seg_row + jnp.where(row_ids >= end, 1, 0)
            seg_col = seg_col + jnp.where(col_ids >= end, 1, 0)
        live_row = marks[m, 0:1, :].astype(F32)
        live_col = jnp.broadcast_to(live_row, (8, tokens)).T[:, 0:1]
        code = jnp.where(live_col == 1.0, seg_col, -1)
        allowed = (code == seg_row) | (col_ids == row_ids)
        mask[...] = jnp.where(allowed, 0.0, MASKED)
        line = lax.broadcasted_iota(jnp.int32, (128, 128), 0)
        lane = lax.broadcasted_iota(jnp.int32, (128, 128), 1)
        shift = jnp.where(lane < 64, lane, lane - 128)
        bucket = jnp.clip(-shift, -(buckets // 2), buckets // 2 - 1) + buckets // 2
        side = lax.broadcasted_iota(jnp.int32, (buckets, 128), 1)
        heads = mats.shape[0] // 2
        for part, table in enumerate((tab, tabo)):
            exact = table[...]
            upper = exact.astype(BF)
            lower = (exact - upper.astype(F32)).astype(BF)
            for t in range(3):
                pick = jnp.where(line == bucket + t * buckets, 1.0, 0.0).astype(BF)
                inside = (side >= t * buckets) & (side < (t + 1) * buckets)
                for level, source in enumerate((upper, lower)):
                    lines = dg(source, pick, 1, 0)
                    for h in range(heads):
                        wide = jnp.broadcast_to(lines[h : h + 1], (buckets, 128))
                        rolled = pltpu.roll(wide, t * buckets, 1, stride=1, stride_axis=0)
                        begin = level * 3 * buckets + t * buckets
                        mats[part * heads + h, begin : begin + buckets, :] = jnp.where(
                            inside, rolled, 0.0
                        ).astype(BF)

    vt = v_ref[...].T
    for h in range(2):
        for at, action in slots.items():
            if at % 2 == h and at > 0:
                pl.when(step == at // 2)(action)
        span = slice(64 * h, 64 * h + 64)
        kx[:, 0:64] = k_ref[:, span]
        qx[0:64, :] = qt_ref[span, :] * BF(0.125)
        qx[64:256, :] = dg(mats[2 * step + h], hott_ref[...], 1, 0).astype(BF)
        vx[0:64, :] = vt[span, :]
        s = dg(kx[...], qx[...], 1, 0) + mask[...]
        top = jnp.max(s, axis=0, keepdims=True)
        p = jnp.exp(s - top).astype(BF)
        p_ref[h] = p
        o = dg(vx[...], p, 1, 0)
        r = 1.0 / o[64:65, :]
        o_ref[span, :] = (o[0:64] * r).astype(BF)
        r_ref[0, h : h + 1, :] = r
    pl.when(step == pl.num_programs(0) - 1)(last)


def attend(lengths, marks, tab, tabo, qt, kv, cot, wo, wup, wdn, upo, buckets):
    channels, tokens = qt.shape
    width, hidden = wup.shape
    inner = wo.shape[0]
    pairs = channels // 128
    half = pairs // 2
    whole = lambda shape: pl.BlockSpec(shape, lambda i: (0,) * len(shape))
    return pl.pallas_call(
        functools.partial(attend_kernel, buckets=buckets),
        grid=(pairs,),
        in_specs=[
            pl.BlockSpec(memory_space=pltpu.SMEM),
            whole(marks.shape),
            whole(tab.shape),
            whole(tabo.shape),
            pl.BlockSpec((128, tokens), lambda i: (i, 0)),
            pl.BlockSpec((tokens, 128), lambda i: (0, (i // half) * 2 * half + i % half)),
            pl.BlockSpec((tokens, 128), lambda i: (0, (i // half) * 2 * half + half + i % half)),
            ANY, ANY, ANY, ANY, ANY,
        ],
        out_specs=[
            pl.BlockSpec((2, tokens, tokens), lambda i: (i, 0, 0)),
            pl.BlockSpec((128, tokens), lambda i: (i, 0)),
            pl.BlockSpec((1, 2, tokens), lambda i: (i, 0, 0)),
            whole((tokens, 128)),
            whole((96, tokens)),
            ANY, ANY, ANY, ANY,
        ],
        out_shape=[
            SHAPE((2 * pairs, tokens, tokens), BF),
            SHAPE((channels, tokens), BF),
            SHAPE((pairs, 2, tokens), F32),
            SHAPE((tokens, 128), BF),
            SHAPE((96, tokens), BF),
            SHAPE((tokens // 2, width), BF),
            SHAPE((inner, width), BF),
            SHAPE((width, hidden), BF),
            SHAPE((hidden, width), BF),
        ],
        input_output_aliases={11: 7},
        scratch_shapes=[
            pltpu.VMEM((tokens, 256), BF),
            pltpu.VMEM((256, tokens), BF),
            pltpu.VMEM((80, tokens), BF),
            pltpu.VMEM((tokens, tokens), F32),
            pltpu.VMEM((2 * pairs, 192, 128), BF),
            pltpu.VMEM((128, tokens), BF),
            pltpu.SemaphoreType.DMA((20,)),
            pltpu.SemaphoreType.DMA((20,)),
        ],
        compiler_params=params(58, collective_id=3, has_side_effects=True),
        name="attend",
    )(lengths, marks, tab, tabo, qt, kv, kv, cot, wo, wup, wdn, upo)


def middle_kernel(
    x_ref, mixt_ref, wo_in, woo_in, cot, dyo, gains, wup_in, upo_in, wdn_in, dno_in,
    y_ref, gwo_ref, dh_ref, dmt_ref, gg_ref,
    sum1u, sum1d, sum2u, sum2d, own3u, own3d, far3u, far3d,
    h1, n2, n2t, yacc, dn, wo_ref, dy_ref, gu, gd, rcu, rcd, ryu, ryd, send, recv,
):
    links = Links(send, recv)
    core = links.d & 1
    step = pl.program_id(0)
    last = pl.num_programs(0) - 1
    half_steps = pl.num_programs(0) // 2
    early = step < half_steps
    width, chunk = gu.shape[1:]
    keep_u, give_u = (rows_at(c * (width // 2), width // 2, 16) for c in (core, 1 - core))
    keep_d, give_d = (rows_at(c * (chunk // 2), chunk // 2, 16) for c in (core, 1 - core))

    def core_copies(i):
        return (
            pltpu.make_async_remote_copy(
                gu.at[i % 2, give_u], rcu.at[i], send.at[0, i], recv.at[0, i],
                device_id=(links.d ^ 1, links.m), device_id_type=MESH,
            ),
            pltpu.make_async_remote_copy(
                gd.at[i % 2, give_d], rcd.at[i], send.at[1, i], recv.at[1, i],
                device_id=(links.d ^ 1, links.m), device_id_type=MESH,
            ),
        )

    def pair_copies(i):
        return (
            pltpu.make_async_remote_copy(
                rcu.at[i], ryu.at[i], send.at[2, i], recv.at[2, i],
                device_id=(links.d, 1 - links.m), device_id_type=MESH,
            ),
            pltpu.make_async_remote_copy(
                rcd.at[i], ryd.at[i], send.at[3, i], recv.at[3, i],
                device_id=(links.d, 1 - links.m), device_id_type=MESH,
            ),
        )

    def settle(i):
        for copy in core_copies(i):
            copy.wait_recv()
        for copy in core_copies(i):
            copy.wait_send()
        accumulate(rcu.at[i], gu.at[i % 2], core * (width // 2))
        accumulate(rcd.at[i], gd.at[i % 2], core * (chunk // 2))

    @pl.when(step == 0)
    def _():
        links.barrier(((0, 1), (1, 0)))
        m = links.m
        rows = dyo.shape[0]
        dy_ref[rows_at(m * rows, rows, rows)] = cot[m]
        dy_ref[rows_at((1 - m) * rows, rows, rows)] = dyo[...]
        inner = wo_in.shape[0]
        wo_ref[0:inner] = wo_in[...]
        wo_ref[inner:] = woo_in[...]
        added = dg(mixt_ref[...], wo_ref[...], 0, 0)
        h = x_ref[...].astype(F32) + added
        h1[...] = h
        yacc[...] = added
        inverse = lax.rsqrt(jnp.mean(h * h, axis=-1, keepdims=True) + EPS)
        normed = (h * inverse * gains[1:2]).astype(BF)
        n2[...] = normed
        n2t[...] = normed.T
        dn[...] = jnp.zeros_like(dn)

    wup = jnp.where(early, upo_in[...], wup_in[...])
    wdn = jnp.where(early, dno_in[...], wdn_in[...])
    dy = dy_ref[...]
    u = dg(n2[...], wup, 1, 0)
    cdf = 0.5 * (1.0 + lax.erf(u * 0.7071067811865476))
    act = (u * cdf).astype(BF)
    grad_act = dg(dy, wdn, 1, 1)
    density = jnp.exp(u * u * (-0.5)) * 0.3989422804014327
    du = (grad_act * (cdf + u * density)).astype(BF)
    yacc[...] += dg(act, wdn, 1, 0)

    @pl.when(step > 0)
    def _():
        settle(step - 1)

    @pl.when((step > 0) & (step < half_steps))
    def _():
        for copy in pair_copies(step - 1):
            copy.start()

    dn[...] += dg(du, wup, 1, 1)
    gu[step % 2] = dg(n2t[...], du, 1, 0).astype(BF)
    gd[step % 2] = dg(act, dy, 0, 0).astype(BF)
    for copy in core_copies(step):
        copy.start()

    @pl.when(step == last)
    def _():
        h = h1[...]
        inverse = lax.rsqrt(jnp.mean(h * h, axis=-1, keepdims=True) + EPS)
        normed = h * inverse
        grad = dn[...]
        gg_ref[...] = jnp.sum(grad * normed, axis=0, keepdims=True)
        inner = grad * gains[1:2]
        added = inverse * (inner - normed * jnp.mean(inner * normed, axis=-1, keepdims=True))
        dh_ref[...] = added
        y_ref[...] = yacc[...].astype(BF)
        low = (dy_ref[...].astype(F32) + added).astype(BF)
        gwo_ref[...] = dg(low, mixt_ref[...], 0, 1).astype(BF)
        dmt_ref[...] = dg(wo_ref[...], low, 1, 1).astype(BF)
        settle(last)
        n = rcu.shape[0] // 2
        for k, (out_u, out_d) in enumerate(((sum1u, sum1d), (sum2u, sum2d))):
            for copy in pair_copies(k):
                copy.wait_recv()
            accumulate(rcu.at[n + k], ryu.at[k])
            accumulate(rcd.at[n + k], ryd.at[k])
            carry_over(out_u, rcu.at[n + k])
            carry_over(out_d, rcd.at[n + k])
        carry_over(own3u, rcu.at[n + 2])
        carry_over(own3d, rcd.at[n + 2])
        carry_over(far3u, rcu.at[2])
        carry_over(far3d, rcd.at[2])
        for k in range(2):
            for copy in pair_copies(k):
                copy.wait_send()


def middle(x, mixt, wo, woo, cot, dyo, gain, wup, upo, wdn, dno):
    tokens, width = x.shape
    half = wup.shape[1]
    chunk = half // 3
    n = 6
    once = lambda shape: pl.BlockSpec(
        shape, lambda i: (0,) * len(shape), pipeline_mode=pl.Buffered(1)
    )
    late = lambda i: jnp.maximum(i - n // 2, 0)
    early = lambda i: jnp.minimum(i, n // 2 - 1)
    part_u, part_d = (width // 2, chunk), (chunk // 2, width)
    outs = [
        ((tokens, width), BF),
        ((width, width), BF),
        ((tokens, width), F32),
        ((width, tokens), BF),
        ((1, width), F32),
    ] + [(part_u, BF), (part_d, BF)] * 4
    return pl.pallas_call(
        middle_kernel,
        grid=(n,),
        in_specs=[
            once((tokens, width)),
            once((width, tokens)),
            once(wo.shape),
            once(woo.shape),
            once(cot.shape),
            once(dyo.shape),
            once((2, width)),
            pl.BlockSpec((width, chunk), lambda i: (0, late(i))),
            pl.BlockSpec((width, chunk), lambda i: (0, early(i))),
            pl.BlockSpec((chunk, width), lambda i: (late(i), 0)),
            pl.BlockSpec((chunk, width), lambda i: (early(i), 0)),
        ],
        out_specs=[once(shape) for shape, _ in outs],
        out_shape=[SHAPE(*entry) for entry in outs],
        scratch_shapes=[
            pltpu.VMEM((tokens, width), F32),
            pltpu.VMEM((tokens, width), BF),
            pltpu.VMEM((width, tokens), BF),
            pltpu.VMEM((tokens, width), F32),
            pltpu.VMEM((tokens, width), F32),
            pltpu.VMEM((width, width), BF),
            pltpu.VMEM((tokens, width), BF),
            pltpu.VMEM((2, width, chunk), BF),
            pltpu.VMEM((2, chunk, width), BF),
            pltpu.VMEM((n,) + part_u, BF),
            pltpu.VMEM((n,) + part_d, BF),
            pltpu.VMEM((2,) + part_u, BF),
            pltpu.VMEM((2,) + part_d, BF),
            pltpu.SemaphoreType.DMA((4, n)),
            pltpu.SemaphoreType.DMA((4, n)),
        ],
        compiler_params=params(60, collective_id=4, has_side_effects=True),
        name="middle",
    )(x, mixt, wo, woo, cot, dyo, gain, wup, upo, wdn, dno)


class Unit:
    def __init__(self, links, n, w, rx, rz, zp, final, far, n_dp, deepest):
        self.links, self.n, self.w = links, n, w
        self.rx, self.rz, self.zp, self.final, self.far = rx, rz, zp, final, far
        self.n_dp, self.stepwise = n_dp, deepest
        d = links.d
        self.core, self.cross = d & 1, (d >> 1) & 1
        self.b0, self.b1 = (d >> 2) & 1, (d >> 3) & 1
        q = n // 16
        self.q = q
        self.xr = links.remote(lambda: self.xr.make_source(), rx, dp_flip=2)
        spot = self.core * 8 + self.cross * 4 + self.b0 * 2 + self.b1
        self.piece = lambda: final(spot * q, q)
        self.home = links.local(zp, self.piece)
        if deepest:
            keep = self.b0 * 2
            give = (1 - self.b0) * 2
            self.z1 = links.remote(lambda: rx.at[rows_at(give * q, 2 * q, 16)], rz[0], dp_flip=4)
            self.z2 = links.remote(
                lambda: rz[0].at[rows_at((1 - self.b1) * q, q, 16)], rz[1], dp_flip=8
            )
            self.g2 = links.remote(zp, self.piece, dp_flip=8)
            both = lambda: final((self.core * 8 + self.cross * 4 + keep) * q, 2 * q)
            self.g1 = links.remote(both, both, dp_flip=4)
        else:
            self.zs, self.gs = [], []
            for r in range(1, 4):
                p0, p1 = self.b0 ^ (r & 1), self.b1 ^ (r >> 1)
                src = lambda p=p0 * 2 + p1: rx.at[rows_at(p * q, q, 16)]
                dst = lambda r=r: rz[0].at[r - 1]
                self.zs.append(links.remote(src, dst, dp_flip=r << 2))
                self.gs.append(links.remote(zp, self.piece, dp_flip=r << 2))
        quad = lambda: final((self.core * 8 + self.cross * 4) * q, 4 * q)
        self.gx = links.remote(quad, quad, dp_flip=2)
        side = lambda: final(self.core * 8 * q, 8 * q)
        self.gc = links.remote(side, side, dp_flip=1)
        if far is not None:
            self.others = [
                links.remote(lambda: far.at[0], lambda r=r: far.at[r], dp_flip=r << 4)
                for r in range(1, n_dp // 16)
            ]

    def start_x(self, source):
        half = self.n // 4
        self.xr.make_source = lambda: now(source).at[rows_at((1 - self.cross) * half, half, 16)]
        self.xr.start()

    def add_x(self, kept):
        half = self.n // 4
        self.xr.wait_recv()
        accumulate(self.rx, now(kept), self.cross * half)

    def start_z(self, kept):
        self.add_x(kept)
        for copy in [self.z1] if self.stepwise else self.zs:
            copy.start()

    def start_z2(self):
        self.z1.wait_recv()
        accumulate(self.rz[0], self.rx, self.b0 * 2 * self.q)
        self.z2.start()

    def start_back(self):
        q = self.q
        if self.stepwise:
            self.z2.wait_recv()
            total = self.rz[0][rows_at(self.b1 * q, q, 16)].astype(F32)
            total = total + self.rz[1][...].astype(F32)
        else:
            for copy in self.zs:
                copy.wait_recv()
            total = self.rx[rows_at((self.b0 * 2 + self.b1) * q, q, 16)].astype(F32)
            for r in range(3):
                total = total + self.rz[0][r].astype(F32)
        if self.far is not None:
            self.far[0] = total.astype(BF)
            for copy in self.others:
                copy.start()
            for r, copy in enumerate(self.others):
                copy.wait_recv()
                total = total + self.far[r + 1].astype(F32)
        self.zp[...] = total.astype(BF)
        self.home.start()
        for copy in [self.g2] if self.stepwise else self.gs:
            copy.start()

    def start_back1(self):
        self.home.wait()
        self.g2.wait_recv()
        self.g1.start()

    def start_back_x(self):
        if self.stepwise:
            self.g1.wait_recv()
        else:
            self.home.wait()
            for copy in self.gs:
                copy.wait_recv()
        self.gx.start()

    def start_back_c(self):
        self.gx.wait_recv()
        self.gc.start()

    def end(self):
        self.gc.wait_recv()
        sent = [self.xr, self.gx, self.gc]
        sent += [self.z1, self.z2, self.g2, self.g1] if self.stepwise else self.zs + self.gs
        if self.far is not None:
            sent += self.others
        for copy in sent:
            copy.wait_send()


def back_kernel(
    p_ref, qt_ref, k_ref, v_ref, ot_ref, dot_ref, r_ref, back_ref, hot_ref,
    x_ref, gains, dh_ref, ggf_ref, wq_ref, wk_ref, wv_ref,
    sum1u, sum1d, sum2u, sum2d, own3u, own3d, far3u, far3d, gwo, y,
    yret, gret, fqkv, fwo, fup, fdn, small,
    vx, dox, kht, n1t, dn, gtab, gp, rcp, ryp, gin,
    k1u, k1d, k2u, k2d, k3u, k3d, ry3u, ry3d, kw, rcw, ryw,
    sums, got, *rest, n_dp, buckets,
):
    units_scratch, rest = rest[: 4 * 10], rest[4 * 10 :]
    far = rest[:10] if n_dp > 16 else [None] * 10
    send, recv = rest[-2:]
    links = Links(send, recv)
    d, m = links.d, links.m
    core = d & 1
    step = pl.program_id(0)
    tokens, width = x_ref.shape
    rows = tokens // 2
    chunk = far3u.shape[1]
    group = gp.shape[2]
    bits = n_dp.bit_length() - 1

    def region(ref, row0, col0, w, lead=None):
        def at(start, count):
            where = rows_at(row0 + start, count, 16)
            if lead is not None:
                return ref.at[lead, where]
            return ref.at[where, col0 : col0 + w]

        return at

    finals = []
    for k in range(3):
        finals.append((width, chunk, region(fup, 0, k * chunk, chunk), True))
        finals.append((chunk, width, region(fdn, k * chunk, 0, width), True))
    finals.append((width, group, region(fwo, 0, 0, group), False))
    for k in range(3):
        finals.append((width, group, region(fqkv, 0, 0, group, lead=k), False))
    units = []
    for i, (n, w, final, deepest) in enumerate(finals):
        rx, zp = units_scratch[4 * i], units_scratch[4 * i + 1]
        rz = units_scratch[4 * i + 2 : 4 * i + 4]
        units.append(Unit(links, n, w, rx, rz, zp, final, far[i], n_dp, deepest))
    ff = (units[0:2], units[2:4], units[4:6])
    wo, pairs = units[6], units[7:10]
    kept = ((k1u, k1d), (k2u, k2d), (ry3u, ry3d))
    heads_half = width // 2

    mine = rows_at(m * rows, rows, rows)
    theirs = rows_at((1 - m) * rows, rows, rows)
    y_home = links.local(lambda: y.at[mine], lambda: yret.at[m])
    y_away = links.remote(lambda: y.at[theirs], lambda: yret.at[m], mp_flip=1)
    gin_home = links.local(lambda: gin.at[mine], lambda: gret.at[m])
    gin_away = links.remote(lambda: gin.at[theirs], lambda: gret.at[m], mp_flip=1)
    loads = [
        links.local(src, dst)
        for src, dst in ((sum1u, k1u), (sum1d, k1d), (sum2u, k2u), (sum2d, k2d), (own3u, k3u), (own3d, k3d))
    ]
    keep = rows_at(core * (width // 2), width // 2, 16)
    give = rows_at((1 - core) * (width // 2), width // 2, 16)
    load_w = links.local(lambda: gwo.at[keep], kw)
    y3 = [links.remote(far3u, ry3u, mp_flip=1), links.remote(far3d, ry3d, mp_flip=1)]
    wo_c = links.remote(lambda: gwo.at[give], rcw, dp_flip=1)
    wo_y = links.remote(lambda: rcw.at[:, heads_half:], ryw, mp_flip=1)
    pair_c = [
        links.remote(lambda i=i: gp.at[i, give], lambda i=i: rcp.at[i], dp_flip=1) for i in range(6)
    ]
    pair_y = [
        links.remote(lambda i=i: rcp.at[i], lambda i=i: ryp.at[i], mp_flip=1) for i in range(3)
    ]

    def settle(i):
        pair_c[i].wait_recv()
        accumulate(rcp.at[i], gp.at[i], core * (width // 2))

    def send_other(i):
        settle(i)
        pair_y[i].start()

    def join_own(k):
        settle(3 + k)
        pair_y[k].wait_recv()
        accumulate(ryp.at[k], rcp.at[3 + k])
        pairs[k].start_x(lambda: ryp.at[k])

    def each(group_of, name, *args):
        for unit in group_of:
            getattr(unit, name)(*args)

    def ff_z(k):
        for unit, held in zip(ff[k], kept[k]):
            unit.start_z(held)

    def slot_start():
        links.barrier(
            [(0, 1)]
            + [(1 << b, 0) for b in range(bits)]
            + [(12, 0)]
            + [(r << 4, 0) for r in range(1, n_dp // 16) if r & (r - 1)]
        )
        for copy in loads:
            copy.start()
        load_w.start()
        wo_c.start()
        for copy in y3:
            copy.start()
        for unit, source in zip(ff[0], (sum1u, sum1d)):
            unit.start_x(source)
        for unit, source in zip(ff[1], (sum2u, sum2d)):
            unit.start_x(source)
        y_home.start()

    def slot_end(i):
        pair_c[i].start()
        if i == 0:
            load_w.wait()
            wo_c.wait_recv()
            accumulate(rcw, kw)
            wo_y.start()
            for copy in loads:
                copy.wait()
        if i == 1:
            ff_z(0)
            send_other(0)
        if i == 2:
            each(ff[0], "start_z2")
            ff_z(1)
            send_other(1)
            for unit, copy, held, own in zip(ff[2], y3, kept[2], (k3u, k3d)):
                copy.wait_recv()
                accumulate(held, own)
                unit.start_x(held)
        if i == 3:
            each(ff[0], "start_back")
            each(ff[1], "start_z2")
            send_other(2)
            wo_y.wait_recv()
            accumulate(ryw, rcw.at[:, 0:heads_half])
            wo.start_x(ryw)
        if i == 4:
            each(ff[0], "start_back1")
            each(ff[1], "start_back")
            ff_z(2)
            join_own(0)
            wo.start_z(ryw)
            y_away.start()
        if i == 5:
            each(ff[0], "start_back_x")
            each(ff[1], "start_back1")
            each(ff[2], "start_z2")
            join_own(1)
            wo.start_back()
            pairs[0].start_z(lambda: ryp.at[0])
            join_own(2)

    @pl.when(step == 0)
    def _():
        slot_start()
        kht[64:160, :] = back_ref[...]
        lanes = lax.broadcasted_iota(jnp.int32, (tokens, 64), 1)
        vx[:, 64:128] = jnp.where(lanes < 2, -1.0, 0.0).astype(BF)
        dox[64:128, :] = jnp.zeros((64, tokens), BF)
        x = x_ref[...].astype(F32)
        inverse = lax.rsqrt(jnp.mean(x * x, axis=-1, keepdims=True) + EPS)
        n1t[...] = (x * inverse * gains[0:1]).astype(BF).T
        dn[...] = jnp.zeros_like(dn)
        gtab[...] = jnp.zeros_like(gtab)

    side = lax.broadcasted_iota(jnp.int32, (buckets, 128), 1)
    first_row = jnp.where(step < 3, 8 + 2 * step, 2 * (step - 3))
    dqs, dks, dvs = [], [], []
    for h in range(2):
        span = slice(64 * h, 64 * h + 64)
        scaled = dot_ref[span, :].astype(F32) * r_ref[0, h : h + 1, :]
        inner = jnp.sum(scaled * ot_ref[span, :].astype(F32), axis=0, keepdims=True)
        upper = inner.astype(BF)
        lower = (inner - upper.astype(F32)).astype(BF)
        dox[0:64, :] = scaled.astype(BF)
        dox[64:66, :] = jnp.concatenate([upper, lower], 0)
        vx[:, 0:64] = v_ref[:, span]
        kht[0:64, :] = k_ref[:, span].T
        dp = dg(vx[...], dox[...], 1, 0)
        p = p_ref[h]
        ds = (p.astype(F32) * dp).astype(BF)
        dvs.append(dg(p, dox[0:64, :], 1, 1).astype(BF))
        dks.append((dg(ds, qt_ref[span, :], 1, 1) * 0.125).astype(BF))
        both = dg(kht[...], ds, 1, 0)
        dqs.append((both[0:64] * 0.125).astype(BF).T)
        left = both[64:160]
        left_hi = left.astype(BF)
        left_lo = (left - left_hi.astype(F32)).astype(BF)
        hot = hot_ref[...]
        blocks = dg(left_hi, hot, 1, 0) + dg(left_lo, hot, 1, 0)
        for t in range(3):
            inside = (side >= t * buckets) & (side < (t + 1) * buckets)
            block = jnp.where(inside, blocks[t * buckets : (t + 1) * buckets], 0.0)
            rolled = pltpu.roll(block, (129 - (t + 1) * buckets) % 128, 1, stride=1, stride_axis=0)
            gtab[t, pl.ds(first_row + h, 1), :] = jnp.sum(rolled, axis=0, keepdims=True)
    grads = jnp.concatenate(dqs + dks + dvs, axis=1)
    weights = jnp.concatenate([wq_ref[...], wk_ref[...], wv_ref[...]], axis=1)
    dn[...] += dg(grads, weights, 1, 1)
    gp[step] = dg(n1t[...], grads, 1, 0).astype(BF)
    for i in range(6):
        pl.when(step == i)(functools.partial(slot_end, i))

    @pl.when(step == pl.num_programs(0) - 1)
    def _():
        x = x_ref[...].astype(F32)
        inverse = lax.rsqrt(jnp.mean(x * x, axis=-1, keepdims=True) + EPS)
        normed = x * inverse
        total = dn[...]
        grad_gain = jnp.sum(total * normed, axis=0, keepdims=True)
        inner = total * gains[0:1]
        added = inverse * (inner - normed * jnp.mean(inner * normed, axis=-1, keepdims=True))
        gin[...] = (dh_ref[...] + added).astype(BF)
        lines = width // 128
        for j in range(lines):
            lane = slice(j * 128, (j + 1) * 128)
            sums[0, j : j + 1, :] = grad_gain[:, lane]
            sums[0, lines + j : lines + j + 1, :] = ggf_ref[:, lane]
        sums[0, 2 * lines : 16, :] = jnp.zeros((16 - 2 * lines, 128), F32)
        line = lax.broadcasted_iota(jnp.int32, (128, 128), 0)
        lane = lax.broadcasted_iota(jnp.int32, (128, 128), 1)
        shift = jnp.where(lane < 64, lane, lane - 128)
        bucket = jnp.clip(-shift, -(buckets // 2), buckets // 2 - 1) + buckets // 2
        table = jnp.zeros((16, 128), F32)
        for t in range(3):
            pick = jnp.where(line == bucket + t * buckets, 1.0, 0.0)
            table = table + lax.dot_general(
                gtab[t], pick, (((1,), (1,)), ((), ())),
                precision=lax.Precision.HIGHEST, preferred_element_type=F32,
            )
        sums[0, 16:32, :] = table
        hops = bits + 1
        hop = None
        count = 0

        def small_hop():
            nonlocal hop, count
            if hop is not None:
                hop.wait_recv()
                k = count
                if k == 1:
                    sums[1, 0:16] = sums[0, 0:16] + got[0, 0:16]
                    sums[1, 16:24] = sums[0, 16:24] + got[0, 24:32]
                    sums[1, 24:32] = jnp.zeros((8, 128), F32)
                else:
                    sums[k] = sums[k - 1] + got[k - 1]
                hop = None
            if count < hops:
                flips = dict(mp_flip=1) if count == 0 else dict(dp_flip=1 << (count - 1))
                k = count
                hop = links.remote(lambda: sums.at[k], lambda: got.at[k], **flips)
                hop.start()
                started.append(hop)
                count += 1

        started = []
        small_hop()
        gin_away.start()
        gin_home.start()
        each(ff[0], "start_back_c")
        each(ff[1], "start_back_x")
        each(ff[2], "start_back")
        wo.start_back_x()
        pairs[1].start_z(lambda: ryp.at[1])
        pairs[0].start_back()
        small_hop()
        pairs[2].start_z(lambda: ryp.at[2])
        pairs[0].start_back_x()
        each(ff[1], "start_back_c")
        each(ff[2], "start_back1")
        pairs[1].start_back()
        wo.start_back_c()
        small_hop()
        pairs[2].start_back()
        each(ff[2], "start_back_x")
        pairs[1].start_back_x()
        pairs[0].start_back_c()
        small_hop()
        pairs[2].start_back_x()
        each(ff[2], "start_back_c")
        pairs[1].start_back_c()
        small_hop()
        pairs[2].start_back_c()
        while count < hops or hop is not None:
            small_hop()
        small[...] = sums[hops]
        y_away.wait_recv()
        gin_away.wait_recv()
        for unit in units:
            unit.end()
        for copy in [y_away, gin_away, wo_c, wo_y] + y3 + pair_c + pair_y + started:
            copy.wait_send()
        y_home.wait()
        gin_home.wait()


def backward(p, qt, kv, ot, dot, r, back, hot, x, gain, dh, ggf, wqkv, parts, gwo, y, n_dp, buckets):
    channels, tokens = qt.shape
    width = x.shape[1]
    n_pairs = channels // 128
    half = n_pairs // 2
    chunk = parts[0].shape[1]
    group = 3 * 128
    once = lambda shape: pl.BlockSpec(
        shape, lambda i: (0,) * len(shape), pipeline_mode=pl.Buffered(1)
    )
    pick = lambda i: lax.rem(i + half, n_pairs)
    side = lambda i: pick(i) // half
    place = lambda i: lax.rem(pick(i), half)
    turned = pl.BlockSpec((128, tokens), lambda i: (pick(i), 0))
    column = lambda rows, j, n: pl.BlockSpec(
        (rows, 128), lambda i: (0, side(i) * n * half + j * half + place(i))
    )
    shapes = []
    for k in range(3):
        shapes += [(width, chunk, True), (chunk, width, True)]
    shapes += [(width, group, False)] * 4
    units, far = [], []
    for n, w, deepest in shapes:
        units += [
            pltpu.VMEM((n // 4, w), BF),
            pltpu.VMEM((n // 16, w), BF),
            pltpu.VMEM((n // 8, w) if deepest else (3, n // 16, w), BF),
            pltpu.VMEM((n // 16, w), BF),
        ]
        far.append(pltpu.VMEM((max(n_dp // 16, 1), n // 16, w), BF))
    bits = n_dp.bit_length() - 1
    part_u, part_d = parts[0].shape, parts[1].shape
    copies = 160 + (10 * (n_dp // 16) if n_dp > 16 else 0)
    scratch = [
        pltpu.VMEM((tokens, 128), BF),
        pltpu.VMEM((128, tokens), BF),
        pltpu.VMEM((160, tokens), BF),
        pltpu.VMEM((width, tokens), BF),
        pltpu.VMEM((tokens, width), F32),
        pltpu.VMEM((3, 16, 128), F32),
        pltpu.VMEM((6, width, group), BF),
        pltpu.VMEM((6, width // 2, group), BF),
        pltpu.VMEM((3, width // 2, group), BF),
        pltpu.VMEM((tokens, width), BF),
        pltpu.VMEM(part_u, BF),
        pltpu.VMEM(part_d, BF),
        pltpu.VMEM(part_u, BF),
        pltpu.VMEM(part_d, BF),
        pltpu.VMEM(part_u, BF),
        pltpu.VMEM(part_d, BF),
        pltpu.VMEM(part_u, BF),
        pltpu.VMEM(part_d, BF),
        pltpu.VMEM((width // 2, width), BF),
        pltpu.VMEM((width // 2, width), BF),
        pltpu.VMEM((width // 2, width // 2), BF),
        pltpu.VMEM((bits + 2, 32, 128), F32),
        pltpu.VMEM((bits + 2, 32, 128), F32),
    ]
    scratch += units
    if n_dp > 16:
        scratch += far
    scratch += [pltpu.SemaphoreType.DMA((copies,))] * 2
    return pl.pallas_call(
        functools.partial(back_kernel, n_dp=n_dp, buckets=buckets),
        grid=(n_pairs,),
        in_specs=[
            pl.BlockSpec((2, tokens, tokens), lambda i: (pick(i), 0, 0)),
            turned,
            column(tokens, 0, 2),
            column(tokens, 1, 2),
            turned,
            turned,
            pl.BlockSpec((1, 2, tokens), lambda i: (pick(i), 0, 0)),
            once((96, tokens)),
            once((tokens, 128)),
            once((tokens, width)),
            once((2, width)),
            once((tokens, width)),
            once((1, width)),
            column(width, 0, 3),
            column(width, 1, 3),
            column(width, 2, 3),
        ]
        + [ANY] * 10,
        out_specs=[ANY] * 6 + [once((32, 128))],
        out_shape=[
            SHAPE((2, tokens // 2, width), BF),
            SHAPE((2, tokens // 2, width), BF),
            SHAPE((3, width, group), BF),
            SHAPE((width, group), BF),
            SHAPE((width, 3 * chunk), BF),
            SHAPE((3 * chunk, width), BF),
            SHAPE((32, 128), F32),
        ],
        scratch_shapes=scratch,
        compiler_params=params(60, collective_id=5, has_side_effects=True),
        name="backward",
    )(p, qt, kv, kv, ot, dot, r, back, hot, x, gain, dh, ggf, wqkv, wqkv, wqkv, *parts, gwo, y)


def local(
    n_dp, inputs, roi, cotangent, doc_lengths, live_mask, bucket_cells,
    gain_attn, gain_ffn, w_query, w_key, w_value, w_out, w_up, w_down, tables,
):
    rows, width = inputs.shape[1], inputs.shape[2]
    tokens = 2 * rows
    third = w_query.shape[1]
    heads = third // HDIM
    buckets = tables.shape[1]
    tab = jnp.pad(
        tables.transpose(2, 0, 1).reshape(heads, 3 * buckets), ((0, 2), (0, 128 - 3 * buckets))
    )
    marks = jnp.concatenate([live_mask[:, None, :], bucket_cells], axis=1)
    gains = jnp.stack([gain_attn, gain_ffn])
    x, tabo, wqkv, qt, kv, upo = entry(
        inputs, roi, tab, gains, w_query, w_key, w_value, w_up
    )
    p, mixt, r, hot, back, dyo, woo, upo, dno = attend(
        doc_lengths, marks, tab, tabo, qt, kv,
        cotangent, w_out, w_up, w_down, upo, buckets,
    )
    y, gwo, dh, dmt, gain_f, *parts = middle(
        x, mixt, w_out, woo, cotangent, dyo, gains, w_up, upo, w_down, dno
    )
    yret, gret, fqkv, fwo, fup, fdn, small = backward(
        p, qt, kv, mixt, dmt, r, back, hot, x, gains, dh, gain_f, wqkv, parts, gwo, y, n_dp, buckets
    )
    lines = width // 128
    out = inputs.astype(F32) + roi.astype(F32) + yret.astype(F32)
    grad_in = cotangent.astype(F32) + gret.astype(F32)
    table_out = small[16 : 16 + heads, : 3 * buckets].reshape(heads, 3, buckets).transpose(1, 2, 0)
    gq, gk, gv = (
        jnp.concatenate([fqkv[k, :, j * 128 : (j + 1) * 128] for k in range(3)], axis=1).astype(F32)
        for j in range(3)
    )
    return (
        out,
        grad_in,
        small[0:lines].reshape(width),
        small[lines : 2 * lines].reshape(width),
        gq,
        gk,
        gv,
        fwo.T.astype(F32),
        fup.astype(F32),
        fdn.astype(F32),
        table_out,
    )


def solution(mesh):
    n_dp = mesh.shape["dp"]
    rows = P(None, ("dp", "mp"), None)
    columns, lines = P(None, "mp"), P("mp", None)
    tables = P(None, None, "mp")
    return jax.shard_map(
        functools.partial(local, n_dp),
        mesh=mesh,
        in_specs=(
            rows, rows, rows, P(None, "dp", None), P(None, "dp"), P(None, None, "dp"),
            P(), P(), columns, columns, columns, lines, columns, lines, tables,
        ),
        out_specs=(
            rows, rows, P(), P(), columns, columns, columns, lines, columns, lines, tables,
        ),
        check_vma=False,
    )
```
